32 devices in a mesh: dp: 4 (over y, x), mp: 8 (over z, core).
Axes of the slice: x: 2, y: 2, z: 4, core: 2. Of those that a mesh axis runs over, the one named last changes fastest.
Arguments:
- tokens: bfloat16 [4096, 2048], P(('dp', 'mp')), may hold values from -6 to 6
- grad_out: bfloat16 [4096, 2048], P(('dp', 'mp')), may hold values from -6 to 6
- doc_ids: int32 [4096], P('dp'), may hold values from 0 to 3, as said below
- norm_gain: float32 [2048], replicated, may hold values from 0.5 to 1.5
- qkv_weight: bfloat16 [3, 2048, 2048], P(None, None, 'mp'), may hold values from -0.125 to 0.125
- beta_weight: bfloat16 [2048, 16], P(None, 'mp'), may hold values from -0.125 to 0.125
- conv_weight: float32 [3, 4, 2048], P(None, None, 'mp'), may hold values from -3 to 3
- head_gain: float32 [128], replicated, may hold values from 0.5 to 1.5
- out_weight: bfloat16 [2048, 2048], P('mp'), may hold values from -0.125 to 0.125
- ffn_gain: float32 [2048], replicated, may hold values from 0.5 to 1.5
- gate_up_weight: bfloat16 [2, 2048, 5632], P(None, None, 'mp'), may hold values from -0.125 to 0.125
- down_weight: bfloat16 [5632, 2048], P('mp'), may hold values from -0.078125 to 0.078125
Outputs:
- block_out: bfloat16 [4096, 2048], P(('dp', 'mp'))
- grad_tokens: float32 [4096, 2048], P(('dp', 'mp'))
- grad_norm_gain: float32 [2048], replicated
- grad_qkv: float32 [3, 2048, 2048], P(None, None, 'mp')
- grad_beta: float32 [2048, 16], P(None, 'mp')
- grad_conv: float32 [3, 4, 2048], P(None, None, 'mp')
- grad_head_gain: float32 [128], replicated
- grad_out_weight: float32 [2048, 2048], P('mp')
- grad_ffn_gain: float32 [2048], replicated
- grad_gate_up: float32 [2, 2048, 5632], P(None, None, 'mp')
- grad_down: float32 [5632, 2048], P('mp')
The draws below stay inside these ranges and needn't reach their ends.
Inputs may be any that keep to these rules, and one draw needn't show every extreme that they name: `doc_ids`: in each sequence of 1024 tokens the number starts at 0 on its first token and rises by exactly one at 3 positions, each a multiple of 64 tokens from the sequence's start; it never falls inside a sequence.
All inputs are finite; a program needn't handle non-finite values.
Results may differ from the reference program's by a relative error of at most 0.023.
Values may be sent and summed in bfloat16 or wider, within the bound.
A program may use at most 256 MiB of HBM per device.

```python
import jax
import jax.numpy as jnp
from jax import lax

D = 2048
H = 16
DH = 128
FF = 5632
KCONV = 4
SPAN = 64
LEN = 1024
DOCS = 4
TOKENS = 4096
N_MP = 8


def draw_doc_ids(key, part):
    sequences = TOKENS // LEN
    blocks = LEN // SPAN
    seq_keys = jax.random.split(key, sequences)
    orders = jax.vmap(lambda one_key: jax.random.permutation(one_key, blocks - 1))(seq_keys)
    rises = (orders < DOCS - 1).astype(jnp.int32)
    rises = jnp.concatenate([jnp.zeros((sequences, 1), jnp.int32), rises], 1)
    block_ids = jnp.cumsum(rises, axis=1).astype(jnp.int32)
    return jnp.repeat(block_ids, SPAN, axis=1).reshape(TOKENS)


def block_scale(rng, extent, shards, low, high):
    gain, own = 1.0, jax.random.fold_in(rng, 6)
    for dim, shards_of in shards:
        steps = jnp.exp(jax.random.uniform(jax.random.fold_in(own, dim), (shards_of,), jnp.float32, low / len(shards), high / len(shards)))
        gain = gain * jnp.repeat(steps, extent[dim] // shards_of).reshape([-1 if axis == dim else 1 for axis in range(len(extent))])
    return gain


def bell_draw(rng, dims, deviation, reach, cuts=(), held_as=jnp.bfloat16):
    gain = block_scale(rng, dims, cuts, -0.22, 0.18) if cuts else 1.0
    result = jax.random.normal(rng, dims, jnp.float32) * deviation * gain
    return jnp.minimum(jnp.maximum(result, -reach), reach).astype(held_as)


def setup_inputs(seed: int = 0) -> dict:
    keys = jax.random.split(jax.random.key(seed), 13)
    tokens = bell_draw(keys[0], (TOKENS, D), 1.0, 6.0, ((0, 32),))
    grad_out = bell_draw(keys[1], (TOKENS, D), 1.0, 6.0, ((0, 32),))
    doc_ids = draw_doc_ids(jax.random.fold_in(keys[12], 71), 0)
    norm_gain = jnp.clip(1.0 + 0.1 * jax.random.normal(keys[3], (D,), jnp.float32), 0.5, 1.5)
    qkv_weight = bell_draw(keys[4], (3, D, D), D ** -0.5, 0.125, ((2, 8),))
    beta_weight = bell_draw(keys[5], (D, H), D ** -0.5, 0.125, ((1, 8),))
    conv_weight = bell_draw(keys[6], (3, KCONV, D), KCONV ** -0.5, 3.0, ((2, 8),), jnp.float32)
    head_gain = jnp.clip(1.0 + 0.1 * jax.random.normal(keys[7], (DH,), jnp.float32), 0.5, 1.5)
    out_weight = bell_draw(keys[8], (D, D), D ** -0.5, 0.125, ((0, 8),))
    ffn_gain = jnp.clip(1.0 + 0.1 * jax.random.normal(keys[9], (D,), jnp.float32), 0.5, 1.5)
    gate_up_weight = bell_draw(keys[10], (2, D, FF), D ** -0.5, 0.125, ((2, 8),))
    down_weight = bell_draw(keys[11], (FF, D), FF ** -0.5, 0.078125, ((0, 8),))
    return dict(tokens=tokens, grad_out=grad_out, doc_ids=doc_ids, norm_gain=norm_gain, qkv_weight=qkv_weight, beta_weight=beta_weight, conv_weight=conv_weight, head_gain=head_gain, out_weight=out_weight, ffn_gain=ffn_gain, gate_up_weight=gate_up_weight, down_weight=down_weight)


@jax.custom_vjp
def low(v):
    return lax.optimization_barrier(v.astype(jnp.bfloat16)).astype(jnp.float32)

@jax.custom_vjp
def low_back(v):
    return v

def low_keep(v):
    return (low(v), None)

def low_pass(kept, grad):
    return (grad,)

def back_keep(v):
    return (v, None)

def back_low(kept, grad):
    return (low(grad),)
low.defvjp(low_keep, low_pass)
low_back.defvjp(back_keep, back_low)
EPSILON = 1e-06
HIGHEST = lax.Precision.HIGHEST

def row_scale(values):
    return lax.rsqrt(lax.optimization_barrier(jnp.mean(values * values, axis=-1, keepdims=True)) + EPSILON)

def matmul(left, right):
    return jnp.dot(left.astype(jnp.float32), right.astype(jnp.float32), precision=HIGHEST, preferred_element_type=jnp.float32)

def short_conv(values, weights, doc_ids):
    rows_total = values.shape[0]
    place = lax.iota(jnp.int32, rows_total) % LEN
    running = weights[KCONV - 1] * values
    for offset in range(1, KCONV):
        earlier = jnp.concatenate([jnp.zeros((offset, values.shape[1]), jnp.float32), values[:-offset]], 0)
        prior_ids = jnp.concatenate([jnp.full((offset,), -1, jnp.int32), doc_ids[:-offset]], 0)
        valid = jnp.logical_and(prior_ids == doc_ids, place >= offset)
        running = running + weights[KCONV - 1 - offset] * jnp.where(valid[:, None], earlier, 0.0)
    return running

def unit_rows(values, heads_here):
    shaped = values.reshape(values.shape[0], heads_here, DH)
    return shaped * lax.rsqrt(lax.optimization_barrier(jnp.sum(shaped * shaped, axis=-1, keepdims=True)) + EPSILON)

def span_keep(doc_ids):
    firsts = doc_ids[::SPAN]
    lasts = doc_ids[SPAN - 1::SPAN]
    before = jnp.concatenate([jnp.full((1,), -1, jnp.int32), lasts[:-1]], 0)
    starts = lax.iota(jnp.int32, firsts.shape[0]) * SPAN
    return jnp.logical_and(firsts == before, starts % LEN != 0).astype(jnp.float32)

def delta_rule(queries, key_rows, values, beta, keep):
    blocks = queries.shape[0] // SPAN
    heads_here = queries.shape[1]

    def split_rows(tensor):
        return jnp.transpose(tensor.reshape(blocks, SPAN, heads_here, DH), (0, 2, 1, 3))
    query_blocks = split_rows(queries)
    key_blocks = split_rows(key_rows)
    value_blocks = split_rows(values)
    beta_blocks = jnp.transpose(beta.reshape(blocks, SPAN, heads_here), (0, 2, 1))
    strict_lower = jnp.tril(jnp.ones((SPAN, SPAN), jnp.float32), -1)
    lower_incl = jnp.tril(jnp.ones((SPAN, SPAN), jnp.float32))
    identity = jnp.eye(SPAN, dtype=jnp.float32)

    @jax.checkpoint
    def one_block(memory, pieces):
        query_now, key_now, value_now, beta_now, keep_now = pieces
        memory = memory * keep_now
        inner = jnp.einsum('hcd,hed->hce', key_now, key_now, precision=HIGHEST)
        system = identity + inner * beta_now[:, :, None] * strict_lower
        right_side = jnp.concatenate([key_now * beta_now[:, :, None], value_now * beta_now[:, :, None]], -1)
        solved = jax.scipy.linalg.solve_triangular(system, right_side, lower=True, unit_diagonal=True)
        w_part = solved[..., :DH]
        u_part = solved[..., DH:]
        updates = u_part - jnp.einsum('hcd,hde->hce', w_part, memory, precision=HIGHEST)
        scores = jnp.einsum('hcd,hed->hce', query_now, key_now, precision=HIGHEST) * lower_incl
        output = jnp.einsum('hcd,hde->hce', query_now, memory, precision=HIGHEST)
        output = output + jnp.einsum('hce,hef->hcf', scores, updates, precision=HIGHEST)
        memory = memory + jnp.einsum('hcd,hce->hde', key_now, updates, precision=HIGHEST)
        return (memory, output)
    initial = jnp.zeros((heads_here, DH, DH), jnp.float32)
    _, outputs = lax.scan(one_block, initial, (query_blocks, key_blocks, value_blocks, beta_blocks, keep))
    return jnp.transpose(outputs, (0, 2, 1, 3)).reshape(blocks * SPAN, heads_here, DH)

def mixer(projected, conv_weight, head_gain, doc_ids):
    width = conv_weight.shape[2]
    heads_here = width // DH
    rows_total = projected.shape[0]
    q_conv = short_conv(projected[:, :width], conv_weight[0], doc_ids)
    k_conv = short_conv(projected[:, width:2 * width], conv_weight[1], doc_ids)
    v_conv = short_conv(projected[:, 2 * width:3 * width], conv_weight[2], doc_ids)
    queries = unit_rows(jax.nn.silu(q_conv), heads_here) * DH ** (-0.5)
    key_rows = unit_rows(jax.nn.silu(k_conv), heads_here)
    values = jax.nn.silu(v_conv).reshape(rows_total, heads_here, DH)
    beta = jax.nn.sigmoid(projected[:, 3 * width:])
    mixed = delta_rule(queries, key_rows, values, beta, span_keep(doc_ids))
    scale = lax.rsqrt(lax.optimization_barrier(jnp.mean(mixed * mixed, axis=-1, keepdims=True)) + EPSILON)
    return (mixed * scale * head_gain).reshape(rows_total, width)

def group_sum(left, right):
    rows_total = left.shape[0]
    inner = left.shape[1] // N_MP
    terms = jnp.einsum('rgc,gcd->grd', left.reshape(rows_total, N_MP, inner), right.reshape(N_MP, inner, right.shape[1]), precision=HIGHEST)
    return lax.optimization_barrier(jnp.sum(low(terms), axis=0))

def layer(tokens_f, params, doc_ids):
    norm_gain, qkv_weight, beta_weight, conv_weight, head_gain, out_weight, ffn_gain, gate_up_weight, down_weight = params
    normed_one = low(tokens_f * row_scale(tokens_f) * norm_gain)
    q_proj = low_back(matmul(normed_one, qkv_weight[0]))
    k_proj = low_back(matmul(normed_one, qkv_weight[1]))
    v_proj = low_back(matmul(normed_one, qkv_weight[2]))
    beta_logit = low_back(matmul(normed_one, beta_weight))
    projected = jnp.concatenate([q_proj, k_proj, v_proj, beta_logit], 1)
    heads_out = low(mixer(projected, conv_weight, head_gain, doc_ids))
    attn_sum = low_back(group_sum(heads_out, out_weight))
    residual = tokens_f + attn_sum
    normed_two = low(residual * row_scale(residual) * ffn_gain)
    gate = low_back(matmul(normed_two, gate_up_weight[0]))
    upward = low_back(matmul(normed_two, gate_up_weight[1]))
    hidden = low(jax.nn.silu(gate) * upward)
    return residual + group_sum(hidden, down_weight)

def reference(tokens, grad_out, doc_ids, norm_gain, qkv_weight, beta_weight, conv_weight, head_gain, out_weight, ffn_gain, gate_up_weight, down_weight):
    params = tuple((weight.astype(jnp.float32) for weight in (norm_gain, qkv_weight, beta_weight, conv_weight, head_gain, out_weight, ffn_gain, gate_up_weight, down_weight)))
    sequences = tokens.shape[0] // LEN
    token_seq = tokens.astype(jnp.float32).reshape(sequences, LEN, tokens.shape[1])
    grad_seq = grad_out.astype(jnp.float32).reshape(sequences, LEN, tokens.shape[1])
    ids_seq = doc_ids.reshape(sequences, LEN)
    zeros_init = tuple((jnp.zeros_like(weight) for weight in params))

    def one_sequence(running, pieces):
        token_rows, id_rows, grad_rows = pieces
        block_rows, backward = jax.vjp(lambda tok_in, par_in: layer(tok_in, par_in, id_rows), token_rows, params)
        grad_tok, grad_par = backward(grad_rows)
        running = jax.tree.map(jnp.add, running, grad_par)
        return (running, (block_rows.astype(jnp.bfloat16), grad_tok))
    totals, (block_all, grad_all) = lax.scan(one_sequence, zeros_init, (token_seq, ids_seq, grad_seq))
    return (block_all.reshape(tokens.shape), grad_all.reshape(tokens.shape), totals[0], totals[1], totals[2], totals[3], totals[4], totals[5], totals[6], totals[7], totals[8])
```

```python
import functools

import jax
import jax.numpy as jnp
from jax import lax
from jax.experimental import pallas as pl
from jax.experimental.pallas import tpu as pltpu
from jax.sharding import PartitionSpec as P

DH = 128
KCONV = 4
SPAN = 64
LEN = 1024


EPSILON = 1e-06


def row_scale(values):
    return lax.rsqrt(jnp.mean(values * values, axis=-1, keepdims=True) + EPSILON)


BF16 = jnp.bfloat16
F32 = jnp.float32
GROUP = 256
PER_GROUP = GROUP // SPAN


def dot_nn(left, right):
    return lax.dot_general(
        left.astype(BF16), right.astype(BF16), (((1,), (0,)), ((), ())), preferred_element_type=F32
    )


def dot_nt(left, right):
    return lax.dot_general(
        left.astype(BF16), right.astype(BF16), (((1,), (1,)), ((), ())), preferred_element_type=F32
    )


def dot_tn(left, right):
    return lax.dot_general(
        left.astype(BF16), right.astype(BF16), (((0,), (0,)), ((), ())), preferred_element_type=F32
    )


def span_keep(doc_ids):
    firsts = doc_ids[::SPAN]
    lasts = doc_ids[SPAN - 1 :: SPAN]
    before = jnp.concatenate([jnp.full((1,), -1, jnp.int32), lasts[:-1]], 0)
    starts = lax.iota(jnp.int32, firsts.shape[0]) * SPAN
    return jnp.logical_and(firsts == before, starts % LEN != 0).astype(jnp.float32)


def grid_masks():
    row = lax.broadcasted_iota(jnp.int32, (GROUP, GROUP), 0)
    col = lax.broadcasted_iota(jnp.int32, (GROUP, GROUP), 1)
    return row, col


def same_block(row, col, size):
    return (row // size) == (col // size)


def tap_rows(offset, keep_rows):
    place = lax.broadcasted_iota(jnp.int32, (GROUP, 1), 0) % SPAN
    return jnp.logical_or(place >= offset, keep_rows > 0.0)


def earlier_rows(ref, group, first_col, offset, keep_rows):
    start = pl.multiple_of(group * GROUP, GROUP)
    prior = pl.multiple_of(jnp.maximum(start - 8, 0), 8)
    cols = slice(first_col, first_col + DH)
    joined = jnp.concatenate([ref[pl.ds(prior, 8), cols], ref[pl.ds(start, GROUP), cols]], 0)
    shifted = pltpu.roll(joined, offset, 0)[8:]
    return jnp.where(tap_rows(offset, keep_rows), shifted, 0.0)


def conv_rows(ref, conv_ref, group, kind, first_col, head, keep_rows):
    taps = conv_ref[kind, :, head * DH : (head + 1) * DH]
    start = pl.multiple_of(group * GROUP, GROUP)
    running = taps[KCONV - 1 : KCONV] * ref[pl.ds(start, GROUP), first_col : first_col + DH]
    for offset in range(1, KCONV):
        running = running + taps[KCONV - 1 - offset : KCONV - offset] * earlier_rows(
            ref, group, first_col, offset, keep_rows
        )
    return running


def unit_scale(values):
    return lax.rsqrt(jnp.sum(values * values, axis=-1, keepdims=True) + EPSILON)


def mixer_forward_kernel(
    heads_here,
    keep_ref,
    keep_rows_ref,
    proj_ref,
    conv_ref,
    gain_ref,
    heads_ref,
    mixed_ref,
    query_ref,
    key_ref,
    solve_ref,
    w_ref,
    score_ref,
    map_ref,
    start_ref,
    update_ref,
    u_scr,
    add_scr,
):
    rows_total = proj_ref.shape[0]
    width = heads_here * DH
    groups = rows_total // GROUP
    spans = LEN // SPAN
    sequences = rows_total // LEN

    def local_part(group, carry):
        start = pl.multiple_of(group * GROUP, GROUP)
        rows = pl.ds(start, GROUP)
        keep_rows = keep_rows_ref[rows, :]
        row, col = grid_masks()
        for head in range(heads_here):
            cols = slice(head * DH, (head + 1) * DH)
            act_q = jax.nn.silu(
                conv_rows(proj_ref, conv_ref, group, 0, head * DH, head, keep_rows)
            )
            query = (act_q * (unit_scale(act_q) * DH ** (-0.5))).astype(BF16)
            act_k = jax.nn.silu(
                conv_rows(proj_ref, conv_ref, group, 1, width + head * DH, head, keep_rows)
            )
            key = act_k * unit_scale(act_k)
            value = jax.nn.silu(
                conv_rows(proj_ref, conv_ref, group, 2, 2 * width + head * DH, head, keep_rows)
            )
            beta = jax.nn.sigmoid(proj_ref[rows, 3 * width + head : 3 * width + head + 1])
            key_low = key.astype(BF16)
            query_ref[rows, cols] = query
            key_ref[rows, cols] = key_low
            inside = same_block(row, col, SPAN)
            system = jnp.where(
                jnp.logical_and(inside, row > col), dot_nt(key_low, key_low) * beta, 0.0
            )
            score = jnp.where(jnp.logical_and(inside, row >= col), dot_nt(query, key_low), 0.0)
            score_ref[group * heads_here + head] = score.astype(BF16)
            solve = jnp.where(
                row == col, 1.0, jnp.where(same_block(row, col, 2), -system, 0.0)
            )
            size = 2
            while size < SPAN:
                cross = jnp.where(
                    jnp.logical_and(
                        same_block(row, col, 2 * size),
                        jnp.logical_not(same_block(row, col, size)),
                    ),
                    system,
                    0.0,
                )
                solve_low = solve.astype(BF16)
                solve = solve - dot_nn(solve_low, dot_nn(cross, solve_low))
                size *= 2
            solve_low = solve.astype(BF16)
            solve_ref[group * heads_here + head] = solve_low
            both = dot_nn(solve_low, jnp.concatenate([key * beta, value * beta], 1))
            both_low = both.astype(BF16)
            w_ref[rows, cols] = both_low[:, :DH]
            u_scr[rows, cols] = both[:, DH:]
            for piece in range(PER_GROUP):
                part = slice(piece * SPAN, (piece + 1) * SPAN)
                carry_pair = dot_tn(key_low[part], both_low[part])
                slot = (group * PER_GROUP + piece) * heads_here + head
                map_ref[slot] = carry_pair[:, :DH].astype(BF16)
                add_scr[slot] = carry_pair[:, DH:]
        return carry

    lax.fori_loop(0, groups, local_part, 0)

    def scan_part(span, states):
        ended = []
        for sequence in range(sequences):
            for head in range(heads_here):
                block = sequence * spans + span
                slot = block * heads_here + head
                memory = states[sequence * heads_here + head] * keep_ref[block]
                memory_low = memory.astype(BF16)
                start_ref[slot] = memory_low
                ended.append(memory - dot_nn(map_ref[slot], memory_low) + add_scr[slot])
        return tuple(ended)

    blank = tuple(jnp.zeros((DH, DH), F32) for _ in range(sequences * heads_here))
    lax.fori_loop(0, spans, scan_part, blank)

    def output_part(group, carry):
        start = pl.multiple_of(group * GROUP, GROUP)
        rows = pl.ds(start, GROUP)
        for head in range(heads_here):
            cols = slice(head * DH, (head + 1) * DH)
            query = query_ref[rows, cols]
            w_part = w_ref[rows, cols]
            updates, reads = [], []
            for piece in range(PER_GROUP):
                part = slice(piece * SPAN, (piece + 1) * SPAN)
                slot = (group * PER_GROUP + piece) * heads_here + head
                pair = dot_nn(jnp.concatenate([w_part[part], query[part]], 0), start_ref[slot])
                updates.append(pair[:SPAN])
                reads.append(pair[SPAN:])
            update = (u_scr[rows, cols] - jnp.concatenate(updates, 0)).astype(BF16)
            update_ref[rows, cols] = update
            mixed = jnp.concatenate(reads, 0) + dot_nn(score_ref[group * heads_here + head], update)
            mixed_ref[rows, cols] = mixed
            scale = lax.rsqrt(jnp.mean(mixed * mixed, axis=-1, keepdims=True) + EPSILON)
            heads_ref[rows, cols] = (mixed * scale * gain_ref[...]).astype(BF16)
        return carry

    lax.fori_loop(0, groups, output_part, 0)


def mixer_backward_kernel(
    heads_here,
    keep_ref,
    keep_rows_ref,
    proj_ref,
    conv_ref,
    gain_ref,
    mixed_ref,
    query_ref,
    key_ref,
    solve_ref,
    w_ref,
    score_ref,
    map_ref,
    start_ref,
    update_ref,
    d_heads_ref,
    d_proj_ref,
    grad_conv_ref,
    grad_gain_ref,
    y_scr,
    add_scr,
    end_scr,
    d_query_scr,
    d_key_scr,
    d_conv_scr,
):
    rows_total = proj_ref.shape[0]
    width = heads_here * DH
    groups = rows_total // GROUP
    spans = LEN // SPAN
    sequences = rows_total // LEN
    grad_gain_ref[...] = jnp.zeros_like(grad_gain_ref)
    grad_conv_ref[...] = jnp.zeros_like(grad_conv_ref)

    def local_part(group, carry):
        start = pl.multiple_of(group * GROUP, GROUP)
        rows = pl.ds(start, GROUP)
        row, col = grid_masks()
        for head in range(heads_here):
            cols = slice(head * DH, (head + 1) * DH)
            mixed = mixed_ref[rows, cols]
            d_heads = d_heads_ref[rows, cols]
            scale = lax.rsqrt(jnp.mean(mixed * mixed, axis=-1, keepdims=True) + EPSILON)
            hat = mixed * scale
            grad_gain_ref[...] += jnp.sum(d_heads * hat, axis=0, keepdims=True)
            weighted = gain_ref[...] * d_heads
            d_mixed = scale * (
                weighted - hat * jnp.mean(weighted * hat, axis=-1, keepdims=True)
            )
            d_low = d_mixed.astype(BF16)
            query = query_ref[rows, cols]
            key = key_ref[rows, cols]
            w_part = w_ref[rows, cols]
            inside = jnp.logical_and(same_block(row, col, SPAN), row >= col)
            d_score = jnp.where(inside, dot_nt(d_low, update_ref[rows, cols]), 0.0).astype(BF16)
            y_part = dot_tn(score_ref[group * heads_here + head], d_low)
            y_scr[rows, cols] = y_part
            y_low = y_part.astype(BF16)
            d_key_scr[rows, cols] = dot_tn(d_score, query)
            reads = []
            for piece in range(PER_GROUP):
                part = slice(piece * SPAN, (piece + 1) * SPAN)
                slot = (group * PER_GROUP + piece) * heads_here + head
                add_scr[slot] = dot_tn(
                    jnp.concatenate([query[part], w_part[part]], 0),
                    jnp.concatenate([d_low[part], -y_low[part]], 0),
                )
                reads.append(dot_nt(d_low[part], start_ref[slot]))
            d_query_scr[rows, cols] = dot_nn(d_score, key) + jnp.concatenate(reads, 0)
        return carry

    lax.fori_loop(0, groups, local_part, 0)

    def scan_part(step, states):
        span = spans - 1 - step
        begun = []
        for sequence in range(sequences):
            for head in range(heads_here):
                block = sequence * spans + span
                slot = block * heads_here + head
                d_end = states[sequence * heads_here + head]
                d_end_low = d_end.astype(BF16)
                end_scr[slot] = d_end_low
                begun.append(
                    (d_end - dot_tn(map_ref[slot], d_end_low) + add_scr[slot]) * keep_ref[block]
                )
        return tuple(begun)

    blank = tuple(jnp.zeros((DH, DH), F32) for _ in range(sequences * heads_here))
    lax.fori_loop(0, spans, scan_part, blank)

    def finish_part(group, carry):
        start = pl.multiple_of(group * GROUP, GROUP)
        rows = pl.ds(start, GROUP)
        keep_rows = keep_rows_ref[rows, :]
        row, col = grid_masks()
        for head in range(heads_here):
            cols = slice(head * DH, (head + 1) * DH)
            beta = jax.nn.sigmoid(proj_ref[rows, 3 * width + head : 3 * width + head + 1])
            key = key_ref[rows, cols]
            update = update_ref[rows, cols]
            reads = []
            for piece in range(PER_GROUP):
                part = slice(piece * SPAN, (piece + 1) * SPAN)
                slot = (group * PER_GROUP + piece) * heads_here + head
                reads.append(dot_nn(key[part], end_scr[slot]))
            d_update = y_scr[rows, cols] + jnp.concatenate(reads, 0)
            d_right = dot_tn(solve_ref[group * heads_here + head], d_update)
            d_value = beta * d_right
            d_value_low = d_value.astype(BF16)
            d_logit = (1.0 - beta) * jnp.sum(
                d_right * update.astype(F32), axis=-1, keepdims=True
            )
            d_proj_ref[rows, 3 * width + head : 3 * width + head + 1] = d_logit.astype(BF16)
            inside = jnp.logical_and(same_block(row, col, SPAN), row > col)
            d_inner = jnp.where(inside, dot_nt(d_value_low, update), 0.0)
            reads = []
            for piece in range(PER_GROUP):
                part = slice(piece * SPAN, (piece + 1) * SPAN)
                slot = (group * PER_GROUP + piece) * heads_here + head
                reads.append(
                    dot_nt(
                        jnp.concatenate([update[part], -d_value_low[part]], 1),
                        jnp.concatenate([end_scr[slot], start_ref[slot]], 1),
                    )
                )
            d_key = (
                d_key_scr[rows, cols]
                + jnp.concatenate(reads, 0)
                - dot_nn(d_inner + d_inner.T, key)
            )
            grads = (d_query_scr[rows, cols] * DH ** (-0.5), d_key, d_value)
            for kind in range(3):
                pre = conv_rows(
                    proj_ref, conv_ref, group, kind, kind * width + head * DH, head, keep_rows
                )
                gate = jax.nn.sigmoid(pre)
                act = pre * gate
                d_act = grads[kind]
                if kind < 2:
                    scale = unit_scale(act)
                    hat = act * scale
                    d_act = scale * (d_act - hat * jnp.sum(hat * d_act, axis=-1, keepdims=True))
                first = kind * width + head * DH
                d_conv_scr[rows, first : first + DH] = d_act * gate * (1.0 + pre * (1.0 - gate))
        return carry

    lax.fori_loop(0, groups, finish_part, 0)
    d_conv_scr[rows_total : rows_total + 8, :] = jnp.zeros((8, 3 * width), F32)

    def conv_part(group, carry):
        start = pl.multiple_of(group * GROUP, GROUP)
        rows = pl.ds(start, GROUP)
        after = pl.ds(pl.multiple_of(start + GROUP, GROUP), 8)
        keep_rows = keep_rows_ref[rows, :]
        keep_after = keep_rows_ref[
            pl.ds(pl.multiple_of(jnp.minimum(start + GROUP, rows_total - 8), 8), 8), :
        ]
        keep_joined = jnp.concatenate([keep_rows, keep_after], 0)
        place = lax.broadcasted_iota(jnp.int32, (GROUP + 8, 1), 0) % SPAN
        for kind in range(3):
            for head in range(heads_here):
                first = kind * width + head * DH
                cols = slice(first, first + DH)
                taps = conv_ref[kind, :, head * DH : (head + 1) * DH]
                here = d_conv_scr[rows, cols]
                joined = jnp.concatenate([here, d_conv_scr[after, cols]], 0)
                total = taps[KCONV - 1 : KCONV] * here
                sums = [jnp.sum(here * proj_ref[rows, cols], axis=0, keepdims=True)]
                for offset in range(1, KCONV):
                    counted = jnp.logical_or(place >= offset, keep_joined > 0.0)
                    masked = jnp.where(counted, joined, 0.0)
                    shifted = pltpu.roll(masked, GROUP + 8 - offset, 0)[:GROUP]
                    total = total + taps[KCONV - 1 - offset : KCONV - offset] * shifted
                    sums.append(
                        jnp.sum(
                            here * earlier_rows(proj_ref, group, first, offset, keep_rows),
                            axis=0,
                            keepdims=True,
                        )
                    )
                d_proj_ref[rows, cols] = total.astype(BF16)
                grad_conv_ref[kind, :, head * DH : (head + 1) * DH] += jnp.concatenate(
                    sums[::-1], 0
                )
        return carry

    lax.fori_loop(0, groups, conv_part, 0)


VMEM_LIMIT = 56 * 1024 * 1024


def whole():
    return pl.BlockSpec(memory_space=pltpu.VMEM)


def mixer_forward(projected, conv_weight, head_gain, keep, keep_rows):
    rows_total = projected.shape[0]
    width = conv_weight.shape[2]
    heads_here = width // DH
    grids = rows_total // GROUP * heads_here
    slots = rows_total // SPAN * heads_here
    shapes = (
        jax.ShapeDtypeStruct((rows_total, width), BF16),
        jax.ShapeDtypeStruct((rows_total, width), F32),
        jax.ShapeDtypeStruct((rows_total, width), BF16),
        jax.ShapeDtypeStruct((rows_total, width), BF16),
        jax.ShapeDtypeStruct((grids, GROUP, GROUP), BF16),
        jax.ShapeDtypeStruct((rows_total, width), BF16),
        jax.ShapeDtypeStruct((grids, GROUP, GROUP), BF16),
        jax.ShapeDtypeStruct((slots, DH, DH), BF16),
        jax.ShapeDtypeStruct((slots, DH, DH), BF16),
        jax.ShapeDtypeStruct((rows_total, width), BF16),
    )
    return pl.pallas_call(
        functools.partial(mixer_forward_kernel, heads_here),
        out_shape=shapes,
        in_specs=[pl.BlockSpec(memory_space=pltpu.SMEM)] + [whole()] * 4,
        out_specs=tuple(whole() for _ in shapes),
        scratch_shapes=[pltpu.VMEM((rows_total, width), F32), pltpu.VMEM((slots, DH, DH), F32)],
        compiler_params=pltpu.CompilerParams(vmem_limit_bytes=VMEM_LIMIT),
        name="mixer_forward",
    )(keep, keep_rows, projected, conv_weight, head_gain.reshape(1, DH))


def mixer_backward(projected, conv_weight, head_gain, keep, keep_rows, kept, d_heads):
    rows_total = projected.shape[0]
    width = conv_weight.shape[2]
    heads_here = width // DH
    slots = rows_total // SPAN * heads_here
    shapes = (
        jax.ShapeDtypeStruct(projected.shape, BF16),
        jax.ShapeDtypeStruct(conv_weight.shape, F32),
        jax.ShapeDtypeStruct((1, DH), F32),
    )
    return pl.pallas_call(
        functools.partial(mixer_backward_kernel, heads_here),
        out_shape=shapes,
        in_specs=[pl.BlockSpec(memory_space=pltpu.SMEM)] + [whole()] * 14,
        out_specs=tuple(whole() for _ in shapes),
        scratch_shapes=[
            pltpu.VMEM((rows_total, width), F32),
            pltpu.VMEM((slots, DH, DH), F32),
            pltpu.VMEM((slots, DH, DH), BF16),
            pltpu.VMEM((rows_total, width), F32),
            pltpu.VMEM((rows_total, width), F32),
            pltpu.VMEM((rows_total + 8, 3 * width), F32),
        ],
        compiler_params=pltpu.CompilerParams(vmem_limit_bytes=VMEM_LIMIT),
        name="mixer_backward",
    )(keep, keep_rows, projected, conv_weight, head_gain.reshape(1, DH), *kept, d_heads)


def body(
    tokens,
    grad_out,
    doc_ids,
    norm_gain,
    qkv_weight,
    beta_weight,
    conv_weight,
    head_gain,
    out_weight,
    ffn_gain,
    gate_up_weight,
    down_weight,
):
    width = qkv_weight.shape[2]
    tokens_f = tokens.astype(jnp.float32)
    scale_one = row_scale(tokens_f)
    normed_one = (tokens_f * scale_one * norm_gain).astype(jnp.bfloat16)
    proj_weight = jnp.concatenate([qkv_weight[0], qkv_weight[1], qkv_weight[2], beta_weight], 1)
    rows_one = lax.all_gather(normed_one, "mp", axis=0, tiled=True)
    projected = jnp.dot(rows_one, proj_weight, preferred_element_type=jnp.float32)
    keep = span_keep(doc_ids)
    keep_rows = jnp.repeat(keep, SPAN)[:, None]
    heads_out, *kept = mixer_forward(projected, conv_weight, head_gain, keep, keep_rows)
    attn_sum = lax.psum_scatter(
        jnp.dot(heads_out, out_weight, preferred_element_type=jnp.float32).astype(jnp.bfloat16),
        "mp",
        scatter_dimension=0,
        tiled=True,
    ).astype(jnp.float32)
    residual = tokens_f + attn_sum
    scale_two = row_scale(residual)
    normed_two = (residual * scale_two * ffn_gain).astype(jnp.bfloat16)
    rows_two = lax.all_gather(normed_two, "mp", axis=0, tiled=True)
    gate_up = jnp.einsum(
        "td,gdf->tgf", rows_two, gate_up_weight, preferred_element_type=jnp.float32
    )
    gate = gate_up[:, 0]
    upward = gate_up[:, 1]
    sigmoid_gate = jax.nn.sigmoid(gate)
    activated = gate * sigmoid_gate
    hidden = (activated * upward).astype(jnp.bfloat16)
    ffn_sum = lax.psum_scatter(
        jnp.dot(hidden, down_weight, preferred_element_type=jnp.float32).astype(jnp.bfloat16),
        "mp",
        scatter_dimension=0,
        tiled=True,
    ).astype(jnp.float32)
    block_out = (residual + ffn_sum).astype(jnp.bfloat16)
    grads_all = lax.all_gather(grad_out, "mp", axis=0, tiled=True)
    grad_down = jnp.einsum("tf,td->fd", hidden, grads_all, preferred_element_type=jnp.float32)
    d_hidden = jnp.einsum("td,fd->tf", grads_all, down_weight, preferred_element_type=jnp.float32)
    d_gate = d_hidden * upward * sigmoid_gate * (1.0 + gate * (1.0 - sigmoid_gate))
    d_upward = d_hidden * activated
    d_gate_up = jnp.stack([d_gate, d_upward], 1).astype(jnp.bfloat16)
    grad_gate_up = jnp.einsum(
        "td,tgf->gdf", rows_two, d_gate_up, preferred_element_type=jnp.float32
    )
    part_rows = d_gate_up
    d_normed_two = lax.psum_scatter(
        jnp.einsum(
            "tgf,gdf->td", part_rows, gate_up_weight, preferred_element_type=jnp.float32
        ).astype(jnp.bfloat16),
        "mp",
        scatter_dimension=0,
        tiled=True,
    ).astype(jnp.float32)
    hat_two = residual * scale_two
    weighted_two = ffn_gain * d_normed_two
    part_ffn_gain = jnp.sum(d_normed_two * hat_two, axis=0)
    d_residual = grad_out.astype(jnp.float32) + scale_two * (
        weighted_two - hat_two * jnp.mean(weighted_two * hat_two, axis=-1, keepdims=True)
    )
    d_attn = lax.all_gather(d_residual.astype(jnp.bfloat16), "mp", axis=0, tiled=True)
    grad_out_weight = jnp.einsum("tw,td->wd", heads_out, d_attn, preferred_element_type=jnp.float32)
    d_heads = jnp.einsum("td,wd->tw", d_attn, out_weight, preferred_element_type=jnp.float32)
    d_projected, grad_conv, part_head_gain = mixer_backward(
        projected, conv_weight, head_gain, keep, keep_rows, kept, d_heads
    )
    part_head_gain = part_head_gain.reshape(DH)
    grad_proj = jnp.einsum("td,tc->dc", rows_one, d_projected, preferred_element_type=jnp.float32)
    part_rows = d_projected
    d_normed_one = lax.psum_scatter(
        jnp.einsum("tc,dc->td", part_rows, proj_weight, preferred_element_type=jnp.float32).astype(
            jnp.bfloat16
        ),
        "mp",
        scatter_dimension=0,
        tiled=True,
    ).astype(jnp.float32)
    hat_one = tokens_f * scale_one
    weighted_one = norm_gain * d_normed_one
    part_norm_gain = jnp.sum(d_normed_one * hat_one, axis=0)
    grad_tokens = d_residual + scale_one * (
        weighted_one - hat_one * jnp.mean(weighted_one * hat_one, axis=-1, keepdims=True)
    )
    grad_qkv = jnp.stack(
        [
            grad_proj[:, :width],
            grad_proj[:, width : 2 * width],
            grad_proj[:, 2 * width : 3 * width],
        ],
        0,
    )
    grad_beta = grad_proj[:, 3 * width :]
    summed = (
        lax.psum(grad_qkv.astype(jnp.bfloat16), "dp").astype(jnp.float32),
        lax.psum(grad_beta.astype(jnp.bfloat16), "dp").astype(jnp.float32),
        lax.psum(grad_conv.astype(jnp.bfloat16), "dp").astype(jnp.float32),
        lax.psum(grad_out_weight.astype(jnp.bfloat16), "dp").astype(jnp.float32),
        lax.psum(grad_gate_up.astype(jnp.bfloat16), "dp").astype(jnp.float32),
        lax.psum(grad_down.astype(jnp.bfloat16), "dp").astype(jnp.float32),
    )
    gains = lax.psum((part_norm_gain, part_head_gain, part_ffn_gain), ("dp", "mp"))
    return (
        block_out,
        grad_tokens,
        gains[0],
        summed[0],
        summed[1],
        summed[2],
        gains[1],
        summed[3],
        gains[2],
        summed[4],
        summed[5],
    )


def solution(mesh):
    in_specs = (
        P(("dp", "mp"), None),
        P(("dp", "mp"), None),
        P("dp"),
        P(),
        P(None, None, "mp"),
        P(None, "mp"),
        P(None, None, "mp"),
        P(),
        P("mp", None),
        P(),
        P(None, None, "mp"),
        P("mp", None),
    )
    out_specs = (
        P(("dp", "mp"), None),
        P(("dp", "mp"), None),
        P(),
        P(None, None, "mp"),
        P(None, "mp"),
        P(None, None, "mp"),
        P(),
        P("mp", None),
        P(),
        P(None, None, "mp"),
        P("mp", None),
    )
    return jax.shard_map(body, mesh=mesh, in_specs=in_specs, out_specs=out_specs, check_vma=False)
```

```python
import functools

import jax
import jax.numpy as jnp
from jax import lax
from jax.experimental import pallas as pl
from jax.experimental.pallas import tpu as pltpu
from jax.sharding import PartitionSpec as P

DH = 128
KCONV = 4
SPAN = 64
LEN = 1024


EPSILON = 1e-06


def row_scale(values):
    return lax.rsqrt(jnp.mean(values * values, axis=-1, keepdims=True) + EPSILON)


BF16 = jnp.bfloat16
F32 = jnp.float32
GROUP = 256
LANES = 128
PER_GROUP = GROUP // SPAN


def dot_nn(left, right):
    return lax.dot_general(
        left.astype(BF16), right.astype(BF16), (((1,), (0,)), ((), ())), preferred_element_type=F32
    )


def dot_nt(left, right):
    return lax.dot_general(
        left.astype(BF16), right.astype(BF16), (((1,), (1,)), ((), ())), preferred_element_type=F32
    )


def dot_tn(left, right):
    return lax.dot_general(
        left.astype(BF16), right.astype(BF16), (((0,), (0,)), ((), ())), preferred_element_type=F32
    )


def span_keep(doc_ids):
    firsts = doc_ids[::SPAN]
    lasts = doc_ids[SPAN - 1 :: SPAN]
    before = jnp.concatenate([jnp.full((1,), -1, jnp.int32), lasts[:-1]], 0)
    starts = lax.iota(jnp.int32, firsts.shape[0]) * SPAN
    return jnp.logical_and(firsts == before, starts % LEN != 0).astype(jnp.float32)


def grid_masks():
    row = lax.broadcasted_iota(jnp.int32, (GROUP, GROUP), 0)
    col = lax.broadcasted_iota(jnp.int32, (GROUP, GROUP), 1)
    return row, col


def same_block(row, col, size):
    return (row // size) == (col // size)


def tap_rows(offset, keep_rows):
    place = lax.broadcasted_iota(jnp.int32, (GROUP, 1), 0) % SPAN
    return jnp.logical_or(place >= offset, keep_rows > 0.0)


def earlier_rows(ref, group, first_col, offset, keep_rows):
    start = pl.multiple_of(group * GROUP, GROUP)
    prior = pl.multiple_of(jnp.maximum(start - 8, 0), 8)
    cols = slice(first_col, first_col + DH)
    joined = jnp.concatenate([ref[pl.ds(prior, 8), cols], ref[pl.ds(start, GROUP), cols]], 0)
    shifted = pltpu.roll(joined, offset, 0)[8:]
    return jnp.where(tap_rows(offset, keep_rows), shifted, 0.0)


def conv_rows(ref, conv_ref, group, kind, first_col, head, keep_rows):
    taps = conv_ref[kind, :, head * DH : (head + 1) * DH]
    start = pl.multiple_of(group * GROUP, GROUP)
    running = taps[KCONV - 1 : KCONV] * ref[pl.ds(start, GROUP), first_col : first_col + DH]
    for offset in range(1, KCONV):
        running = running + taps[KCONV - 1 - offset : KCONV - offset] * earlier_rows(
            ref, group, first_col, offset, keep_rows
        )
    return running


def unit_scale(values):
    return lax.rsqrt(jnp.sum(values * values, axis=-1, keepdims=True) + EPSILON)


VMEM_LIMIT = 60 * 1024 * 1024


def whole():
    return pl.BlockSpec(memory_space=pltpu.VMEM)


MESH = pl.DeviceIdType.MESH
TILE = 512
CORE, RIGHT, LEFT = 0, 1, 2


def line_place():
    me = lax.axis_index("mp")
    core = lax.rem(me, 2)
    return me, me // 2, core


def flip_bit(axis, bit):
    place = lax.axis_index(axis)
    scale = 2**bit
    mine = lax.rem(place // scale, 2)
    return mine, {axis: place + (1 - 2 * mine) * scale}


def line_barrier(chips, flips=(), peers=1):
    me, chip, core = line_place()
    barrier = pltpu.get_barrier_semaphore()
    for axis, bit in flips:
        pl.semaphore_signal(
            barrier, inc=1, device_id=flip_bit(axis, bit)[1], device_id_type=MESH
        )
    for step in range(1, peers):
        place = lax.rem(lax.axis_index("dp") + step, peers)
        pl.semaphore_signal(barrier, inc=1, device_id={"dp": place}, device_id_type=MESH)

    def greet(other):
        pl.semaphore_signal(barrier, inc=1, device_id={"mp": other}, device_id_type=MESH)

    greet(me + 1 - 2 * core)

    @pl.when(chip > 0)
    def _():
        greet(me - 2)

    @pl.when(chip < chips - 1)
    def _():
        greet(me + 2)

    beside = (chip > 0).astype(jnp.int32) + (chip < chips - 1).astype(jnp.int32)
    pl.semaphore_wait(barrier, beside + len(flips) + peers)


def line_target(kind):
    me, chip, core = line_place()
    return {CORE: me + 1 - 2 * core, RIGHT: me + 2, LEFT: me - 2}[kind]


class LineGather:
    def __init__(self, chips, out_ref, sems):
        self.chips, self.out_ref, self.sems = chips, out_ref, sems
        self.block = out_ref.shape[0] // (2 * chips)
        self.me, self.chip, self.core = line_place()

    def rows(self, chip, core):
        return pl.ds(pl.multiple_of((2 * chip + core) * self.block, self.block), self.block)

    def copy(self, kind, chip, core):
        part = self.out_ref.at[self.rows(chip, core), :]
        return pltpu.make_async_remote_copy(
            src_ref=part,
            dst_ref=part,
            send_sem=self.sems.at[2 * kind, chip],
            recv_sem=self.sems.at[2 * kind + 1, chip],
            device_id={"mp": line_target(kind)},
            device_id_type=MESH,
        )

    def start(self, block):
        self.out_ref[self.rows(self.chip, self.core), :] = block

        @pl.when(self.chip < self.chips - 1)
        def _():
            self.copy(RIGHT, self.chip, self.core).start()

        @pl.when(self.chip > 0)
        def _():
            self.copy(LEFT, self.chip, self.core).start()

        self.copy(CORE, self.chip, self.core).start()

    def arrive(self, chip):
        self.copy(CORE, chip, 1 - self.core).wait_recv()

    def each_new(self, step, use):
        behind, ahead = self.chip - step, self.chip + step

        @pl.when(behind >= 0)
        def _():
            use(behind)

        @pl.when(ahead < self.chips)
        def _():
            use(ahead)

    def pass_on(self, behind, ahead):
        @pl.when(jnp.logical_and(behind >= 0, self.chip < self.chips - 1))
        def _():
            self.copy(RIGHT, behind, self.core).start()

        @pl.when(jnp.logical_and(ahead < self.chips, self.chip > 0))
        def _():
            self.copy(LEFT, ahead, self.core).start()

    def hop(self, step, forward=True):
        behind, ahead = self.chip - step, self.chip + step

        @pl.when(behind >= 0)
        def _():
            self.copy(RIGHT, behind, self.core).wait_recv()

        @pl.when(ahead < self.chips)
        def _():
            self.copy(LEFT, ahead, self.core).wait_recv()

        if forward:
            self.pass_on(behind, ahead)

        self.each_new(step, lambda chip: self.copy(CORE, chip, self.core).start())
        self.each_new(step, self.arrive)

    def hops(self, after):
        def one_hop(step, carry):
            self.hop(step)
            after(step)
            return carry

        lax.fori_loop(1, self.chips, one_hop, 0)

    def finish(self, first=0, end=None):
        end = self.chips if end is None else end

        def sent(chip, carry):
            apart = jnp.abs(chip - self.chip)
            relay = jnp.logical_and(apart >= first - 1, apart < end - 1)
            if first == 0:
                relay = jnp.logical_or(relay, apart == 0)
            to_right = jnp.logical_and(chip <= self.chip, self.chip < self.chips - 1)
            to_left = jnp.logical_and(chip >= self.chip, self.chip > 0)

            @pl.when(jnp.logical_and(relay, to_right))
            def _():
                self.copy(RIGHT, chip, self.core).wait_send()

            @pl.when(jnp.logical_and(relay, to_left))
            def _():
                self.copy(LEFT, chip, self.core).wait_send()

            @pl.when(jnp.logical_and(apart >= first, apart < end))
            def _():
                self.copy(CORE, chip, self.core).wait_send()

            return carry

        lax.fori_loop(0, self.chips, sent, 0)


class LineScatter:
    def __init__(self, chips, term, stage, held, landing, sems):
        self.chips, self.term = chips, term
        self.stage, self.held, self.landing, self.sems = stage, held, landing, sems
        self.me, self.chip, self.core = line_place()

    def left_slot(self, chip, receiver):
        return jnp.where(chip == receiver, self.chips, chip)

    def copy(self, kind, chip):
        source = (self.stage if kind == CORE else self.held).at[chip]
        if kind == CORE:
            target = self.held.at[chip]
        elif kind == RIGHT:
            target = self.landing.at[chip]
        else:
            target = self.landing.at[self.left_slot(chip, self.chip - 1)]
        return pltpu.make_async_remote_copy(
            src_ref=source,
            dst_ref=target,
            send_sem=self.sems.at[2 * kind, chip],
            recv_sem=self.sems.at[2 * kind + 1, chip],
            device_id={"mp": line_target(kind)},
            device_id_type=MESH,
        )

    def exchange(self, chip):
        self.stage[chip] = self.term(chip, 1 - self.core).astype(BF16)
        self.copy(CORE, chip).start()

    def collect(self, chip):
        own = self.term(chip, self.core)
        self.copy(CORE, chip).wait_recv()
        return own + self.held[chip].astype(F32)

    def pass_on(self, kind, chip, first):
        both = self.collect(chip)

        @pl.when(first)
        def _():
            self.held[chip] = both.astype(BF16)

        @pl.when(jnp.logical_not(first))
        def _():
            self.copy(kind, chip).wait_recv()
            self.held[chip] = (both + self.landing[chip].astype(F32)).astype(BF16)

        self.copy(kind, chip).start()

    def exchange_pair(self, step):
        @pl.when(self.chip + step < self.chips)
        def _():
            self.exchange(self.chip + step)

        @pl.when(self.chip - step >= 0)
        def _():
            self.exchange(self.chip - step)

    def begin(self):
        self.exchange_pair(self.chips - 1)

    def step(self, index):
        last = self.chips - 1
        step = last - index

        @pl.when(step > 1)
        def _():
            self.exchange_pair(step - 1)

        @pl.when(self.chip + step < self.chips)
        def _():
            self.pass_on(RIGHT, self.chip + step, self.chip == 0)

        @pl.when(self.chip - step >= 0)
        def _():
            self.pass_on(LEFT, self.chip - step, self.chip == last)

    def steps(self, first, each=None):
        def one_step(index, carry):
            self.step(index)
            if each is not None:
                each(index)
            return carry

        lax.fori_loop(first, self.chips - 1, one_step, 0)

    def end(self, result_ref):
        self.exchange(self.chip)
        result_ref[...] = self.collect(self.chip)

        @pl.when(self.chip > 0)
        def _():
            self.copy(RIGHT, self.chip).wait_recv()
            result_ref[...] += self.landing[self.chip].astype(F32)

        @pl.when(self.chip < self.chips - 1)
        def _():
            self.copy(LEFT, self.chip).wait_recv()
            result_ref[...] += self.landing[self.chips].astype(F32)

    def run(self, result_ref, each=None):
        self.begin()
        self.steps(0, each)
        self.end(result_ref)

    def finish(self):
        def sent(chip, carry):
            @pl.when(chip > self.chip)
            def _():
                self.copy(RIGHT, chip).wait_send()

            @pl.when(chip < self.chip)
            def _():
                self.copy(LEFT, chip).wait_send()

            self.copy(CORE, chip).wait_send()
            return carry

        lax.fori_loop(0, self.chips, sent, 0)


class PlaneSum:
    def __init__(self, bits, bufs, outs, landings, sems):
        self.bits, self.bufs, self.outs = bits, bufs, outs
        self.landings, self.sems = landings, sems
        self.orders = (tuple(range(bits)), tuple(reversed(range(bits))))
        self.half = bufs[0][0].shape[bufs[0][1]] // 2

    def span(self, part, level):
        start = part * self.half
        for index in range(level):
            mine, _ = flip_bit("dp", self.orders[part][index])
            start = start + mine * (self.half >> (index + 1))
        return start

    def view(self, pairs, array, start, size):
        ref, axis = pairs[array]
        where = pl.ds(pl.multiple_of(start, size), size)
        return ref.at[where, :] if axis == 0 else ref.at[:, where]

    def pieces(self, part, index):
        mine, target = flip_bit("dp", self.orders[part][index])
        size = self.half >> (index + 1)
        start = self.span(part, index)
        return target, size, start + mine * size, start + (1 - mine) * size

    def copies(self, step):
        made = []
        for part in range(2):
            index = step if step < self.bits else 2 * self.bits - 1 - step
            target, size, kept, given = self.pieces(part, index)
            for array in range(len(self.bufs)):
                if step < self.bits:
                    source = self.view(self.bufs, array, given, size)
                    landing = self.landings[index][array].at[part]
                else:
                    source = self.view(self.outs, array, kept, size)
                    landing = source
                made.append(
                    pltpu.make_async_remote_copy(
                        src_ref=source,
                        dst_ref=landing,
                        send_sem=self.sems.at[0, part, step, array],
                        recv_sem=self.sems.at[1, part, step, array],
                        device_id=target,
                        device_id_type=MESH,
                    )
                )
        return made

    def advance(self, step, go=True):
        if step > 0:
            for copy in self.copies(step - 1):
                copy.wait()
            if step - 1 < self.bits:
                for part in range(2):
                    _, size, kept, _ = self.pieces(part, step - 1)
                    for array in range(len(self.bufs)):
                        here = self.view(self.bufs, array, kept, size)
                        ended = self.outs if step == self.bits else self.bufs
                        self.view(ended, array, kept, size)[...] = (
                            here[...].astype(F32)
                            + self.landings[step - 1][array][part].astype(F32)
                        ).astype(BF16)
        if go and step < 2 * self.bits:
            for copy in self.copies(step):
                copy.start()


def plane_scratch(bits, shapes):
    made = [pltpu.VMEM(shape, BF16) for shape, _ in shapes]
    for index in range(bits):
        for shape, axis in shapes:
            size = list(shape)
            size[axis] = size[axis] >> (index + 2)
            made.append(pltpu.VMEM((2, *size), BF16))
    return made + [pltpu.SemaphoreType.DMA((2, 2, 2 * bits, len(shapes)))]


def plane_sum(bits, outs, axes, scratch):
    count = len(outs)
    bufs, scratch = scratch[:count], scratch[count:]
    landings = [scratch[index * count : (index + 1) * count] for index in range(bits)]
    return PlaneSum(
        bits, list(zip(bufs, axes)), list(zip(outs, axes)), landings, scratch[bits * count]
    )


class SmallSum:
    def __init__(self, flips, peers, total_ref, landing, everyone, sems, peer_sems):
        self.flips, self.peers, self.total_ref = flips, peers, total_ref
        self.landing, self.everyone = landing, everyone
        self.sems, self.peer_sems = sems, peer_sems

    def copy(self, step):
        return pltpu.make_async_remote_copy(
            src_ref=self.total_ref,
            dst_ref=self.landing.at[step],
            send_sem=self.sems.at[0, step],
            recv_sem=self.sems.at[1, step],
            device_id=flip_bit(*self.flips[step])[1],
            device_id_type=MESH,
        )

    def spread(self):
        me = lax.axis_index("dp")
        return [
            pltpu.make_async_remote_copy(
                src_ref=self.everyone.at[me],
                dst_ref=self.everyone.at[me],
                send_sem=self.peer_sems.at[0, step],
                recv_sem=self.peer_sems.at[1, step],
                device_id={"dp": lax.rem(me + step + 1, self.peers)},
                device_id_type=MESH,
            )
            for step in range(self.peers - 1)
        ]

    def advance(self, step):
        if 0 < step <= len(self.flips):
            self.copy(step - 1).wait()
            self.total_ref[...] += self.landing[step - 1]
        if step < len(self.flips):
            self.copy(step).start()
        elif step == len(self.flips):
            self.everyone[lax.axis_index("dp")] = self.total_ref[...]
            for copy in self.spread():
                copy.start()

    def end(self, result_ref):
        for copy in self.spread():
            copy.wait()
        total = self.everyone[0]
        for peer in range(1, self.peers):
            total = total + self.everyone[peer]
        result_ref[...] = total


def line_sems(chips):
    return pltpu.SemaphoreType.DMA((6, chips))


def scatter_scratch(chips, block, depth):
    return [
        pltpu.VMEM((chips, block, depth), BF16),
        pltpu.VMEM((chips, block, depth), BF16),
        pltpu.VMEM((chips + 1, block, depth), BF16),
        line_sems(chips),
    ]


class Drain:
    def __init__(self, sems):
        self.sems, self.copies = sems, []

    def start(self, source, target):
        copy = pltpu.make_async_copy(source, target, self.sems.at[len(self.copies)])
        copy.start()
        self.copies.append(copy)

    def finish(self):
        for copy in self.copies:
            copy.wait()


def near_item(chips, chip, index):
    ahead, behind = chips - 1 - chip, chip
    both = jnp.minimum(ahead, behind)
    near = (index + 1) // 2
    turn = 1 - 2 * lax.rem(index + 1, 2)
    far = jnp.where(ahead > behind, 1, -1)
    return chip + jnp.where(index <= 2 * both, turn * near, far * (index - both))


def near_copies(chip, chips, source, target, sems):
    pair = source.shape[0] // chips
    made = []
    for index in range(3):
        other = chip + index - 1
        rows = pl.ds(pl.multiple_of(jnp.clip(other, 0, chips - 1) * pair, pair), pair)
        copy = pltpu.make_async_copy(source.at[rows, :], target.at[rows, :], sems.at[index])
        made.append((jnp.logical_and(other >= 0, other < chips), copy))
    return made


def project_mix_kernel(
    chips,
    heads_here,
    keep_ref,
    keep_rows_ref,
    tokens_ref,
    norm_ref,
    weight_ref,
    beta_ref,
    conv_ref,
    gain_ref,
    grad_ref,
    *refs,
):
    outs, bufs, refs = refs[:13], refs[13:26], refs[26:]
    held, u_scr, add_scr, load_sem, drain_sems, sems, grad_sems, near_sems = refs
    (
        rows_ref,
        proj_ref,
        query_ref,
        key_ref,
        solve_ref,
        w_ref,
        score_ref,
        map_ref,
        start_ref,
        heads_ref,
        mixed_ref,
        update_ref,
        grads_ref,
    ) = bufs
    load = pltpu.make_async_copy(weight_ref, held, load_sem)
    load.start()
    tokens = tokens_ref[...].astype(F32)
    normed = (tokens * row_scale(tokens) * norm_ref[...]).astype(BF16)
    line_barrier(chips)
    gather = LineGather(chips, rows_ref, sems)
    gather.start(normed)
    load.wait()
    width = heads_here * DH
    rows_total = rows_ref.shape[0]
    groups = rows_total // GROUP
    spans = LEN // SPAN
    sequences = rows_total // LEN
    drain = Drain(drain_sems)

    def project(chip):
        rows = pl.ds(pl.multiple_of(chip * GROUP, GROUP), GROUP)
        here = rows_ref[rows, :]
        for kind in range(3):
            proj_ref[rows, kind * width : (kind + 1) * width] = dot_nn(here, held[kind])
        proj_ref[rows, 3 * width : 3 * width + LANES] = dot_nt(here, beta_ref[...])

    def local_part(group, carry):
        start = pl.multiple_of(group * GROUP, GROUP)
        rows = pl.ds(start, GROUP)
        keep_rows = keep_rows_ref[rows, :]
        row, col = grid_masks()
        for head in range(heads_here):
            cols = slice(head * DH, (head + 1) * DH)
            act_q = jax.nn.silu(
                conv_rows(proj_ref, conv_ref, group, 0, head * DH, head, keep_rows)
            )
            query = (act_q * (unit_scale(act_q) * DH ** (-0.5))).astype(BF16)
            act_k = jax.nn.silu(
                conv_rows(proj_ref, conv_ref, group, 1, width + head * DH, head, keep_rows)
            )
            key = act_k * unit_scale(act_k)
            value = jax.nn.silu(
                conv_rows(proj_ref, conv_ref, group, 2, 2 * width + head * DH, head, keep_rows)
            )
            beta = jax.nn.sigmoid(proj_ref[rows, 3 * width + head : 3 * width + head + 1])
            key_low = key.astype(BF16)
            query_ref[rows, cols] = query
            key_ref[rows, cols] = key_low
            inside = same_block(row, col, SPAN)
            system = jnp.where(
                jnp.logical_and(inside, row > col), dot_nt(key_low, key_low) * beta, 0.0
            )
            score = jnp.where(jnp.logical_and(inside, row >= col), dot_nt(query, key_low), 0.0)
            score_ref[group * heads_here + head] = score.astype(BF16)
            solve = jnp.where(
                row == col, 1.0, jnp.where(same_block(row, col, 2), -system, 0.0)
            )
            size = 2
            while size < SPAN:
                cross = jnp.where(
                    jnp.logical_and(
                        same_block(row, col, 2 * size),
                        jnp.logical_not(same_block(row, col, size)),
                    ),
                    system,
                    0.0,
                )
                solve_low = solve.astype(BF16)
                solve = solve - dot_nn(solve_low, dot_nn(cross, solve_low))
                size *= 2
            solve_low = solve.astype(BF16)
            solve_ref[group * heads_here + head] = solve_low
            both = dot_nn(solve_low, jnp.concatenate([key * beta, value * beta], 1))
            both_low = both.astype(BF16)
            w_ref[rows, cols] = both_low[:, :DH]
            u_scr[rows, cols] = both[:, DH:]
            for piece in range(PER_GROUP):
                part = slice(piece * SPAN, (piece + 1) * SPAN)
                carry_pair = dot_tn(key_low[part], both_low[part])
                slot = (group * PER_GROUP + piece) * heads_here + head
                map_ref[slot] = carry_pair[:, :DH].astype(BF16)
                add_scr[slot] = carry_pair[:, DH:]
        return carry

    def after(step):
        gather.each_new(step, project)
        local_part(near_item(chips, gather.chip, step - 1), 0)

    gather.arrive(gather.chip)
    project(gather.chip)
    gather.hops(after)
    gather_grads = LineGather(chips, grads_ref, grad_sems)
    gather_grads.start(grad_ref[...])
    drain.start(bufs[0], outs[0])
    drain.start(bufs[1], outs[1])
    local_part(near_item(chips, gather.chip, chips - 1), 0)
    for index in range(2, 8):
        drain.start(bufs[index], outs[index])

    def scan_part(span, states):
        ended = []
        for sequence in range(sequences):
            for head in range(heads_here):
                block = sequence * spans + span
                slot = block * heads_here + head
                memory = states[sequence * heads_here + head] * keep_ref[block]
                memory_low = memory.astype(BF16)
                start_ref[slot] = memory_low
                ended.append(memory - dot_nn(map_ref[slot], memory_low) + add_scr[slot])
        return tuple(ended)

    blank = tuple(jnp.zeros((DH, DH), F32) for _ in range(sequences * heads_here))
    lax.fori_loop(0, spans, scan_part, blank)

    drain.start(bufs[8], outs[8])

    def output_part(group, carry):
        start = pl.multiple_of(group * GROUP, GROUP)
        rows = pl.ds(start, GROUP)
        for head in range(heads_here):
            cols = slice(head * DH, (head + 1) * DH)
            query = query_ref[rows, cols]
            w_part = w_ref[rows, cols]
            updates, reads = [], []
            for piece in range(PER_GROUP):
                part = slice(piece * SPAN, (piece + 1) * SPAN)
                slot = (group * PER_GROUP + piece) * heads_here + head
                pair = dot_nn(jnp.concatenate([w_part[part], query[part]], 0), start_ref[slot])
                updates.append(pair[:SPAN])
                reads.append(pair[SPAN:])
            update = (u_scr[rows, cols] - jnp.concatenate(updates, 0)).astype(BF16)
            update_ref[rows, cols] = update
            mixed = jnp.concatenate(reads, 0) + dot_nn(score_ref[group * heads_here + head], update)
            mixed_ref[rows, cols] = mixed
            scale = lax.rsqrt(jnp.mean(mixed * mixed, axis=-1, keepdims=True) + EPSILON)
            heads_ref[rows, cols] = (mixed * scale * gain_ref[...]).astype(BF16)
        return carry

    lax.fori_loop(0, groups, output_part, 0)
    for index in range(9, 12):
        drain.start(bufs[index], outs[index])
    gather.finish()
    gather_grads.arrive(gather.chip)
    gather_grads.hop(1, False)
    near = near_copies(gather.chip, chips, grads_ref, outs[12], near_sems)
    for when, copy in near:
        pl.when(when)(copy.start)
    gather_grads.finish(0, 2)
    for when, copy in near:
        pl.when(when)(copy.wait)
    drain.finish()


def attend_feed_kernel(
    chips,
    heads_ref,
    weight_ref,
    tokens_ref,
    gain_ref,
    gate_up_any,
    down_any,
    grads_any,
    residual_ref,
    *refs,
):
    feed_outs, grad_outs, refs = refs[:3], refs[3:6], refs[6:]
    (stage, held, landing, scatter_sems, gather_sems, grad_sems, rows_ref) = refs[:7]
    (gate_up_ref, down_ref, grads_ref, d_hidden_ref, acc_ref, tile_ref, feed_ref) = refs[7:14]
    load_sems, tile_sems, feed_sems, near_sems = refs[14:]
    block, depth = tokens_ref.shape
    pair = 2 * block
    loads = [
        pltpu.make_async_copy(source, target, load_sems.at[index])
        for index, (source, target) in enumerate(
            ((down_any, down_ref), (gate_up_any, gate_up_ref))
        )
    ]
    gather_grads = LineGather(chips, grads_ref, grad_sems)
    near = near_copies(gather_grads.chip, chips, grads_any, grads_ref, near_sems)
    for when, copy in near:
        pl.when(when)(copy.start)
    for load in loads:
        load.start()
    line_barrier(chips)

    def pair_rows(chip):
        return pl.ds(pl.multiple_of(chip * pair, pair), pair)

    def term(chip, core):
        rows = pl.ds(pl.multiple_of((2 * chip + core) * block, block), block)
        return dot_nn(heads_ref[rows, :], weight_ref[...])

    def back_hidden(index):
        rows = pair_rows(near_item(chips, gather_grads.chip, index))
        d_hidden_ref[rows, :] = dot_nt(grads_ref[rows, :], down_ref[...]).astype(BF16)

    def each(index):
        @pl.when(index == 0)
        def _():
            loads[0].wait()

        back_hidden(index)

        @pl.when(index + 2 < chips)
        def _():
            gather_grads.hop(index + 2)

    for when, copy in near:
        pl.when(when)(copy.wait)
    gather_grads.pass_on(gather_grads.chip - 1, gather_grads.chip + 1)
    scatter = LineScatter(chips, term, stage, held, landing, scatter_sems)
    scatter.run(residual_ref, each)
    residual = residual_ref[...] + tokens_ref[...].astype(F32)
    residual_ref[...] = residual
    gather = LineGather(chips, rows_ref, gather_sems)
    gather.start((residual * row_scale(residual) * gain_ref[...]).astype(BF16))
    back_hidden(chips - 1)
    loads[1].wait()
    acc_ref[...] = jnp.zeros_like(acc_ref)
    gather.arrive(gather.chip)
    tiles = depth // TILE

    def feed_copies(rows):
        return [
            pltpu.make_async_copy(
                feed_ref.at[index], feed_outs[index].at[rows, :], feed_sems.at[index]
            )
            for index in range(3)
        ]

    def feed(chip):
        rows = pair_rows(chip)
        here = rows_ref[rows, :]
        gate = dot_nt(here, gate_up_ref[0])
        upward = dot_nt(here, gate_up_ref[1])
        d_hidden = d_hidden_ref[rows, :].astype(F32)
        sigmoid_gate = jax.nn.sigmoid(gate)
        activated = gate * sigmoid_gate
        feed_ref[0] = (activated * upward).astype(BF16)
        feed_ref[1] = (
            d_hidden * upward * sigmoid_gate * (1.0 + gate * (1.0 - sigmoid_gate))
        ).astype(BF16)
        feed_ref[2] = (d_hidden * activated).astype(BF16)
        for copy in feed_copies(rows):
            copy.start()
        return rows

    right_refs = (grads_ref, rows_ref, rows_ref)

    def add_grads(rows):
        for index, right_ref in enumerate(right_refs):

            def one_tile(tile, carry):
                cols = pl.ds(pl.multiple_of(tile * TILE, TILE), TILE)
                acc_ref[index, :, cols] += dot_tn(feed_ref[index], right_ref[rows, cols])
                return carry

            lax.fori_loop(0, tiles, one_tile, 0)

    def step_feed(step):
        rows = feed(near_item(chips, gather.chip, step))
        add_grads(rows)
        for copy in feed_copies(rows):
            copy.wait()

    step_feed(0)

    def after(step):
        @pl.when(step < chips - 1)
        def _():
            step_feed(step)

    gather.hops(after)
    rows = feed(near_item(chips, gather.chip, chips - 1))
    sent = []
    for index, right_ref in enumerate(right_refs):
        for tile in range(tiles):
            count = index * tiles + tile
            slot = count % 2
            if count >= 2:
                sent[count - 2].wait()
            cols = slice(tile * TILE, (tile + 1) * TILE)
            tile_ref[slot] = (
                acc_ref[index, :, cols] + dot_tn(feed_ref[index], right_ref[rows, cols])
            ).astype(BF16)
            copy = pltpu.make_async_copy(
                tile_ref.at[slot], grad_outs[index].at[:, cols], tile_sems.at[slot]
            )
            copy.start()
            sent.append(copy)
    for copy in sent[-2:] + feed_copies(rows):
        copy.wait()
    gather_grads.finish(2)
    gather.finish()
    scatter.finish()


def feed_back_kernel(
    chips,
    bits,
    flips,
    d_gate_ref,
    d_upward_ref,
    weight_ref,
    residual_ref,
    gain_ref,
    grad_ref,
    heads_ref,
    out_weight_ref,
    *refs,
):
    feed_in, refs = refs[:1], refs[1:]
    d_residual_ref, d_heads_ref, grad_out_ref, grad_gain_ref = refs[:4]
    feed_outs, refs = refs[4:5], refs[5:]
    stage, held, landing, scatter_sems, gather_sems, rows_ref, acc_ref = refs[:7]
    load_sems, drain_sems, summed = refs[7], refs[8], refs[9:10]
    block, depth = residual_ref.shape
    feed = plane_sum(bits, summed, (1,), refs[10:])
    loads = [
        pltpu.make_async_copy(source, feed.bufs[index][0], load_sems.at[index])
        for index, source in enumerate(feed_in)
    ]
    for load in loads:
        load.start()
    line_barrier(chips, flips)
    for load in loads:
        load.wait()
    feed.advance(0)

    def term(chip, core):
        rows = pl.ds(pl.multiple_of((2 * chip + core) * block, block), block)
        return dot_nn(d_gate_ref[rows, :], weight_ref[0]) + dot_nn(
            d_upward_ref[rows, :], weight_ref[1]
        )

    scatter = LineScatter(chips, term, stage, held, landing, scatter_sems)

    def each(index):
        @pl.when(index == chips - 2)
        def _():
            feed.advance(1)

    scatter.run(d_residual_ref, each)
    d_normed = d_residual_ref[...]
    residual = residual_ref[...]
    scale = row_scale(residual)
    hat = residual * scale
    weighted = gain_ref[...] * d_normed
    grad_gain_ref[...] = jnp.sum(d_normed * hat, axis=0, keepdims=True)
    d_residual = grad_ref[...].astype(F32) + scale * (
        weighted - hat * jnp.mean(weighted * hat, axis=-1, keepdims=True)
    )
    d_residual_ref[...] = d_residual
    gather = LineGather(chips, rows_ref, gather_sems)
    gather.start(d_residual.astype(BF16))
    acc_ref[...] = jnp.zeros_like(acc_ref)
    feed.advance(2)
    gather.arrive(gather.chip)

    def use(chip):
        rows = pl.ds(pl.multiple_of(chip * 2 * block, 2 * block), 2 * block)
        here = rows_ref[rows, :]
        d_heads_ref[rows, :] = dot_nt(here, out_weight_ref[...])
        acc_ref[...] += dot_tn(heads_ref[rows, :], here)

    use(gather.chip)

    def after(step):
        gather.each_new(step, use)

        @pl.when(step == max(chips - 2, 1))
        def _():
            feed.advance(3)

    gather.hops(after)
    grad_out_ref[...] = acc_ref[...].astype(BF16)
    gather.finish()
    scatter.finish()
    for step in range(4, 2 * bits + 1):
        feed.advance(step)
    drain = Drain(drain_sems)
    drain.start(summed[0], feed_outs[0])
    drain.finish()


def mixer_backward_kernel(
    chips,
    bits,
    flips,
    heads_here,
    keep_ref,
    keep_rows_ref,
    conv_ref,
    gain_ref,
    residual_ref,
    hidden_any,
    down_any,
    rows_any,
    *refs,
):
    kept_in, mix_in, refs = refs[:11], refs[11:12], refs[12:]
    d_proj_ref, d_logit_ref, grad_conv_ref, grad_gain_ref, grad_beta_ref, out_ref = refs[:6]
    mix_grads, summed, refs = refs[6:9], refs[9:10], refs[10:]
    y_scr, add_scr, end_scr, d_query_scr, d_key_scr, d_conv_scr = refs[:6]
    hidden_ref, down_ref, rows_ref, result = refs[6:10]
    load_sems = refs[10]
    kept, kept_sems = refs[15:26], refs[26]
    (
        proj_ref,
        mixed_ref,
        query_ref,
        key_ref,
        solve_ref,
        w_ref,
        score_ref,
        map_ref,
        start_ref,
        update_ref,
        d_heads_ref,
    ) = kept
    mix = plane_sum(bits, summed, (1,), refs[27:])
    rows_total = proj_ref.shape[0]
    depth = rows_ref.shape[1]
    block = residual_ref.shape[0]
    loads = [
        pltpu.make_async_copy(source, target, load_sems.at[index])
        for index, (source, target) in enumerate(
            (
                (mix_in[0], mix.bufs[0][0]),
                (hidden_any, hidden_ref),
                (down_any, down_ref),
                (rows_any, rows_ref),
            )
        )
    ]
    for load in loads[:3]:
        load.start()
    keeps = [
        pltpu.make_async_copy(source, target, kept_sems.at[index])
        for index, (source, target) in enumerate(zip(kept_in, kept))
    ]
    for keep_load in keeps:
        keep_load.start()
    loads[3].start()
    line_barrier(chips, flips)
    loads[0].wait()
    mix.advance(0)

    def term_down(chip, core):
        rows = pl.ds(pl.multiple_of((2 * chip + core) * block, block), block)
        return dot_nn(hidden_ref[rows, :], down_ref[...])

    scatter = LineScatter(chips, term_down, *refs[11:15])
    loads[1].wait()
    loads[2].wait()
    scatter.begin()
    scatter.step(0)
    for keep_load in keeps:
        keep_load.wait()
    width = heads_here * DH
    groups = rows_total // GROUP
    spans = LEN // SPAN
    sequences = rows_total // LEN
    grad_gain_ref[...] = jnp.zeros_like(grad_gain_ref)
    grad_conv_ref[...] = jnp.zeros_like(grad_conv_ref)

    def local_part(group, carry):
        start = pl.multiple_of(group * GROUP, GROUP)
        rows = pl.ds(start, GROUP)
        row, col = grid_masks()
        for head in range(heads_here):
            cols = slice(head * DH, (head + 1) * DH)
            mixed = mixed_ref[rows, cols]
            d_heads = d_heads_ref[rows, cols]
            scale = lax.rsqrt(jnp.mean(mixed * mixed, axis=-1, keepdims=True) + EPSILON)
            hat = mixed * scale
            grad_gain_ref[...] += jnp.sum(d_heads * hat, axis=0, keepdims=True)
            weighted = gain_ref[...] * d_heads
            d_mixed = scale * (
                weighted - hat * jnp.mean(weighted * hat, axis=-1, keepdims=True)
            )
            d_low = d_mixed.astype(BF16)
            query = query_ref[rows, cols]
            key = key_ref[rows, cols]
            w_part = w_ref[rows, cols]
            inside = jnp.logical_and(same_block(row, col, SPAN), row >= col)
            d_score = jnp.where(inside, dot_nt(d_low, update_ref[rows, cols]), 0.0).astype(BF16)
            y_part = dot_tn(score_ref[group * heads_here + head], d_low)
            y_scr[rows, cols] = y_part
            y_low = y_part.astype(BF16)
            d_key_scr[rows, cols] = dot_tn(d_score, query)
            reads = []
            for piece in range(PER_GROUP):
                part = slice(piece * SPAN, (piece + 1) * SPAN)
                slot = (group * PER_GROUP + piece) * heads_here + head
                add_scr[slot] = dot_tn(
                    jnp.concatenate([query[part], w_part[part]], 0),
                    jnp.concatenate([d_low[part], -y_low[part]], 0),
                )
                reads.append(dot_nt(d_low[part], start_ref[slot]))
            d_query_scr[rows, cols] = dot_nn(d_score, key) + jnp.concatenate(reads, 0)
        return carry

    lax.fori_loop(0, groups, local_part, 0)
    if chips > 2:
        scatter.step(1)
    mix.advance(1)

    def scan_part(step, states):
        span = spans - 1 - step
        begun = []
        for sequence in range(sequences):
            for head in range(heads_here):
                block = sequence * spans + span
                slot = block * heads_here + head
                d_end = states[sequence * heads_here + head]
                d_end_low = d_end.astype(BF16)
                end_scr[slot] = d_end_low
                begun.append(
                    (d_end - dot_tn(map_ref[slot], d_end_low) + add_scr[slot]) * keep_ref[block]
                )
        return tuple(begun)

    blank = tuple(jnp.zeros((DH, DH), F32) for _ in range(sequences * heads_here))
    lax.fori_loop(0, spans, scan_part, blank)
    scatter.steps(2)
    mix.advance(2)

    def finish_part(group, carry):
        start = pl.multiple_of(group * GROUP, GROUP)
        rows = pl.ds(start, GROUP)
        keep_rows = keep_rows_ref[rows, :]
        row, col = grid_masks()
        d_logits = []
        for head in range(heads_here):
            cols = slice(head * DH, (head + 1) * DH)
            beta = jax.nn.sigmoid(proj_ref[rows, 3 * width + head : 3 * width + head + 1])
            key = key_ref[rows, cols]
            update = update_ref[rows, cols]
            reads = []
            for piece in range(PER_GROUP):
                part = slice(piece * SPAN, (piece + 1) * SPAN)
                slot = (group * PER_GROUP + piece) * heads_here + head
                reads.append(dot_nn(key[part], end_scr[slot]))
            d_update = y_scr[rows, cols] + jnp.concatenate(reads, 0)
            d_right = dot_tn(solve_ref[group * heads_here + head], d_update)
            d_value = beta * d_right
            d_value_low = d_value.astype(BF16)
            d_logit = (1.0 - beta) * jnp.sum(
                d_right * update.astype(F32), axis=-1, keepdims=True
            )
            d_logits.append(d_logit)
            inside = jnp.logical_and(same_block(row, col, SPAN), row > col)
            d_inner = jnp.where(inside, dot_nt(d_value_low, update), 0.0)
            reads = []
            for piece in range(PER_GROUP):
                part = slice(piece * SPAN, (piece + 1) * SPAN)
                slot = (group * PER_GROUP + piece) * heads_here + head
                reads.append(
                    dot_nt(
                        jnp.concatenate([update[part], -d_value_low[part]], 1),
                        jnp.concatenate([end_scr[slot], start_ref[slot]], 1),
                    )
                )
            d_key = (
                d_key_scr[rows, cols]
                + jnp.concatenate(reads, 0)
                - dot_nn(d_inner + d_inner.T, key)
            )
            grads = (d_query_scr[rows, cols] * DH ** (-0.5), d_key, d_value)
            for kind in range(3):
                pre = conv_rows(
                    proj_ref, conv_ref, group, kind, kind * width + head * DH, head, keep_rows
                )
                gate = jax.nn.sigmoid(pre)
                act = pre * gate
                d_act = grads[kind]
                if kind < 2:
                    scale = unit_scale(act)
                    hat = act * scale
                    d_act = scale * (d_act - hat * jnp.sum(hat * d_act, axis=-1, keepdims=True))
                first = kind * width + head * DH
                d_conv_scr[rows, first : first + DH] = d_act * gate * (1.0 + pre * (1.0 - gate))
        lane = lax.broadcasted_iota(jnp.int32, (GROUP, LANES), 1)
        spread = jnp.zeros((GROUP, LANES), F32)
        for head in range(heads_here):
            spread = jnp.where(lane == head, d_logits[head], spread)
        d_logit_ref[rows, :] = spread.astype(BF16)
        return carry

    lax.fori_loop(0, groups, finish_part, 0)
    mix.advance(3)
    d_conv_scr[rows_total : rows_total + 8, :] = jnp.zeros((8, 3 * width), F32)

    def conv_part(group, carry):
        start = pl.multiple_of(group * GROUP, GROUP)
        rows = pl.ds(start, GROUP)
        after = pl.ds(pl.multiple_of(start + GROUP, GROUP), 8)
        keep_rows = keep_rows_ref[rows, :]
        keep_after = keep_rows_ref[
            pl.ds(pl.multiple_of(jnp.minimum(start + GROUP, rows_total - 8), 8), 8), :
        ]
        keep_joined = jnp.concatenate([keep_rows, keep_after], 0)
        place = lax.broadcasted_iota(jnp.int32, (GROUP + 8, 1), 0) % SPAN
        for kind in range(3):
            for head in range(heads_here):
                first = kind * width + head * DH
                cols = slice(first, first + DH)
                taps = conv_ref[kind, :, head * DH : (head + 1) * DH]
                here = d_conv_scr[rows, cols]
                joined = jnp.concatenate([here, d_conv_scr[after, cols]], 0)
                total = taps[KCONV - 1 : KCONV] * here
                sums = [jnp.sum(here * proj_ref[rows, cols], axis=0, keepdims=True)]
                for offset in range(1, KCONV):
                    counted = jnp.logical_or(place >= offset, keep_joined > 0.0)
                    masked = jnp.where(counted, joined, 0.0)
                    shifted = pltpu.roll(masked, GROUP + 8 - offset, 0)[:GROUP]
                    total = total + taps[KCONV - 1 - offset : KCONV - offset] * shifted
                    sums.append(
                        jnp.sum(
                            here * earlier_rows(proj_ref, group, first, offset, keep_rows),
                            axis=0,
                            keepdims=True,
                        )
                    )
                d_proj_ref[rows, cols] = total.astype(BF16)
                grad_conv_ref[kind, :, head * DH : (head + 1) * DH] += jnp.concatenate(
                    sums[::-1], 0
                )
        return carry

    lax.fori_loop(0, groups, conv_part, 0)
    loads[3].wait()

    def grad_part(tile, carry):
        cols = pl.ds(pl.multiple_of(tile * TILE, TILE), TILE)
        here = rows_ref[:, cols]
        grads = dot_tn(here, d_proj_ref[...]).astype(BF16)
        for kind in range(3):
            mix_grads[kind][cols, :] = grads[:, kind * width : (kind + 1) * width]
        grad_beta_ref[:, cols] = dot_tn(d_logit_ref[...], here)[:8]
        return carry

    lax.fori_loop(0, depth // TILE, grad_part, 0)
    scatter.end(result)
    out_ref[...] = (residual_ref[...] + result[...]).astype(BF16)
    for step in range(4, 2 * bits + 1):
        mix.advance(step)
    scatter.finish()


def project_back_kernel(
    chips,
    bits,
    flips,
    d_proj_ref,
    d_logit_ref,
    weight_ref,
    beta_ref,
    tokens_ref,
    gain_ref,
    d_residual_ref,
    grad_beta_ref,
    grad_conv_ref,
    part_head_ref,
    part_ffn_ref,
    *refs,
):
    mix_in, refs = refs[:3], refs[3:]
    grad_tokens_ref, gains_ref = refs[:2]
    mix_out, scratch = refs[2:6], refs[6:]
    block, depth = tokens_ref.shape
    mp_flips, peers = flips, 2**bits
    load_sems, scatter_refs, gain_total = scratch[0], scratch[1:5], scratch[5]
    gains = SmallSum(mp_flips, peers, gain_total, *scratch[6:10])
    mix = plane_sum(bits, mix_out, (0, 0, 0, 1), scratch[10:])
    loads = [
        pltpu.make_async_copy(source, mix.bufs[index][0], load_sems.at[index])
        for index, source in enumerate(mix_in)
    ]
    for load in loads:
        load.start()
    small_ref = mix.bufs[3][0]
    taps = jnp.zeros((8, grad_conv_ref.shape[2]), F32)
    small_ref[...] = jnp.zeros_like(small_ref)
    small_ref[:16, :] = jnp.concatenate(
        [grad_beta_ref[...], jnp.zeros((8, depth), F32)], 0
    ).astype(BF16)
    small_ref[16:32, : grad_conv_ref.shape[2]] = jnp.concatenate(
        [grad_conv_ref[0], grad_conv_ref[1], grad_conv_ref[2], taps[:4]], 0
    ).astype(BF16)
    line_barrier(chips, mp_flips, peers)
    for load in loads:
        load.wait()
    width = weight_ref.shape[2]
    mix.advance(0)

    def term(chip, core):
        rows = pl.ds(pl.multiple_of((2 * chip + core) * block, block), block)
        total = dot_nn(d_logit_ref[rows, :], beta_ref[...])
        for kind in range(3):
            total = total + dot_nt(
                d_proj_ref[rows, kind * width : (kind + 1) * width], weight_ref[kind]
            )
        return total

    def each(index):
        @pl.when(index == max(chips - 3, 0))
        def _():
            mix.advance(1)

        @pl.when(index == chips - 2)
        def _():
            mix.advance(2)

    scatter = LineScatter(chips, term, *scatter_refs)
    scatter.run(grad_tokens_ref, each)
    for step in range(3, 2 * bits):
        mix.advance(step)
    d_normed = grad_tokens_ref[...]
    tokens = tokens_ref[...].astype(F32)
    scale = row_scale(tokens)
    hat = tokens * scale
    weighted = gain_ref[...] * d_normed
    gain_total[...] = jnp.zeros_like(gain_total)
    gain_total[0:1, :] = jnp.sum(d_normed * hat, axis=0, keepdims=True)
    gain_total[1:2, :] = part_ffn_ref[...]
    gain_total[2:3, :DH] = part_head_ref[...]
    gains.advance(0)
    grad_tokens_ref[...] = d_residual_ref[...] + scale * (
        weighted - hat * jnp.mean(weighted * hat, axis=-1, keepdims=True)
    )
    for step in range(1, len(mp_flips) + 1):
        gains.advance(step)
    scatter.finish()
    mix.advance(2 * bits)
    gains.end(gains_ref)


def line_call(kernel, name, collective, shapes, scratch, specs, args, out_specs=None):
    return pl.pallas_call(
        kernel,
        out_shape=shapes,
        in_specs=specs,
        out_specs=tuple(out_specs or [whole()] * len(shapes)),
        scratch_shapes=scratch,
        compiler_params=pltpu.CompilerParams(
            collective_id=collective, has_side_effects=True, vmem_limit_bytes=VMEM_LIMIT
        ),
        name=name,
    )(*args)


def widen_kernel(*refs):
    gate_ref, upward_ref, down_ref, q_ref, k_ref, v_ref, out_ref = refs[:7]
    wide_gate_up, wide_down, wide_qkv, wide_out = refs[7:]
    wide_gate_up[0] = gate_ref[...].astype(F32)
    wide_gate_up[1] = upward_ref[...].astype(F32)
    wide_down[...] = down_ref[...].astype(F32)
    for kind, ref in enumerate((q_ref, k_ref, v_ref)):
        wide_qkv[kind] = ref[...].astype(F32)
    wide_out[...] = out_ref[...].astype(F32)


def widen(gate, upward, down, query, key, value, out):
    hidden_width, depth = gate.shape
    width = query.shape[1]
    steps = depth // LANES // 2
    across = pl.BlockSpec((hidden_width, depth // steps), lambda step: (0, step))
    along = pl.BlockSpec((depth // steps, width), lambda step: (step, 0))
    flat = pl.BlockSpec((width, depth // steps), lambda step: (0, step))
    like = jax.ShapeDtypeStruct
    return pl.pallas_call(
        widen_kernel,
        out_shape=(
            like((2, hidden_width, depth), F32),
            like((hidden_width, depth), F32),
            like((3, depth, width), F32),
            like((width, depth), F32),
        ),
        grid=(steps,),
        in_specs=[across] * 3 + [along] * 3 + [flat],
        out_specs=(
            pl.BlockSpec((2, hidden_width, depth // steps), lambda step: (0, 0, step)),
            across,
            pl.BlockSpec((3, depth // steps, width), lambda step: (0, step, 0)),
            flat,
        ),
        compiler_params=pltpu.CompilerParams(vmem_limit_bytes=VMEM_LIMIT),
        name="widen_sums",
    )(gate, upward, down, query, key, value, out)


def body(
    chips,
    dp_bits,
    mp_bits,
    tokens,
    grad_out,
    doc_ids,
    norm_gain,
    qkv_weight,
    beta_weight,
    conv_weight,
    head_gain,
    out_weight,
    ffn_gain,
    gate_up_weight,
    down_weight,
):
    width = qkv_weight.shape[2]
    heads_here = width // DH
    block, depth = tokens.shape
    rows_total = 2 * chips * block
    hidden_width = down_weight.shape[0]
    like = jax.ShapeDtypeStruct
    any_spec = pl.BlockSpec(memory_space=pl.ANY)
    norm_row = norm_gain.reshape(1, depth)
    ffn_row = ffn_gain.reshape(1, depth)
    beta_pad = jnp.pad(beta_weight.T, ((0, LANES - heads_here), (0, 0)))
    gate_up_rows = jnp.swapaxes(gate_up_weight, 1, 2)
    keep = span_keep(doc_ids)
    keep_rows = jnp.repeat(keep, SPAN)[:, None]

    f32_rows = pltpu.VMEM((rows_total, width), F32)
    grids = rows_total // GROUP * heads_here
    slots = rows_total // SPAN * heads_here
    mix_shapes = (
        like((rows_total, depth), BF16),
        like((rows_total, 3 * width + LANES), F32),
        like((rows_total, width), BF16),
        like((rows_total, width), BF16),
        like((grids, GROUP, GROUP), BF16),
        like((rows_total, width), BF16),
        like((grids, GROUP, GROUP), BF16),
        like((slots, DH, DH), BF16),
        like((slots, DH, DH), BF16),
        like((rows_total, width), BF16),
        like((rows_total, width), F32),
        like((rows_total, width), BF16),
        like((rows_total, depth), BF16),
    )
    rows_one, projected, query, key, solve, w_part, score, maps, starts, *rest = (
        line_call(
            functools.partial(project_mix_kernel, chips, heads_here),
            "project_mix",
            1,
            mix_shapes,
            [pltpu.VMEM(shape.shape, shape.dtype) for shape in mix_shapes]
            + [
                pltpu.VMEM(qkv_weight.shape, BF16),
                f32_rows,
                pltpu.VMEM((slots, DH, DH), F32),
                pltpu.SemaphoreType.DMA,
                pltpu.SemaphoreType.DMA((len(mix_shapes),)),
                line_sems(chips),
                line_sems(chips),
                pltpu.SemaphoreType.DMA((3,)),
            ],
            [pl.BlockSpec(memory_space=pltpu.SMEM)] + [whole()] * 3 + [any_spec] + [whole()] * 4,
            (
                keep,
                keep_rows,
                tokens,
                norm_row,
                qkv_weight,
                beta_pad,
                conv_weight,
                head_gain.reshape(1, DH),
                grad_out,
            ),
            [any_spec] * len(mix_shapes),
        )
    )
    heads_out, mixed, update, grads_all = rest
    kept = (mixed, query, key, solve, w_part, score, maps, starts, update)
    feed_shape = like((rows_total, hidden_width), BF16)
    grad_shape = like((hidden_width, depth), BF16)
    residual, hidden, d_gate, d_upward, *feed_grads = line_call(
        functools.partial(attend_feed_kernel, chips),
        "attend_feed",
        2,
        (like((block, depth), F32),) + (feed_shape,) * 3 + (grad_shape,) * 3,
        scatter_scratch(chips, block, depth)
        + [
            line_sems(chips),
            line_sems(chips),
            pltpu.VMEM((rows_total, depth), BF16),
            pltpu.VMEM(gate_up_rows.shape, BF16),
            pltpu.VMEM(down_weight.shape, BF16),
            pltpu.VMEM((rows_total, depth), BF16),
            pltpu.VMEM((rows_total, hidden_width), BF16),
            pltpu.VMEM((3, hidden_width, depth), F32),
            pltpu.VMEM((2, hidden_width, TILE), BF16),
            pltpu.VMEM((3, 2 * block, hidden_width), BF16),
            pltpu.SemaphoreType.DMA((2,)),
            pltpu.SemaphoreType.DMA((2,)),
            pltpu.SemaphoreType.DMA((3,)),
            pltpu.SemaphoreType.DMA((3,)),
        ],
        [whole()] * 4 + [any_spec] * 3,
        (heads_out, out_weight, tokens, ffn_row, gate_up_rows, down_weight, grads_all),
        [whole()] + [any_spec] * 6,
    )
    dp_flips = tuple(("dp", bit) for bit in range(dp_bits))
    mp_flips = tuple(("mp", bit) for bit in range(mp_bits))
    feed_sums = lax.psum(tuple(feed_grads[1:]), "dp")
    d_residual, d_heads, grad_out_weight, part_ffn_gain, sum_down = line_call(
        functools.partial(feed_back_kernel, chips, dp_bits, dp_flips),
        "feed_back",
        3,
        (
            like((block, depth), F32),
            like((rows_total, width), F32),
            like((width, depth), BF16),
            like((1, depth), F32),
        )
        + (grad_shape,),
        scatter_scratch(chips, block, depth)
        + [
            line_sems(chips),
            pltpu.VMEM((rows_total, depth), BF16),
            pltpu.VMEM((width, depth), F32),
            pltpu.SemaphoreType.DMA((1,)),
            pltpu.SemaphoreType.DMA((1,)),
            pltpu.VMEM(grad_shape.shape, BF16),
        ]
        + plane_scratch(dp_bits, [(grad_shape.shape, 1)]),
        [whole()] * 8 + [any_spec],
        (
            d_gate,
            d_upward,
            gate_up_rows,
            residual,
            ffn_row,
            grad_out,
            heads_out,
            out_weight,
            feed_grads[0],
        ),
        [whole()] * 4 + [any_spec],
    )
    qkv_shape = like((depth, width), BF16)
    kept = (projected, *kept, d_heads)
    d_projected, d_logit, grad_conv, part_head_gain, grad_beta, block_out, *sums = line_call(
        functools.partial(mixer_backward_kernel, chips, dp_bits, dp_flips, heads_here),
        "mixer_backward",
        5,
        (
            like((rows_total, 3 * width), BF16),
            like((rows_total, LANES), BF16),
            like(conv_weight.shape, F32),
            like((1, DH), F32),
            like((8, depth), F32),
            like((block, depth), BF16),
        )
        + (qkv_shape,) * 3
        + (like((width, depth), BF16),),
        [
            f32_rows,
            pltpu.VMEM((slots, DH, DH), F32),
            pltpu.VMEM((slots, DH, DH), BF16),
            f32_rows,
            f32_rows,
            pltpu.VMEM((rows_total + 8, 3 * width), F32),
            pltpu.VMEM((rows_total, hidden_width), BF16),
            pltpu.VMEM(down_weight.shape, BF16),
            pltpu.VMEM((rows_total, depth), BF16),
            pltpu.VMEM((block, depth), F32),
            pltpu.SemaphoreType.DMA((4,)),
        ]
        + scatter_scratch(chips, block, depth)
        + [pltpu.VMEM(array.shape, array.dtype) for array in kept]
        + [pltpu.SemaphoreType.DMA((len(kept),))]
        + plane_scratch(dp_bits, [((width, depth), 1)]),
        [pl.BlockSpec(memory_space=pltpu.SMEM)] + [whole()] * 4 + [any_spec] * 15,
        (
            keep,
            keep_rows,
            conv_weight,
            head_gain.reshape(1, DH),
            residual,
            hidden,
            down_weight,
            rows_one,
            *kept,
            grad_out_weight,
        ),
    )
    mix_grads, sum_out = sums[:3], sums[3]
    sum_shapes = (qkv_shape,) * 3 + (like((32, depth), BF16),)
    grad_tokens, gains, *mix_sums = line_call(
        functools.partial(project_back_kernel, chips, dp_bits, mp_flips),
        "project_back",
        4,
        (like((block, depth), F32), like((8, depth), F32), *sum_shapes),
        [pltpu.SemaphoreType.DMA((3,))]
        + scatter_scratch(chips, block, depth)
        + [
            pltpu.VMEM((8, depth), F32),
            pltpu.VMEM((mp_bits, 8, depth), F32),
            pltpu.VMEM((2**dp_bits, 8, depth), F32),
            pltpu.SemaphoreType.DMA((2, mp_bits)),
            pltpu.SemaphoreType.DMA((2, 2**dp_bits - 1)),
        ]
        + plane_scratch(
            dp_bits, [(shape.shape, 1 if index == 3 else 0) for index, shape in enumerate(sum_shapes)]
        ),
        [whole()] * 11 + [any_spec] * 3,
        (
            d_projected,
            d_logit,
            qkv_weight,
            beta_pad,
            tokens,
            norm_row,
            d_residual,
            grad_beta,
            grad_conv,
            part_head_gain,
            part_ffn_gain,
            *mix_grads,
        ),
    )
    small = mix_sums[3].astype(F32)
    sum_beta = small[:heads_here].T
    sum_conv = small[16 : 16 + 3 * KCONV, :width].reshape(3, KCONV, width)
    wide_gate_up, wide_down, wide_qkv, wide_out = widen(*feed_sums, sum_down, *mix_sums[:3], sum_out)
    return (
        block_out,
        grad_tokens,
        gains[0],
        wide_qkv,
        sum_beta,
        sum_conv,
        gains[2, :DH],
        wide_out,
        gains[1],
        jnp.swapaxes(wide_gate_up, 1, 2),
        wide_down,
    )


def solution(mesh):
    in_specs = (
        P(("dp", "mp"), None),
        P(("dp", "mp"), None),
        P("dp"),
        P(),
        P(None, None, "mp"),
        P(None, "mp"),
        P(None, None, "mp"),
        P(),
        P("mp", None),
        P(),
        P(None, None, "mp"),
        P("mp", None),
    )
    out_specs = (
        P(("dp", "mp"), None),
        P(("dp", "mp"), None),
        P(),
        P(None, None, "mp"),
        P(None, "mp"),
        P(None, None, "mp"),
        P(),
        P("mp", None),
        P(),
        P(None, None, "mp"),
        P("mp", None),
    )
    chips = mesh.shape["mp"] // 2
    dp_bits = mesh.shape["dp"].bit_length() - 1
    mp_bits = mesh.shape["mp"].bit_length() - 1
    part = functools.partial(body, chips, dp_bits, mp_bits)
    return jax.shard_map(part, mesh=mesh, in_specs=in_specs, out_specs=out_specs, check_vma=False)
```

```python
import functools

import jax
import jax.numpy as jnp
from jax import lax
from jax.experimental import pallas as pl
from jax.experimental.pallas import tpu as pltpu
from jax.sharding import PartitionSpec as P

DH = 128
KCONV = 4
SPAN = 64
LEN = 1024


EPSILON = 1e-06


def row_scale(values):
    return lax.rsqrt(jnp.mean(values * values, axis=-1, keepdims=True) + EPSILON)


BF16 = jnp.bfloat16
F32 = jnp.float32
GROUP = 256
LANES = 128
PER_GROUP = GROUP // SPAN


def dot_nn(left, right):
    return lax.dot_general(
        left.astype(BF16), right.astype(BF16), (((1,), (0,)), ((), ())), preferred_element_type=F32
    )


def dot_nt(left, right):
    return lax.dot_general(
        left.astype(BF16), right.astype(BF16), (((1,), (1,)), ((), ())), preferred_element_type=F32
    )


def dot_tn(left, right):
    return lax.dot_general(
        left.astype(BF16), right.astype(BF16), (((0,), (0,)), ((), ())), preferred_element_type=F32
    )


def span_keep(ids_ref, block):
    first = block * SPAN
    same = ids_ref[first] == ids_ref[jnp.maximum(first - 1, 0)]
    return jnp.where(jnp.logical_and(same, lax.rem(first, LEN) != 0), 1.0, 0.0)


def span_rows(ids_ref, group):
    piece = lax.broadcasted_iota(jnp.int32, (GROUP, 1), 0) // SPAN
    rows = jnp.zeros((GROUP, 1), F32)
    for index in range(PER_GROUP):
        rows = jnp.where(piece == index, span_keep(ids_ref, group * PER_GROUP + index), rows)
    return rows


def grid_masks():
    row = lax.broadcasted_iota(jnp.int32, (GROUP, GROUP), 0)
    col = lax.broadcasted_iota(jnp.int32, (GROUP, GROUP), 1)
    return row, col


def same_block(row, col, size):
    return (row // size) == (col // size)


def tap_rows(offset, keep_rows):
    place = lax.broadcasted_iota(jnp.int32, (GROUP, 1), 0) % SPAN
    return jnp.logical_or(place >= offset, keep_rows > 0.0)


def earlier_rows(ref, group, first_col, offset, keep_rows):
    start = pl.multiple_of(group * GROUP, GROUP)
    prior = pl.multiple_of(jnp.maximum(start - 8, 0), 8)
    cols = slice(first_col, first_col + DH)
    joined = jnp.concatenate([ref[pl.ds(prior, 8), cols], ref[pl.ds(start, GROUP), cols]], 0)
    shifted = pltpu.roll(joined, offset, 0)[8:]
    return jnp.where(tap_rows(offset, keep_rows), shifted, 0.0)


def conv_rows(ref, conv_ref, group, kind, first_col, head, keep_rows):
    taps = conv_ref[kind, :, head * DH : (head + 1) * DH]
    start = pl.multiple_of(group * GROUP, GROUP)
    running = taps[KCONV - 1 : KCONV] * ref[pl.ds(start, GROUP), first_col : first_col + DH]
    for offset in range(1, KCONV):
        running = running + taps[KCONV - 1 - offset : KCONV - offset] * earlier_rows(
            ref, group, first_col, offset, keep_rows
        )
    return running


def unit_scale(values):
    return lax.rsqrt(jnp.sum(values * values, axis=-1, keepdims=True) + EPSILON)


VMEM_LIMIT = 60 * 1024 * 1024


def whole():
    return pl.BlockSpec(memory_space=pltpu.VMEM)


MESH = pl.DeviceIdType.MESH
TILE = 512
CORE, RIGHT, LEFT = 0, 1, 2


def line_place():
    me = lax.axis_index("mp")
    core = lax.rem(me, 2)
    return me, me // 2, core


def flip_bit(axis, bit):
    place = lax.axis_index(axis)
    scale = 2**bit
    mine = lax.rem(place // scale, 2)
    return mine, {axis: place + (1 - 2 * mine) * scale}


def line_barrier(chips, flips=(), peers=1):
    me, chip, core = line_place()
    barrier = pltpu.get_barrier_semaphore()
    for axis, bit in flips:
        pl.semaphore_signal(
            barrier, inc=1, device_id=flip_bit(axis, bit)[1], device_id_type=MESH
        )
    for step in range(1, peers):
        place = lax.rem(lax.axis_index("dp") + step, peers)
        pl.semaphore_signal(barrier, inc=1, device_id={"dp": place}, device_id_type=MESH)

    def greet(other):
        pl.semaphore_signal(barrier, inc=1, device_id={"mp": other}, device_id_type=MESH)

    greet(me + 1 - 2 * core)

    @pl.when(chip > 0)
    def _():
        greet(me - 2)

    @pl.when(chip < chips - 1)
    def _():
        greet(me + 2)

    beside = (chip > 0).astype(jnp.int32) + (chip < chips - 1).astype(jnp.int32)
    pl.semaphore_wait(barrier, beside + len(flips) + peers)


def line_target(kind):
    me, chip, core = line_place()
    return {CORE: me + 1 - 2 * core, RIGHT: me + 2, LEFT: me - 2}[kind]


class LineGather:
    def __init__(self, chips, out_ref, sems):
        self.chips, self.out_ref, self.sems = chips, out_ref, sems
        self.block = out_ref.shape[0] // (2 * chips)
        self.me, self.chip, self.core = line_place()

    def rows(self, chip, core):
        return pl.ds(pl.multiple_of((2 * chip + core) * self.block, self.block), self.block)

    def copy(self, kind, chip, core):
        part = self.out_ref.at[self.rows(chip, core), :]
        return pltpu.make_async_remote_copy(
            src_ref=part,
            dst_ref=part,
            send_sem=self.sems.at[2 * kind, chip],
            recv_sem=self.sems.at[2 * kind + 1, chip],
            device_id={"mp": line_target(kind)},
            device_id_type=MESH,
        )

    def start(self, block):
        self.out_ref[self.rows(self.chip, self.core), :] = block

        @pl.when(self.chip < self.chips - 1)
        def _():
            self.copy(RIGHT, self.chip, self.core).start()

        @pl.when(self.chip > 0)
        def _():
            self.copy(LEFT, self.chip, self.core).start()

        self.copy(CORE, self.chip, self.core).start()

    def arrive(self, chip):
        self.copy(CORE, chip, 1 - self.core).wait_recv()

    def each_new(self, step, use):
        behind, ahead = self.chip - step, self.chip + step

        @pl.when(behind >= 0)
        def _():
            use(behind)

        @pl.when(ahead < self.chips)
        def _():
            use(ahead)

    def pass_on(self, behind, ahead):
        @pl.when(jnp.logical_and(behind >= 0, self.chip < self.chips - 1))
        def _():
            self.copy(RIGHT, behind, self.core).start()

        @pl.when(jnp.logical_and(ahead < self.chips, self.chip > 0))
        def _():
            self.copy(LEFT, ahead, self.core).start()

    def hop(self, step, forward=True):
        behind, ahead = self.chip - step, self.chip + step

        @pl.when(behind >= 0)
        def _():
            self.copy(RIGHT, behind, self.core).wait_recv()

        @pl.when(ahead < self.chips)
        def _():
            self.copy(LEFT, ahead, self.core).wait_recv()

        if forward:
            self.pass_on(behind, ahead)

        self.each_new(step, lambda chip: self.copy(CORE, chip, self.core).start())
        self.each_new(step, self.arrive)

    def hops(self, after):
        def one_hop(step, carry):
            self.hop(step)
            after(step)
            return carry

        lax.fori_loop(1, self.chips, one_hop, 0)

    def finish(self, first=0, end=None):
        end = self.chips if end is None else end

        def sent(chip, carry):
            apart = jnp.abs(chip - self.chip)
            relay = jnp.logical_and(apart >= first - 1, apart < end - 1)
            if first == 0:
                relay = jnp.logical_or(relay, apart == 0)
            to_right = jnp.logical_and(chip <= self.chip, self.chip < self.chips - 1)
            to_left = jnp.logical_and(chip >= self.chip, self.chip > 0)

            @pl.when(jnp.logical_and(relay, to_right))
            def _():
                self.copy(RIGHT, chip, self.core).wait_send()

            @pl.when(jnp.logical_and(relay, to_left))
            def _():
                self.copy(LEFT, chip, self.core).wait_send()

            @pl.when(jnp.logical_and(apart >= first, apart < end))
            def _():
                self.copy(CORE, chip, self.core).wait_send()

            return carry

        lax.fori_loop(0, self.chips, sent, 0)


class LineScatter:
    def __init__(self, chips, term, stage, held, landing, sems):
        self.chips, self.term = chips, term
        self.stage, self.held, self.landing, self.sems = stage, held, landing, sems
        self.me, self.chip, self.core = line_place()

    def left_slot(self, chip, receiver):
        return jnp.where(chip == receiver, self.chips, chip)

    def copy(self, kind, chip):
        source = (self.stage if kind == CORE else self.held).at[chip]
        if kind == CORE:
            target = self.held.at[chip]
        elif kind == RIGHT:
            target = self.landing.at[chip]
        else:
            target = self.landing.at[self.left_slot(chip, self.chip - 1)]
        return pltpu.make_async_remote_copy(
            src_ref=source,
            dst_ref=target,
            send_sem=self.sems.at[2 * kind, chip],
            recv_sem=self.sems.at[2 * kind + 1, chip],
            device_id={"mp": line_target(kind)},
            device_id_type=MESH,
        )

    def exchange(self, chip):
        self.stage[chip] = self.term(chip, 1 - self.core).astype(BF16)
        self.copy(CORE, chip).start()

    def collect(self, chip):
        own = self.term(chip, self.core)
        self.copy(CORE, chip).wait_recv()
        return own + self.held[chip].astype(F32)

    def pass_on(self, kind, chip, first):
        both = self.collect(chip)

        @pl.when(first)
        def _():
            self.held[chip] = both.astype(BF16)

        @pl.when(jnp.logical_not(first))
        def _():
            self.copy(kind, chip).wait_recv()
            self.held[chip] = (both + self.landing[chip].astype(F32)).astype(BF16)

        self.copy(kind, chip).start()

    def exchange_pair(self, step):
        @pl.when(self.chip + step < self.chips)
        def _():
            self.exchange(self.chip + step)

        @pl.when(self.chip - step >= 0)
        def _():
            self.exchange(self.chip - step)

    def begin(self):
        self.exchange_pair(self.chips - 1)

    def step(self, index):
        last = self.chips - 1
        step = last - index

        @pl.when(step > 1)
        def _():
            self.exchange_pair(step - 1)

        @pl.when(self.chip + step < self.chips)
        def _():
            self.pass_on(RIGHT, self.chip + step, self.chip == 0)

        @pl.when(self.chip - step >= 0)
        def _():
            self.pass_on(LEFT, self.chip - step, self.chip == last)

    def steps(self, first, each=None):
        def one_step(index, carry):
            self.step(index)
            if each is not None:
                each(index)
            return carry

        lax.fori_loop(first, self.chips - 1, one_step, 0)

    def end(self, result_ref):
        self.exchange(self.chip)
        result_ref[...] = self.collect(self.chip)

        @pl.when(self.chip > 0)
        def _():
            self.copy(RIGHT, self.chip).wait_recv()
            result_ref[...] += self.landing[self.chip].astype(F32)

        @pl.when(self.chip < self.chips - 1)
        def _():
            self.copy(LEFT, self.chip).wait_recv()
            result_ref[...] += self.landing[self.chips].astype(F32)

    def run(self, result_ref, each=None):
        self.begin()
        self.steps(0, each)
        self.end(result_ref)

    def finish(self):
        def sent(chip, carry):
            @pl.when(chip > self.chip)
            def _():
                self.copy(RIGHT, chip).wait_send()

            @pl.when(chip < self.chip)
            def _():
                self.copy(LEFT, chip).wait_send()

            self.copy(CORE, chip).wait_send()
            return carry

        lax.fori_loop(0, self.chips, sent, 0)


class PlaneSum:
    def __init__(self, bits, bufs, outs, landings, sems):
        self.bits, self.bufs, self.outs = bits, bufs, outs
        self.landings, self.sems = landings, sems
        self.orders = (tuple(range(bits)), tuple(reversed(range(bits))))
        self.half = bufs[0][0].shape[bufs[0][1]] // 2

    def span(self, part, level):
        start = part * self.half
        for index in range(level):
            mine, _ = flip_bit("dp", self.orders[part][index])
            start = start + mine * (self.half >> (index + 1))
        return start

    def view(self, pairs, array, start, size):
        ref, axis = pairs[array]
        where = pl.ds(pl.multiple_of(start, size), size)
        return ref.at[where, :] if axis == 0 else ref.at[:, where]

    def pieces(self, part, index):
        mine, target = flip_bit("dp", self.orders[part][index])
        size = self.half >> (index + 1)
        start = self.span(part, index)
        return target, size, start + mine * size, start + (1 - mine) * size

    def copies(self, step):
        made = []
        for part in range(2):
            index = step if step < self.bits else 2 * self.bits - 1 - step
            target, size, kept, given = self.pieces(part, index)
            for array in range(len(self.bufs)):
                if step < self.bits:
                    source = self.view(self.bufs, array, given, size)
                    landing = self.landings[index][array].at[part]
                else:
                    source = self.view(self.outs, array, kept, size)
                    landing = source
                made.append(
                    pltpu.make_async_remote_copy(
                        src_ref=source,
                        dst_ref=landing,
                        send_sem=self.sems.at[0, part, step, array],
                        recv_sem=self.sems.at[1, part, step, array],
                        device_id=target,
                        device_id_type=MESH,
                    )
                )
        return made

    def advance(self, step, go=True):
        if step > 0:
            for copy in self.copies(step - 1):
                copy.wait()
            if step - 1 < self.bits:
                for part in range(2):
                    _, size, kept, _ = self.pieces(part, step - 1)
                    for array in range(len(self.bufs)):
                        here = self.view(self.bufs, array, kept, size)
                        ended = self.outs if step == self.bits else self.bufs
                        self.view(ended, array, kept, size)[...] = (
                            here[...].astype(F32)
                            + self.landings[step - 1][array][part].astype(F32)
                        ).astype(BF16)
        if go and step < 2 * self.bits:
            for copy in self.copies(step):
                copy.start()


def plane_scratch(bits, shapes):
    made = [pltpu.VMEM(shape, BF16) for shape, _ in shapes]
    for index in range(bits):
        for shape, axis in shapes:
            size = list(shape)
            size[axis] = size[axis] >> (index + 2)
            made.append(pltpu.VMEM((2, *size), BF16))
    return made + [pltpu.SemaphoreType.DMA((2, 2, 2 * bits, len(shapes)))]


def plane_sum(bits, outs, axes, scratch):
    count = len(outs)
    bufs, scratch = scratch[:count], scratch[count:]
    landings = [scratch[index * count : (index + 1) * count] for index in range(bits)]
    return PlaneSum(
        bits, list(zip(bufs, axes)), list(zip(outs, axes)), landings, scratch[bits * count]
    )


class SmallSum:
    def __init__(self, flips, peers, total_ref, landing, everyone, sems, peer_sems):
        self.flips, self.peers, self.total_ref = flips, peers, total_ref
        self.landing, self.everyone = landing, everyone
        self.sems, self.peer_sems = sems, peer_sems

    def copy(self, step):
        return pltpu.make_async_remote_copy(
            src_ref=self.total_ref,
            dst_ref=self.landing.at[step],
            send_sem=self.sems.at[0, step],
            recv_sem=self.sems.at[1, step],
            device_id=flip_bit(*self.flips[step])[1],
            device_id_type=MESH,
        )

    def spread(self):
        me = lax.axis_index("dp")
        return [
            pltpu.make_async_remote_copy(
                src_ref=self.everyone.at[me],
                dst_ref=self.everyone.at[me],
                send_sem=self.peer_sems.at[0, step],
                recv_sem=self.peer_sems.at[1, step],
                device_id={"dp": lax.rem(me + step + 1, self.peers)},
                device_id_type=MESH,
            )
            for step in range(self.peers - 1)
        ]

    def advance(self, step):
        if 0 < step <= len(self.flips):
            self.copy(step - 1).wait()
            self.total_ref[...] += self.landing[step - 1]
        if step < len(self.flips):
            self.copy(step).start()
        elif step == len(self.flips):
            self.everyone[lax.axis_index("dp")] = self.total_ref[...]
            for copy in self.spread():
                copy.start()

    def end(self, result_ref):
        for copy in self.spread():
            copy.wait()
        total = self.everyone[0]
        for peer in range(1, self.peers):
            total = total + self.everyone[peer]
        result_ref[...] = total


def line_sems(chips):
    return pltpu.SemaphoreType.DMA((6, chips))


def scatter_scratch(chips, block, depth):
    return [
        pltpu.VMEM((chips, block, depth), BF16),
        pltpu.VMEM((chips, block, depth), BF16),
        pltpu.VMEM((chips + 1, block, depth), BF16),
        line_sems(chips),
    ]


class Drain:
    def __init__(self, sems):
        self.sems, self.copies = sems, []

    def start(self, source, target):
        copy = pltpu.make_async_copy(source, target, self.sems.at[len(self.copies)])
        copy.start()
        self.copies.append(copy)

    def finish(self):
        for copy in self.copies:
            copy.wait()


def near_item(chips, chip, index):
    ahead, behind = chips - 1 - chip, chip
    both = jnp.minimum(ahead, behind)
    near = (index + 1) // 2
    turn = 1 - 2 * lax.rem(index + 1, 2)
    far = jnp.where(ahead > behind, 1, -1)
    return chip + jnp.where(index <= 2 * both, turn * near, far * (index - both))


def near_copies(chip, chips, source, target, sems):
    pair = source.shape[0] // chips
    made = []
    for index in range(3):
        other = chip + index - 1
        rows = pl.ds(pl.multiple_of(jnp.clip(other, 0, chips - 1) * pair, pair), pair)
        copy = pltpu.make_async_copy(source.at[rows, :], target.at[rows, :], sems.at[index])
        made.append((jnp.logical_and(other >= 0, other < chips), copy))
    return made


def project_mix_kernel(
    chips,
    heads_here,
    ids_ref,
    tokens_ref,
    norm_ref,
    weight_ref,
    beta_ref,
    conv_ref,
    gain_ref,
    grad_ref,
    *refs,
):
    outs, bufs, refs = refs[:13], refs[13:26], refs[26:]
    held, u_scr, add_scr, load_sem, drain_sems, sems, grad_sems, near_sems = refs
    (
        rows_ref,
        proj_ref,
        query_ref,
        key_ref,
        solve_ref,
        w_ref,
        score_ref,
        map_ref,
        start_ref,
        heads_ref,
        mixed_ref,
        update_ref,
        grads_ref,
    ) = bufs
    load = pltpu.make_async_copy(weight_ref, held, load_sem)
    load.start()
    tokens = tokens_ref[...].astype(F32)
    normed = (tokens * row_scale(tokens) * norm_ref[...]).astype(BF16)
    line_barrier(chips)
    gather = LineGather(chips, rows_ref, sems)
    gather.start(normed)
    load.wait()
    width = heads_here * DH
    rows_total = rows_ref.shape[0]
    groups = rows_total // GROUP
    spans = LEN // SPAN
    sequences = rows_total // LEN
    drain = Drain(drain_sems)

    def project(chip):
        rows = pl.ds(pl.multiple_of(chip * GROUP, GROUP), GROUP)
        here = rows_ref[rows, :]
        for kind in range(3):
            proj_ref[rows, kind * width : (kind + 1) * width] = dot_nn(here, held[kind])
        proj_ref[rows, 3 * width : 3 * width + LANES] = dot_nt(here, beta_ref[...])

    def local_part(group, carry):
        start = pl.multiple_of(group * GROUP, GROUP)
        rows = pl.ds(start, GROUP)
        keep_rows = span_rows(ids_ref, group)
        row, col = grid_masks()
        for head in range(heads_here):
            cols = slice(head * DH, (head + 1) * DH)
            act_q = jax.nn.silu(
                conv_rows(proj_ref, conv_ref, group, 0, head * DH, head, keep_rows)
            )
            query = (act_q * (unit_scale(act_q) * DH ** (-0.5))).astype(BF16)
            act_k = jax.nn.silu(
                conv_rows(proj_ref, conv_ref, group, 1, width + head * DH, head, keep_rows)
            )
            key = act_k * unit_scale(act_k)
            value = jax.nn.silu(
                conv_rows(proj_ref, conv_ref, group, 2, 2 * width + head * DH, head, keep_rows)
            )
            beta = jax.nn.sigmoid(proj_ref[rows, 3 * width + head : 3 * width + head + 1])
            key_low = key.astype(BF16)
            query_ref[rows, cols] = query
            key_ref[rows, cols] = key_low
            inside = same_block(row, col, SPAN)
            system = jnp.where(
                jnp.logical_and(inside, row > col), dot_nt(key_low, key_low) * beta, 0.0
            )
            score = jnp.where(jnp.logical_and(inside, row >= col), dot_nt(query, key_low), 0.0)
            score_ref[group * heads_here + head] = score.astype(BF16)
            solve = jnp.where(
                row == col, 1.0, jnp.where(same_block(row, col, 2), -system, 0.0)
            )
            size = 2
            while size < SPAN:
                cross = jnp.where(
                    jnp.logical_and(
                        same_block(row, col, 2 * size),
                        jnp.logical_not(same_block(row, col, size)),
                    ),
                    system,
                    0.0,
                )
                solve_low = solve.astype(BF16)
                solve = solve - dot_nn(solve_low, dot_nn(cross, solve_low))
                size *= 2
            solve_low = solve.astype(BF16)
            solve_ref[group * heads_here + head] = solve_low
            both = dot_nn(solve_low, jnp.concatenate([key * beta, value * beta], 1))
            both_low = both.astype(BF16)
            w_ref[rows, cols] = both_low[:, :DH]
            u_scr[rows, cols] = both[:, DH:]
            for piece in range(PER_GROUP):
                part = slice(piece * SPAN, (piece + 1) * SPAN)
                carry_pair = dot_tn(key_low[part], both_low[part])
                slot = (group * PER_GROUP + piece) * heads_here + head
                map_ref[slot] = carry_pair[:, :DH].astype(BF16)
                add_scr[slot] = carry_pair[:, DH:]
        return carry

    def after(step):
        gather.each_new(step, project)
        local_part(near_item(chips, gather.chip, step - 1), 0)

    gather.arrive(gather.chip)
    project(gather.chip)
    gather.hops(after)
    gather_grads = LineGather(chips, grads_ref, grad_sems)
    gather_grads.start(grad_ref[...])
    drain.start(bufs[0], outs[0])
    drain.start(bufs[1], outs[1])
    local_part(near_item(chips, gather.chip, chips - 1), 0)
    for index in range(2, 8):
        drain.start(bufs[index], outs[index])

    def scan_part(span, states):
        ended = []
        for sequence in range(sequences):
            for head in range(heads_here):
                block = sequence * spans + span
                slot = block * heads_here + head
                memory = states[sequence * heads_here + head] * span_keep(ids_ref, block)
                memory_low = memory.astype(BF16)
                start_ref[slot] = memory_low
                ended.append(memory - dot_nn(map_ref[slot], memory_low) + add_scr[slot])
        return tuple(ended)

    blank = tuple(jnp.zeros((DH, DH), F32) for _ in range(sequences * heads_here))
    lax.fori_loop(0, spans, scan_part, blank)

    drain.start(bufs[8], outs[8])

    def output_part(group, carry):
        start = pl.multiple_of(group * GROUP, GROUP)
        rows = pl.ds(start, GROUP)
        for head in range(heads_here):
            cols = slice(head * DH, (head + 1) * DH)
            query = query_ref[rows, cols]
            w_part = w_ref[rows, cols]
            updates, reads = [], []
            for piece in range(PER_GROUP):
                part = slice(piece * SPAN, (piece + 1) * SPAN)
                slot = (group * PER_GROUP + piece) * heads_here + head
                pair = dot_nn(jnp.concatenate([w_part[part], query[part]], 0), start_ref[slot])
                updates.append(pair[:SPAN])
                reads.append(pair[SPAN:])
            update = (u_scr[rows, cols] - jnp.concatenate(updates, 0)).astype(BF16)
            update_ref[rows, cols] = update
            mixed = jnp.concatenate(reads, 0) + dot_nn(score_ref[group * heads_here + head], update)
            mixed_ref[rows, cols] = mixed
            scale = lax.rsqrt(jnp.mean(mixed * mixed, axis=-1, keepdims=True) + EPSILON)
            heads_ref[rows, cols] = (mixed * scale * gain_ref[...]).astype(BF16)
        return carry

    lax.fori_loop(0, groups, output_part, 0)
    for index in range(9, 12):
        drain.start(bufs[index], outs[index])
    gather.finish()
    gather_grads.arrive(gather.chip)
    gather_grads.hop(1, False)
    near = near_copies(gather.chip, chips, grads_ref, outs[12], near_sems)
    for when, copy in near:
        pl.when(when)(copy.start)
    gather_grads.finish(0, 2)
    for when, copy in near:
        pl.when(when)(copy.wait)
    drain.finish()


def attend_feed_kernel(
    chips,
    heads_ref,
    weight_ref,
    tokens_ref,
    gain_ref,
    gate_up_any,
    down_any,
    grads_any,
    residual_ref,
    *refs,
):
    feed_outs, grad_outs, refs = refs[:3], refs[3:6], refs[6:]
    (stage, held, landing, scatter_sems, gather_sems, grad_sems, rows_ref) = refs[:7]
    (gate_up_ref, down_ref, grads_ref, d_hidden_ref, acc_ref, tile_ref, feed_ref) = refs[7:14]
    load_sems, tile_sems, feed_sems, near_sems = refs[14:]
    block, depth = tokens_ref.shape
    pair = 2 * block
    loads = [
        pltpu.make_async_copy(source, target, load_sems.at[index])
        for index, (source, target) in enumerate(
            ((down_any, down_ref), (gate_up_any, gate_up_ref))
        )
    ]
    gather_grads = LineGather(chips, grads_ref, grad_sems)
    near = near_copies(gather_grads.chip, chips, grads_any, grads_ref, near_sems)
    for when, copy in near:
        pl.when(when)(copy.start)
    for load in loads:
        load.start()
    line_barrier(chips)

    def pair_rows(chip):
        return pl.ds(pl.multiple_of(chip * pair, pair), pair)

    def term(chip, core):
        rows = pl.ds(pl.multiple_of((2 * chip + core) * block, block), block)
        return dot_nn(heads_ref[rows, :], weight_ref[...])

    def back_hidden(index):
        rows = pair_rows(near_item(chips, gather_grads.chip, index))
        d_hidden_ref[rows, :] = dot_nt(grads_ref[rows, :], down_ref[...]).astype(BF16)

    def each(index):
        @pl.when(index == 0)
        def _():
            loads[0].wait()

        back_hidden(index)

        @pl.when(index + 2 < chips)
        def _():
            gather_grads.hop(index + 2)

    for when, copy in near:
        pl.when(when)(copy.wait)
    gather_grads.pass_on(gather_grads.chip - 1, gather_grads.chip + 1)
    scatter = LineScatter(chips, term, stage, held, landing, scatter_sems)
    scatter.run(residual_ref, each)
    residual = residual_ref[...] + tokens_ref[...].astype(F32)
    residual_ref[...] = residual
    gather = LineGather(chips, rows_ref, gather_sems)
    gather.start((residual * row_scale(residual) * gain_ref[...]).astype(BF16))
    back_hidden(chips - 1)
    loads[1].wait()
    acc_ref[...] = jnp.zeros_like(acc_ref)
    gather.arrive(gather.chip)
    tiles = depth // TILE

    def feed_copies(rows):
        return [
            pltpu.make_async_copy(
                feed_ref.at[index], feed_outs[index].at[rows, :], feed_sems.at[index]
            )
            for index in range(3)
        ]

    def feed(chip):
        rows = pair_rows(chip)
        here = rows_ref[rows, :]
        gate = dot_nt(here, gate_up_ref[0])
        upward = dot_nt(here, gate_up_ref[1])
        d_hidden = d_hidden_ref[rows, :].astype(F32)
        sigmoid_gate = jax.nn.sigmoid(gate)
        activated = gate * sigmoid_gate
        feed_ref[0] = (activated * upward).astype(BF16)
        feed_ref[1] = (
            d_hidden * upward * sigmoid_gate * (1.0 + gate * (1.0 - sigmoid_gate))
        ).astype(BF16)
        feed_ref[2] = (d_hidden * activated).astype(BF16)
        for copy in feed_copies(rows):
            copy.start()
        return rows

    right_refs = (grads_ref, rows_ref, rows_ref)

    def add_grads(rows):
        for index, right_ref in enumerate(right_refs):

            def one_tile(tile, carry):
                cols = pl.ds(pl.multiple_of(tile * TILE, TILE), TILE)
                acc_ref[index, :, cols] += dot_tn(feed_ref[index], right_ref[rows, cols])
                return carry

            lax.fori_loop(0, tiles, one_tile, 0)

    def step_feed(step):
        rows = feed(near_item(chips, gather.chip, step))
        add_grads(rows)
        for copy in feed_copies(rows):
            copy.wait()

    step_feed(0)

    def after(step):
        @pl.when(step < chips - 1)
        def _():
            step_feed(step)

    gather.hops(after)
    rows = feed(near_item(chips, gather.chip, chips - 1))
    sent = []
    for index, right_ref in enumerate(right_refs):
        for tile in range(tiles):
            count = index * tiles + tile
            slot = count % 2
            if count >= 2:
                sent[count - 2].wait()
            cols = slice(tile * TILE, (tile + 1) * TILE)
            tile_ref[slot] = (
                acc_ref[index, :, cols] + dot_tn(feed_ref[index], right_ref[rows, cols])
            ).astype(BF16)
            copy = pltpu.make_async_copy(
                tile_ref.at[slot], grad_outs[index].at[:, cols], tile_sems.at[slot]
            )
            copy.start()
            sent.append(copy)
    for copy in sent[-2:] + feed_copies(rows):
        copy.wait()
    gather_grads.finish(2)
    gather.finish()
    scatter.finish()


def feed_back_kernel(
    chips,
    bits,
    flips,
    d_gate_ref,
    d_upward_ref,
    weight_ref,
    residual_ref,
    gain_ref,
    grad_ref,
    heads_ref,
    out_weight_ref,
    *refs,
):
    feed_in, refs = refs[:1], refs[1:]
    d_residual_ref, d_heads_ref, grad_out_ref, grad_gain_ref = refs[:4]
    feed_outs, refs = refs[4:5], refs[5:]
    stage, held, landing, scatter_sems, gather_sems, rows_ref, acc_ref = refs[:7]
    load_sems, drain_sems, summed = refs[7], refs[8], refs[9:10]
    block, depth = residual_ref.shape
    feed = plane_sum(bits, summed, (1,), refs[10:])
    loads = [
        pltpu.make_async_copy(source, feed.bufs[index][0], load_sems.at[index])
        for index, source in enumerate(feed_in)
    ]
    for load in loads:
        load.start()
    line_barrier(chips, flips)
    for load in loads:
        load.wait()
    feed.advance(0)

    def term(chip, core):
        rows = pl.ds(pl.multiple_of((2 * chip + core) * block, block), block)
        return dot_nn(d_gate_ref[rows, :], weight_ref[0]) + dot_nn(
            d_upward_ref[rows, :], weight_ref[1]
        )

    scatter = LineScatter(chips, term, stage, held, landing, scatter_sems)

    def each(index):
        @pl.when(index == chips - 2)
        def _():
            feed.advance(1)

    scatter.run(d_residual_ref, each)
    d_normed = d_residual_ref[...]
    residual = residual_ref[...]
    scale = row_scale(residual)
    hat = residual * scale
    weighted = gain_ref[...] * d_normed
    grad_gain_ref[...] = jnp.sum(d_normed * hat, axis=0, keepdims=True)
    d_residual = grad_ref[...].astype(F32) + scale * (
        weighted - hat * jnp.mean(weighted * hat, axis=-1, keepdims=True)
    )
    d_residual_ref[...] = d_residual
    gather = LineGather(chips, rows_ref, gather_sems)
    gather.start(d_residual.astype(BF16))
    acc_ref[...] = jnp.zeros_like(acc_ref)
    feed.advance(2)
    gather.arrive(gather.chip)

    def use(chip):
        rows = pl.ds(pl.multiple_of(chip * 2 * block, 2 * block), 2 * block)
        here = rows_ref[rows, :]
        d_heads_ref[rows, :] = dot_nt(here, out_weight_ref[...])
        acc_ref[...] += dot_tn(heads_ref[rows, :], here)

    use(gather.chip)

    def after(step):
        gather.each_new(step, use)

        @pl.when(step == max(chips - 2, 1))
        def _():
            feed.advance(3)

    gather.hops(after)
    grad_out_ref[...] = acc_ref[...].astype(BF16)
    gather.finish()
    scatter.finish()
    for step in range(4, 2 * bits + 1):
        feed.advance(step)
    drain = Drain(drain_sems)
    drain.start(summed[0], feed_outs[0])
    drain.finish()


def mixer_backward_kernel(
    chips,
    bits,
    flips,
    heads_here,
    ids_ref,
    conv_ref,
    gain_ref,
    residual_ref,
    hidden_any,
    down_any,
    rows_any,
    *refs,
):
    kept_in, mix_in, refs = refs[:11], refs[11:12], refs[12:]
    d_proj_ref, d_logit_ref, grad_conv_ref, grad_gain_ref, grad_beta_ref, out_ref = refs[:6]
    mix_grads, summed, refs = refs[6:9], refs[9:10], refs[10:]
    y_scr, add_scr, end_scr, d_query_scr, d_key_scr, d_conv_scr = refs[:6]
    hidden_ref, down_ref, rows_ref, result = refs[6:10]
    load_sems = refs[10]
    kept, kept_sems = refs[15:26], refs[26]
    (
        proj_ref,
        mixed_ref,
        query_ref,
        key_ref,
        solve_ref,
        w_ref,
        score_ref,
        map_ref,
        start_ref,
        update_ref,
        d_heads_ref,
    ) = kept
    mix = plane_sum(bits, summed, (1,), refs[27:])
    rows_total = proj_ref.shape[0]
    depth = rows_ref.shape[1]
    block = residual_ref.shape[0]
    loads = [
        pltpu.make_async_copy(source, target, load_sems.at[index])
        for index, (source, target) in enumerate(
            (
                (mix_in[0], mix.bufs[0][0]),
                (hidden_any, hidden_ref),
                (down_any, down_ref),
                (rows_any, rows_ref),
            )
        )
    ]
    for load in loads[:3]:
        load.start()
    keeps = [
        pltpu.make_async_copy(source, target, kept_sems.at[index])
        for index, (source, target) in enumerate(zip(kept_in, kept))
    ]
    for keep_load in keeps:
        keep_load.start()
    loads[3].start()
    line_barrier(chips, flips)
    loads[0].wait()
    mix.advance(0)

    def term_down(chip, core):
        rows = pl.ds(pl.multiple_of((2 * chip + core) * block, block), block)
        return dot_nn(hidden_ref[rows, :], down_ref[...])

    scatter = LineScatter(chips, term_down, *refs[11:15])
    loads[1].wait()
    loads[2].wait()
    scatter.begin()
    scatter.step(0)
    for keep_load in keeps:
        keep_load.wait()
    width = heads_here * DH
    groups = rows_total // GROUP
    spans = LEN // SPAN
    sequences = rows_total // LEN
    grad_gain_ref[...] = jnp.zeros_like(grad_gain_ref)
    grad_conv_ref[...] = jnp.zeros_like(grad_conv_ref)

    def local_part(group, carry):
        start = pl.multiple_of(group * GROUP, GROUP)
        rows = pl.ds(start, GROUP)
        row, col = grid_masks()
        for head in range(heads_here):
            cols = slice(head * DH, (head + 1) * DH)
            mixed = mixed_ref[rows, cols]
            d_heads = d_heads_ref[rows, cols]
            scale = lax.rsqrt(jnp.mean(mixed * mixed, axis=-1, keepdims=True) + EPSILON)
            hat = mixed * scale
            grad_gain_ref[...] += jnp.sum(d_heads * hat, axis=0, keepdims=True)
            weighted = gain_ref[...] * d_heads
            d_mixed = scale * (
                weighted - hat * jnp.mean(weighted * hat, axis=-1, keepdims=True)
            )
            d_low = d_mixed.astype(BF16)
            query = query_ref[rows, cols]
            key = key_ref[rows, cols]
            w_part = w_ref[rows, cols]
            inside = jnp.logical_and(same_block(row, col, SPAN), row >= col)
            d_score = jnp.where(inside, dot_nt(d_low, update_ref[rows, cols]), 0.0).astype(BF16)
            y_part = dot_tn(score_ref[group * heads_here + head], d_low)
            y_scr[rows, cols] = y_part
            y_low = y_part.astype(BF16)
            d_key_scr[rows, cols] = dot_tn(d_score, query)
            reads = []
            for piece in range(PER_GROUP):
                part = slice(piece * SPAN, (piece + 1) * SPAN)
                slot = (group * PER_GROUP + piece) * heads_here + head
                add_scr[slot] = dot_tn(
                    jnp.concatenate([query[part], w_part[part]], 0),
                    jnp.concatenate([d_low[part], -y_low[part]], 0),
                )
                reads.append(dot_nt(d_low[part], start_ref[slot]))
            d_query_scr[rows, cols] = dot_nn(d_score, key) + jnp.concatenate(reads, 0)
        return carry

    lax.fori_loop(0, groups, local_part, 0)
    if chips > 2:
        scatter.step(1)
    mix.advance(1)

    def scan_part(step, states):
        span = spans - 1 - step
        begun = []
        for sequence in range(sequences):
            for head in range(heads_here):
                block = sequence * spans + span
                slot = block * heads_here + head
                d_end = states[sequence * heads_here + head]
                d_end_low = d_end.astype(BF16)
                end_scr[slot] = d_end_low
                begun.append(
                    (d_end - dot_tn(map_ref[slot], d_end_low) + add_scr[slot])
                    * span_keep(ids_ref, block)
                )
        return tuple(begun)

    blank = tuple(jnp.zeros((DH, DH), F32) for _ in range(sequences * heads_here))
    lax.fori_loop(0, spans, scan_part, blank)
    scatter.steps(2)
    mix.advance(2)

    def finish_part(group, carry):
        start = pl.multiple_of(group * GROUP, GROUP)
        rows = pl.ds(start, GROUP)
        keep_rows = span_rows(ids_ref, group)
        row, col = grid_masks()
        d_logits = []
        for head in range(heads_here):
            cols = slice(head * DH, (head + 1) * DH)
            beta = jax.nn.sigmoid(proj_ref[rows, 3 * width + head : 3 * width + head + 1])
            key = key_ref[rows, cols]
            update = update_ref[rows, cols]
            reads = []
            for piece in range(PER_GROUP):
                part = slice(piece * SPAN, (piece + 1) * SPAN)
                slot = (group * PER_GROUP + piece) * heads_here + head
                reads.append(dot_nn(key[part], end_scr[slot]))
            d_update = y_scr[rows, cols] + jnp.concatenate(reads, 0)
            d_right = dot_tn(solve_ref[group * heads_here + head], d_update)
            d_value = beta * d_right
            d_value_low = d_value.astype(BF16)
            d_logit = (1.0 - beta) * jnp.sum(
                d_right * update.astype(F32), axis=-1, keepdims=True
            )
            d_logits.append(d_logit)
            inside = jnp.logical_and(same_block(row, col, SPAN), row > col)
            d_inner = jnp.where(inside, dot_nt(d_value_low, update), 0.0)
            reads = []
            for piece in range(PER_GROUP):
                part = slice(piece * SPAN, (piece + 1) * SPAN)
                slot = (group * PER_GROUP + piece) * heads_here + head
                reads.append(
                    dot_nt(
                        jnp.concatenate([update[part], -d_value_low[part]], 1),
                        jnp.concatenate([end_scr[slot], start_ref[slot]], 1),
                    )
                )
            d_key = (
                d_key_scr[rows, cols]
                + jnp.concatenate(reads, 0)
                - dot_nn(d_inner + d_inner.T, key)
            )
            grads = (d_query_scr[rows, cols] * DH ** (-0.5), d_key, d_value)
            for kind in range(3):
                pre = conv_rows(
                    proj_ref, conv_ref, group, kind, kind * width + head * DH, head, keep_rows
                )
                gate = jax.nn.sigmoid(pre)
                act = pre * gate
                d_act = grads[kind]
                if kind < 2:
                    scale = unit_scale(act)
                    hat = act * scale
                    d_act = scale * (d_act - hat * jnp.sum(hat * d_act, axis=-1, keepdims=True))
                first = kind * width + head * DH
                d_conv_scr[rows, first : first + DH] = d_act * gate * (1.0 + pre * (1.0 - gate))
        lane = lax.broadcasted_iota(jnp.int32, (GROUP, LANES), 1)
        spread = jnp.zeros((GROUP, LANES), F32)
        for head in range(heads_here):
            spread = jnp.where(lane == head, d_logits[head], spread)
        d_logit_ref[rows, :] = spread.astype(BF16)
        return carry

    lax.fori_loop(0, groups, finish_part, 0)
    mix.advance(3)
    d_conv_scr[rows_total : rows_total + 8, :] = jnp.zeros((8, 3 * width), F32)

    def conv_part(group, carry):
        start = pl.multiple_of(group * GROUP, GROUP)
        rows = pl.ds(start, GROUP)
        after = pl.ds(pl.multiple_of(start + GROUP, GROUP), 8)
        keep_rows = span_rows(ids_ref, group)
        follower = jnp.minimum((group + 1) * PER_GROUP, rows_total // SPAN - 1)
        keep_after = jnp.full((8, 1), 1.0, F32) * span_keep(ids_ref, follower)
        keep_joined = jnp.concatenate([keep_rows, keep_after], 0)
        place = lax.broadcasted_iota(jnp.int32, (GROUP + 8, 1), 0) % SPAN
        for kind in range(3):
            for head in range(heads_here):
                first = kind * width + head * DH
                cols = slice(first, first + DH)
                taps = conv_ref[kind, :, head * DH : (head + 1) * DH]
                here = d_conv_scr[rows, cols]
                joined = jnp.concatenate([here, d_conv_scr[after, cols]], 0)
                total = taps[KCONV - 1 : KCONV] * here
                sums = [jnp.sum(here * proj_ref[rows, cols], axis=0, keepdims=True)]
                for offset in range(1, KCONV):
                    counted = jnp.logical_or(place >= offset, keep_joined > 0.0)
                    masked = jnp.where(counted, joined, 0.0)
                    shifted = pltpu.roll(masked, GROUP + 8 - offset, 0)[:GROUP]
                    total = total + taps[KCONV - 1 - offset : KCONV - offset] * shifted
                    sums.append(
                        jnp.sum(
                            here * earlier_rows(proj_ref, group, first, offset, keep_rows),
                            axis=0,
                            keepdims=True,
                        )
                    )
                d_proj_ref[rows, cols] = total.astype(BF16)
                grad_conv_ref[kind, :, head * DH : (head + 1) * DH] += jnp.concatenate(
                    sums[::-1], 0
                )
        return carry

    lax.fori_loop(0, groups, conv_part, 0)
    loads[3].wait()

    def grad_part(tile, carry):
        cols = pl.ds(pl.multiple_of(tile * TILE, TILE), TILE)
        here = rows_ref[:, cols]
        grads = dot_tn(here, d_proj_ref[...]).astype(BF16)
        for kind in range(3):
            mix_grads[kind][cols, :] = grads[:, kind * width : (kind + 1) * width]
        grad_beta_ref[:, cols] = dot_tn(d_logit_ref[...], here)[:8]
        return carry

    lax.fori_loop(0, depth // TILE, grad_part, 0)
    scatter.end(result)
    out_ref[...] = (residual_ref[...] + result[...]).astype(BF16)
    for step in range(4, 2 * bits + 1):
        mix.advance(step)
    scatter.finish()


def project_back_kernel(
    chips,
    bits,
    flips,
    d_proj_ref,
    d_logit_ref,
    weight_ref,
    beta_ref,
    tokens_ref,
    gain_ref,
    d_residual_ref,
    grad_beta_ref,
    grad_conv_ref,
    part_head_ref,
    part_ffn_ref,
    *refs,
):
    mix_in, refs = refs[:3], refs[3:]
    grad_tokens_ref, gains_ref = refs[:2]
    mix_out, scratch = refs[2:6], refs[6:]
    block, depth = tokens_ref.shape
    mp_flips, peers = flips, 2**bits
    load_sems, scatter_refs, gain_total = scratch[0], scratch[1:5], scratch[5]
    gains = SmallSum(mp_flips, peers, gain_total, *scratch[6:10])
    mix = plane_sum(bits, mix_out, (0, 0, 0, 1), scratch[10:])
    loads = [
        pltpu.make_async_copy(source, mix.bufs[index][0], load_sems.at[index])
        for index, source in enumerate(mix_in)
    ]
    for load in loads:
        load.start()
    small_ref = mix.bufs[3][0]
    taps = jnp.zeros((8, grad_conv_ref.shape[2]), F32)
    small_ref[...] = jnp.zeros_like(small_ref)
    small_ref[:16, :] = jnp.concatenate(
        [grad_beta_ref[...], jnp.zeros((8, depth), F32)], 0
    ).astype(BF16)
    small_ref[16:32, : grad_conv_ref.shape[2]] = jnp.concatenate(
        [grad_conv_ref[0], grad_conv_ref[1], grad_conv_ref[2], taps[:4]], 0
    ).astype(BF16)
    line_barrier(chips, mp_flips, peers)
    for load in loads:
        load.wait()
    width = weight_ref.shape[2]
    mix.advance(0)

    def term(chip, core):
        rows = pl.ds(pl.multiple_of((2 * chip + core) * block, block), block)
        total = dot_nn(d_logit_ref[rows, :], beta_ref[...])
        for kind in range(3):
            total = total + dot_nt(
                d_proj_ref[rows, kind * width : (kind + 1) * width], weight_ref[kind]
            )
        return total

    def each(index):
        @pl.when(index == max(chips - 3, 0))
        def _():
            mix.advance(1)

        @pl.when(index == chips - 2)
        def _():
            mix.advance(2)

    scatter = LineScatter(chips, term, *scatter_refs)
    scatter.run(grad_tokens_ref, each)
    for step in range(3, 2 * bits):
        mix.advance(step)
    d_normed = grad_tokens_ref[...]
    tokens = tokens_ref[...].astype(F32)
    scale = row_scale(tokens)
    hat = tokens * scale
    weighted = gain_ref[...] * d_normed
    gain_total[...] = jnp.zeros_like(gain_total)
    gain_total[0:1, :] = jnp.sum(d_normed * hat, axis=0, keepdims=True)
    gain_total[1:2, :] = part_ffn_ref[...]
    gain_total[2:3, :DH] = part_head_ref[...]
    gains.advance(0)
    grad_tokens_ref[...] = d_residual_ref[...] + scale * (
        weighted - hat * jnp.mean(weighted * hat, axis=-1, keepdims=True)
    )
    for step in range(1, len(mp_flips) + 1):
        gains.advance(step)
    scatter.finish()
    mix.advance(2 * bits)
    gains.end(gains_ref)


def line_call(kernel, name, collective, shapes, scratch, specs, args, out_specs=None):
    return pl.pallas_call(
        kernel,
        out_shape=shapes,
        in_specs=specs,
        out_specs=tuple(out_specs or [whole()] * len(shapes)),
        scratch_shapes=scratch,
        compiler_params=pltpu.CompilerParams(
            collective_id=collective, has_side_effects=True, vmem_limit_bytes=VMEM_LIMIT
        ),
        name=name,
    )(*args)


def widen_kernel(*refs):
    gate_ref, upward_ref, down_ref, q_ref, k_ref, v_ref, out_ref, small_ref, gains_ref = refs[:9]
    wide_gate_up, wide_down, wide_qkv, wide_out = refs[9:13]
    beta_ref, conv_ref, norm_ref, ffn_ref, head_ref = refs[13:]
    wide_gate_up[0] = gate_ref[...].astype(F32)
    wide_gate_up[1] = upward_ref[...].astype(F32)
    wide_down[...] = down_ref[...].astype(F32)
    for kind, ref in enumerate((q_ref, k_ref, v_ref)):
        wide_qkv[kind] = ref[...].astype(F32)
    wide_out[...] = out_ref[...].astype(F32)

    @pl.when(pl.program_id(0) == 0)
    def _():
        small = small_ref[...].astype(F32)
        beta_ref[...] = small[: beta_ref.shape[0]]
        for kind in range(3):
            first = 16 + KCONV * kind
            conv_ref[kind] = small[first : first + KCONV, : conv_ref.shape[2]]
        norm_ref[...] = gains_ref[0:1, :]
        ffn_ref[...] = gains_ref[1:2, :]
        head_ref[...] = gains_ref[2:3, :DH]


def widen(gate, upward, down, query, key, value, out, small, gains):
    hidden_width, depth = gate.shape
    width = query.shape[1]
    steps = depth // LANES // 2
    across = pl.BlockSpec((hidden_width, depth // steps), lambda step: (0, step))
    along = pl.BlockSpec((depth // steps, width), lambda step: (step, 0))
    flat = pl.BlockSpec((width, depth // steps), lambda step: (0, step))

    def fixed(shape):
        return pl.BlockSpec(shape, lambda step: (0,) * len(shape))

    like = jax.ShapeDtypeStruct
    return pl.pallas_call(
        widen_kernel,
        out_shape=(
            like((2, hidden_width, depth), F32),
            like((hidden_width, depth), F32),
            like((3, depth, width), F32),
            like((width, depth), F32),
            like((width // DH, depth), F32),
            like((3, KCONV, width), F32),
            like((1, depth), F32),
            like((1, depth), F32),
            like((1, DH), F32),
        ),
        grid=(steps,),
        in_specs=[across] * 3 + [along] * 3 + [flat, fixed((32, depth)), fixed((8, depth))],
        out_specs=(
            pl.BlockSpec((2, hidden_width, depth // steps), lambda step: (0, 0, step)),
            across,
            pl.BlockSpec((3, depth // steps, width), lambda step: (0, step, 0)),
            flat,
            fixed((width // DH, depth)),
            fixed((3, KCONV, width)),
            fixed((1, depth)),
            fixed((1, depth)),
            fixed((1, DH)),
        ),
        compiler_params=pltpu.CompilerParams(vmem_limit_bytes=VMEM_LIMIT),
        name="widen_sums",
    )(gate, upward, down, query, key, value, out, small, gains)


def body(
    chips,
    dp_bits,
    mp_bits,
    tokens,
    grad_out,
    doc_ids,
    norm_gain,
    qkv_weight,
    beta_weight,
    conv_weight,
    head_gain,
    out_weight,
    ffn_gain,
    gate_up_weight,
    down_weight,
):
    width = qkv_weight.shape[2]
    heads_here = width // DH
    block, depth = tokens.shape
    rows_total = 2 * chips * block
    hidden_width = down_weight.shape[0]
    like = jax.ShapeDtypeStruct
    any_spec = pl.BlockSpec(memory_space=pl.ANY)
    norm_row = norm_gain.reshape(1, depth)
    ffn_row = ffn_gain.reshape(1, depth)
    beta_pad = jnp.pad(beta_weight.T, ((0, LANES - heads_here), (0, 0)))
    gate_up_rows = jnp.swapaxes(gate_up_weight, 1, 2)

    f32_rows = pltpu.VMEM((rows_total, width), F32)
    grids = rows_total // GROUP * heads_here
    slots = rows_total // SPAN * heads_here
    mix_shapes = (
        like((rows_total, depth), BF16),
        like((rows_total, 3 * width + LANES), F32),
        like((rows_total, width), BF16),
        like((rows_total, width), BF16),
        like((grids, GROUP, GROUP), BF16),
        like((rows_total, width), BF16),
        like((grids, GROUP, GROUP), BF16),
        like((slots, DH, DH), BF16),
        like((slots, DH, DH), BF16),
        like((rows_total, width), BF16),
        like((rows_total, width), F32),
        like((rows_total, width), BF16),
        like((rows_total, depth), BF16),
    )
    rows_one, projected, query, key, solve, w_part, score, maps, starts, *rest = (
        line_call(
            functools.partial(project_mix_kernel, chips, heads_here),
            "project_mix",
            1,
            mix_shapes,
            [pltpu.VMEM(shape.shape, shape.dtype) for shape in mix_shapes]
            + [
                pltpu.VMEM(qkv_weight.shape, BF16),
                f32_rows,
                pltpu.VMEM((slots, DH, DH), F32),
                pltpu.SemaphoreType.DMA,
                pltpu.SemaphoreType.DMA((len(mix_shapes),)),
                line_sems(chips),
                line_sems(chips),
                pltpu.SemaphoreType.DMA((3,)),
            ],
            [pl.BlockSpec(memory_space=pltpu.SMEM)] + [whole()] * 2 + [any_spec] + [whole()] * 4,
            (
                doc_ids,
                tokens,
                norm_row,
                qkv_weight,
                beta_pad,
                conv_weight,
                head_gain.reshape(1, DH),
                grad_out,
            ),
            [any_spec] * len(mix_shapes),
        )
    )
    heads_out, mixed, update, grads_all = rest
    kept = (mixed, query, key, solve, w_part, score, maps, starts, update)
    feed_shape = like((rows_total, hidden_width), BF16)
    grad_shape = like((hidden_width, depth), BF16)
    residual, hidden, d_gate, d_upward, *feed_grads = line_call(
        functools.partial(attend_feed_kernel, chips),
        "attend_feed",
        2,
        (like((block, depth), F32),) + (feed_shape,) * 3 + (grad_shape,) * 3,
        scatter_scratch(chips, block, depth)
        + [
            line_sems(chips),
            line_sems(chips),
            pltpu.VMEM((rows_total, depth), BF16),
            pltpu.VMEM(gate_up_rows.shape, BF16),
            pltpu.VMEM(down_weight.shape, BF16),
            pltpu.VMEM((rows_total, depth), BF16),
            pltpu.VMEM((rows_total, hidden_width), BF16),
            pltpu.VMEM((3, hidden_width, depth), F32),
            pltpu.VMEM((2, hidden_width, TILE), BF16),
            pltpu.VMEM((3, 2 * block, hidden_width), BF16),
            pltpu.SemaphoreType.DMA((2,)),
            pltpu.SemaphoreType.DMA((2,)),
            pltpu.SemaphoreType.DMA((3,)),
            pltpu.SemaphoreType.DMA((3,)),
        ],
        [whole()] * 4 + [any_spec] * 3,
        (heads_out, out_weight, tokens, ffn_row, gate_up_rows, down_weight, grads_all),
        [whole()] + [any_spec] * 6,
    )
    dp_flips = tuple(("dp", bit) for bit in range(dp_bits))
    mp_flips = tuple(("mp", bit) for bit in range(mp_bits))
    feed_sums = lax.psum(tuple(feed_grads[1:]), "dp")
    d_residual, d_heads, grad_out_weight, part_ffn_gain, sum_down = line_call(
        functools.partial(feed_back_kernel, chips, dp_bits, dp_flips),
        "feed_back",
        3,
        (
            like((block, depth), F32),
            like((rows_total, width), F32),
            like((width, depth), BF16),
            like((1, depth), F32),
        )
        + (grad_shape,),
        scatter_scratch(chips, block, depth)
        + [
            line_sems(chips),
            pltpu.VMEM((rows_total, depth), BF16),
            pltpu.VMEM((width, depth), F32),
            pltpu.SemaphoreType.DMA((1,)),
            pltpu.SemaphoreType.DMA((1,)),
            pltpu.VMEM(grad_shape.shape, BF16),
        ]
        + plane_scratch(dp_bits, [(grad_shape.shape, 1)]),
        [whole()] * 8 + [any_spec],
        (
            d_gate,
            d_upward,
            gate_up_rows,
            residual,
            ffn_row,
            grad_out,
            heads_out,
            out_weight,
            feed_grads[0],
        ),
        [whole()] * 4 + [any_spec],
    )
    qkv_shape = like((depth, width), BF16)
    kept = (projected, *kept, d_heads)
    d_projected, d_logit, grad_conv, part_head_gain, grad_beta, block_out, *sums = line_call(
        functools.partial(mixer_backward_kernel, chips, dp_bits, dp_flips, heads_here),
        "mixer_backward",
        5,
        (
            like((rows_total, 3 * width), BF16),
            like((rows_total, LANES), BF16),
            like(conv_weight.shape, F32),
            like((1, DH), F32),
            like((8, depth), F32),
            like((block, depth), BF16),
        )
        + (qkv_shape,) * 3
        + (like((width, depth), BF16),),
        [
            f32_rows,
            pltpu.VMEM((slots, DH, DH), F32),
            pltpu.VMEM((slots, DH, DH), BF16),
            f32_rows,
            f32_rows,
            pltpu.VMEM((rows_total + 8, 3 * width), F32),
            pltpu.VMEM((rows_total, hidden_width), BF16),
            pltpu.VMEM(down_weight.shape, BF16),
            pltpu.VMEM((rows_total, depth), BF16),
            pltpu.VMEM((block, depth), F32),
            pltpu.SemaphoreType.DMA((4,)),
        ]
        + scatter_scratch(chips, block, depth)
        + [pltpu.VMEM(array.shape, array.dtype) for array in kept]
        + [pltpu.SemaphoreType.DMA((len(kept),))]
        + plane_scratch(dp_bits, [((width, depth), 1)]),
        [pl.BlockSpec(memory_space=pltpu.SMEM)] + [whole()] * 3 + [any_spec] * 15,
        (
            doc_ids,
            conv_weight,
            head_gain.reshape(1, DH),
            residual,
            hidden,
            down_weight,
            rows_one,
            *kept,
            grad_out_weight,
        ),
    )
    mix_grads, sum_out = sums[:3], sums[3]
    sum_shapes = (qkv_shape,) * 3 + (like((32, depth), BF16),)
    grad_tokens, gains, *mix_sums = line_call(
        functools.partial(project_back_kernel, chips, dp_bits, mp_flips),
        "project_back",
        4,
        (like((block, depth), F32), like((8, depth), F32), *sum_shapes),
        [pltpu.SemaphoreType.DMA((3,))]
        + scatter_scratch(chips, block, depth)
        + [
            pltpu.VMEM((8, depth), F32),
            pltpu.VMEM((mp_bits, 8, depth), F32),
            pltpu.VMEM((2**dp_bits, 8, depth), F32),
            pltpu.SemaphoreType.DMA((2, mp_bits)),
            pltpu.SemaphoreType.DMA((2, 2**dp_bits - 1)),
        ]
        + plane_scratch(
            dp_bits, [(shape.shape, 1 if index == 3 else 0) for index, shape in enumerate(sum_shapes)]
        ),
        [whole()] * 11 + [any_spec] * 3,
        (
            d_projected,
            d_logit,
            qkv_weight,
            beta_pad,
            tokens,
            norm_row,
            d_residual,
            grad_beta,
            grad_conv,
            part_head_gain,
            part_ffn_gain,
            *mix_grads,
        ),
    )
    wide_gate_up, wide_down, wide_qkv, wide_out, *rest = widen(
        *feed_sums, sum_down, *mix_sums[:3], sum_out, mix_sums[3], gains
    )
    sum_beta, sum_conv, sum_norm, sum_ffn, sum_head = rest
    return (
        block_out,
        grad_tokens,
        sum_norm.reshape(depth),
        wide_qkv,
        sum_beta.T,
        sum_conv,
        sum_head.reshape(DH),
        wide_out,
        sum_ffn.reshape(depth),
        jnp.swapaxes(wide_gate_up, 1, 2),
        wide_down,
    )


def solution(mesh):
    in_specs = (
        P(("dp", "mp"), None),
        P(("dp", "mp"), None),
        P("dp"),
        P(),
        P(None, None, "mp"),
        P(None, "mp"),
        P(None, None, "mp"),
        P(),
        P("mp", None),
        P(),
        P(None, None, "mp"),
        P("mp", None),
    )
    out_specs = (
        P(("dp", "mp"), None),
        P(("dp", "mp"), None),
        P(),
        P(None, None, "mp"),
        P(None, "mp"),
        P(None, None, "mp"),
        P(),
        P("mp", None),
        P(),
        P(None, None, "mp"),
        P("mp", None),
    )
    chips = mesh.shape["mp"] // 2
    dp_bits = mesh.shape["dp"].bit_length() - 1
    mp_bits = mesh.shape["mp"].bit_length() - 1
    part = functools.partial(body, chips, dp_bits, mp_bits)
    return jax.shard_map(part, mesh=mesh, in_specs=in_specs, out_specs=out_specs, check_vma=False)
```

```python
import functools

import jax
import jax.numpy as jnp
from jax import lax
from jax.experimental import pallas as pl
from jax.experimental.pallas import tpu as pltpu
from jax.sharding import PartitionSpec as P

DH = 128
KCONV = 4
SPAN = 64
LEN = 1024


EPSILON = 1e-06


def row_scale(values):
    return lax.rsqrt(jnp.mean(values * values, axis=-1, keepdims=True) + EPSILON)


BF16 = jnp.bfloat16
F32 = jnp.float32
GROUP = 256
LANES = 128
PER_GROUP = GROUP // SPAN


def dot_nn(left, right):
    return lax.dot_general(
        left.astype(BF16), right.astype(BF16), (((1,), (0,)), ((), ())), preferred_element_type=F32
    )


def dot_nt(left, right):
    return lax.dot_general(
        left.astype(BF16), right.astype(BF16), (((1,), (1,)), ((), ())), preferred_element_type=F32
    )


def dot_tn(left, right):
    return lax.dot_general(
        left.astype(BF16), right.astype(BF16), (((0,), (0,)), ((), ())), preferred_element_type=F32
    )


def span_keep(ids_ref, block):
    first = block * SPAN
    same = ids_ref[first] == ids_ref[jnp.maximum(first - 1, 0)]
    return jnp.where(jnp.logical_and(same, lax.rem(first, LEN) != 0), 1.0, 0.0)


def span_rows(ids_ref, group):
    piece = lax.broadcasted_iota(jnp.int32, (GROUP, 1), 0) // SPAN
    rows = jnp.zeros((GROUP, 1), F32)
    for index in range(PER_GROUP):
        rows = jnp.where(piece == index, span_keep(ids_ref, group * PER_GROUP + index), rows)
    return rows


def grid_masks():
    row = lax.broadcasted_iota(jnp.int32, (GROUP, GROUP), 0)
    col = lax.broadcasted_iota(jnp.int32, (GROUP, GROUP), 1)
    return row, col


def same_block(row, col, size):
    return (row // size) == (col // size)


def tap_rows(offset, keep_rows):
    place = lax.broadcasted_iota(jnp.int32, (GROUP, 1), 0) % SPAN
    return jnp.logical_or(place >= offset, keep_rows > 0.0)


def earlier_rows(ref, group, first_col, offset, keep_rows):
    start = pl.multiple_of(group * GROUP, GROUP)
    prior = pl.multiple_of(jnp.maximum(start - 8, 0), 8)
    cols = slice(first_col, first_col + DH)
    joined = jnp.concatenate([ref[pl.ds(prior, 8), cols], ref[pl.ds(start, GROUP), cols]], 0)
    shifted = pltpu.roll(joined, offset, 0)[8:]
    return jnp.where(tap_rows(offset, keep_rows), shifted, 0.0)


def conv_rows(ref, conv_ref, group, kind, first_col, head, keep_rows):
    taps = conv_ref[kind, :, head * DH : (head + 1) * DH]
    start = pl.multiple_of(group * GROUP, GROUP)
    running = taps[KCONV - 1 : KCONV] * ref[pl.ds(start, GROUP), first_col : first_col + DH]
    for offset in range(1, KCONV):
        running = running + taps[KCONV - 1 - offset : KCONV - offset] * earlier_rows(
            ref, group, first_col, offset, keep_rows
        )
    return running


def unit_scale(values):
    return lax.rsqrt(jnp.sum(values * values, axis=-1, keepdims=True) + EPSILON)


VMEM_LIMIT = 60 * 1024 * 1024


def whole():
    return pl.BlockSpec(memory_space=pltpu.VMEM)


MESH = pl.DeviceIdType.MESH
TILE = 512
CORE, RIGHT, LEFT = 0, 1, 2


def line_place():
    me = lax.axis_index("mp")
    core = lax.rem(me, 2)
    return me, me // 2, core


def flip_bit(axis, bit):
    place = lax.axis_index(axis)
    scale = 2**bit
    mine = lax.rem(place // scale, 2)
    return mine, {axis: place + (1 - 2 * mine) * scale}


def line_barrier(chips, flips=(), peers=1):
    me, chip, core = line_place()
    barrier = pltpu.get_barrier_semaphore()
    for axis, bit in flips:
        pl.semaphore_signal(
            barrier, inc=1, device_id=flip_bit(axis, bit)[1], device_id_type=MESH
        )
    for step in range(1, peers):
        place = lax.rem(lax.axis_index("dp") + step, peers)
        pl.semaphore_signal(barrier, inc=1, device_id={"dp": place}, device_id_type=MESH)

    def greet(other):
        pl.semaphore_signal(barrier, inc=1, device_id={"mp": other}, device_id_type=MESH)

    greet(me + 1 - 2 * core)

    @pl.when(chip > 0)
    def _():
        greet(me - 2)

    @pl.when(chip < chips - 1)
    def _():
        greet(me + 2)

    beside = (chip > 0).astype(jnp.int32) + (chip < chips - 1).astype(jnp.int32)
    pl.semaphore_wait(barrier, beside + len(flips) + peers)


def line_target(kind):
    me, chip, core = line_place()
    return {CORE: me + 1 - 2 * core, RIGHT: me + 2, LEFT: me - 2}[kind]


class LineGather:
    def __init__(self, chips, out_ref, sems):
        self.chips, self.out_ref, self.sems = chips, out_ref, sems
        self.block = out_ref.shape[0] // (2 * chips)
        self.me, self.chip, self.core = line_place()

    def rows(self, chip, core):
        return pl.ds(pl.multiple_of((2 * chip + core) * self.block, self.block), self.block)

    def copy(self, kind, chip, core):
        part = self.out_ref.at[self.rows(chip, core), :]
        return pltpu.make_async_remote_copy(
            src_ref=part,
            dst_ref=part,
            send_sem=self.sems.at[2 * kind, chip],
            recv_sem=self.sems.at[2 * kind + 1, chip],
            device_id={"mp": line_target(kind)},
            device_id_type=MESH,
        )

    def start(self, block):
        self.out_ref[self.rows(self.chip, self.core), :] = block

        @pl.when(self.chip < self.chips - 1)
        def _():
            self.copy(RIGHT, self.chip, self.core).start()

        @pl.when(self.chip > 0)
        def _():
            self.copy(LEFT, self.chip, self.core).start()

        self.copy(CORE, self.chip, self.core).start()

    def arrive(self, chip):
        self.copy(CORE, chip, 1 - self.core).wait_recv()

    def each_new(self, step, use):
        behind, ahead = self.chip - step, self.chip + step

        @pl.when(behind >= 0)
        def _():
            use(behind)

        @pl.when(ahead < self.chips)
        def _():
            use(ahead)

    def pass_on(self, behind, ahead):
        @pl.when(jnp.logical_and(behind >= 0, self.chip < self.chips - 1))
        def _():
            self.copy(RIGHT, behind, self.core).start()

        @pl.when(jnp.logical_and(ahead < self.chips, self.chip > 0))
        def _():
            self.copy(LEFT, ahead, self.core).start()

    def hop(self, step, forward=True):
        behind, ahead = self.chip - step, self.chip + step

        @pl.when(behind >= 0)
        def _():
            self.copy(RIGHT, behind, self.core).wait_recv()

        @pl.when(ahead < self.chips)
        def _():
            self.copy(LEFT, ahead, self.core).wait_recv()

        if forward:
            self.pass_on(behind, ahead)

        self.each_new(step, lambda chip: self.copy(CORE, chip, self.core).start())
        self.each_new(step, self.arrive)

    def hops(self, after):
        def one_hop(step, carry):
            self.hop(step)
            after(step)
            return carry

        lax.fori_loop(1, self.chips, one_hop, 0)

    def finish(self, first=0, end=None):
        end = self.chips if end is None else end

        def sent(chip, carry):
            apart = jnp.abs(chip - self.chip)
            relay = jnp.logical_and(apart >= first - 1, apart < end - 1)
            if first == 0:
                relay = jnp.logical_or(relay, apart == 0)
            to_right = jnp.logical_and(chip <= self.chip, self.chip < self.chips - 1)
            to_left = jnp.logical_and(chip >= self.chip, self.chip > 0)

            @pl.when(jnp.logical_and(relay, to_right))
            def _():
                self.copy(RIGHT, chip, self.core).wait_send()

            @pl.when(jnp.logical_and(relay, to_left))
            def _():
                self.copy(LEFT, chip, self.core).wait_send()

            @pl.when(jnp.logical_and(apart >= first, apart < end))
            def _():
                self.copy(CORE, chip, self.core).wait_send()

            return carry

        lax.fori_loop(0, self.chips, sent, 0)


class LineScatter:
    def __init__(self, chips, term, stage, held, landing, sems):
        self.chips, self.term = chips, term
        self.stage, self.held, self.landing, self.sems = stage, held, landing, sems
        self.me, self.chip, self.core = line_place()

    def left_slot(self, chip, receiver):
        return jnp.where(chip == receiver, self.chips, chip)

    def copy(self, kind, chip):
        source = (self.stage if kind == CORE else self.held).at[chip]
        if kind == CORE:
            target = self.held.at[chip]
        elif kind == RIGHT:
            target = self.landing.at[chip]
        else:
            target = self.landing.at[self.left_slot(chip, self.chip - 1)]
        return pltpu.make_async_remote_copy(
            src_ref=source,
            dst_ref=target,
            send_sem=self.sems.at[2 * kind, chip],
            recv_sem=self.sems.at[2 * kind + 1, chip],
            device_id={"mp": line_target(kind)},
            device_id_type=MESH,
        )

    def exchange(self, chip):
        self.stage[chip] = self.term(chip, 1 - self.core).astype(BF16)
        self.copy(CORE, chip).start()

    def collect(self, chip):
        own = self.term(chip, self.core)
        self.copy(CORE, chip).wait_recv()
        return own + self.held[chip].astype(F32)

    def pass_on(self, kind, chip, first):
        both = self.collect(chip)

        @pl.when(first)
        def _():
            self.held[chip] = both.astype(BF16)

        @pl.when(jnp.logical_not(first))
        def _():
            self.copy(kind, chip).wait_recv()
            self.held[chip] = (both + self.landing[chip].astype(F32)).astype(BF16)

        self.copy(kind, chip).start()

    def exchange_pair(self, step):
        @pl.when(self.chip + step < self.chips)
        def _():
            self.exchange(self.chip + step)

        @pl.when(self.chip - step >= 0)
        def _():
            self.exchange(self.chip - step)

    def begin(self):
        self.exchange_pair(self.chips - 1)

    def step(self, index):
        last = self.chips - 1
        step = last - index

        @pl.when(step > 1)
        def _():
            self.exchange_pair(step - 1)

        @pl.when(self.chip + step < self.chips)
        def _():
            self.pass_on(RIGHT, self.chip + step, self.chip == 0)

        @pl.when(self.chip - step >= 0)
        def _():
            self.pass_on(LEFT, self.chip - step, self.chip == last)

    def steps(self, first, each=None):
        def one_step(index, carry):
            self.step(index)
            if each is not None:
                each(index)
            return carry

        lax.fori_loop(first, self.chips - 1, one_step, 0)

    def end(self, result_ref):
        self.exchange(self.chip)
        result_ref[...] = self.collect(self.chip)

        @pl.when(self.chip > 0)
        def _():
            self.copy(RIGHT, self.chip).wait_recv()
            result_ref[...] += self.landing[self.chip].astype(F32)

        @pl.when(self.chip < self.chips - 1)
        def _():
            self.copy(LEFT, self.chip).wait_recv()
            result_ref[...] += self.landing[self.chips].astype(F32)

    def run(self, result_ref, each=None):
        self.begin()
        self.steps(0, each)
        self.end(result_ref)

    def finish(self):
        def sent(chip, carry):
            @pl.when(chip > self.chip)
            def _():
                self.copy(RIGHT, chip).wait_send()

            @pl.when(chip < self.chip)
            def _():
                self.copy(LEFT, chip).wait_send()

            self.copy(CORE, chip).wait_send()
            return carry

        lax.fori_loop(0, self.chips, sent, 0)


class PlaneSum:
    def __init__(self, bits, bufs, outs, landings, sems):
        self.bits, self.bufs, self.outs = bits, bufs, outs
        self.landings, self.sems = landings, sems
        self.orders = (tuple(range(bits)), tuple(reversed(range(bits))))
        self.half = bufs[0][0].shape[bufs[0][1]] // 2

    def span(self, part, level):
        start = part * self.half
        for index in range(level):
            mine, _ = flip_bit("dp", self.orders[part][index])
            start = start + mine * (self.half >> (index + 1))
        return start

    def view(self, pairs, array, start, size):
        ref, axis = pairs[array]
        where = pl.ds(pl.multiple_of(start, size), size)
        return ref.at[where, :] if axis == 0 else ref.at[:, where]

    def pieces(self, part, index):
        mine, target = flip_bit("dp", self.orders[part][index])
        size = self.half >> (index + 1)
        start = self.span(part, index)
        return target, size, start + mine * size, start + (1 - mine) * size

    def copies(self, step):
        made = []
        for part in range(2):
            index = step if step < self.bits else 2 * self.bits - 1 - step
            target, size, kept, given = self.pieces(part, index)
            for array in range(len(self.bufs)):
                if step < self.bits:
                    source = self.view(self.bufs, array, given, size)
                    landing = self.landings[index][array].at[part]
                else:
                    source = self.view(self.outs, array, kept, size)
                    landing = source
                made.append(
                    pltpu.make_async_remote_copy(
                        src_ref=source,
                        dst_ref=landing,
                        send_sem=self.sems.at[0, part, step, array],
                        recv_sem=self.sems.at[1, part, step, array],
                        device_id=target,
                        device_id_type=MESH,
                    )
                )
        return made

    def advance(self, step, go=True):
        if step > 0:
            for copy in self.copies(step - 1):
                copy.wait()
            if step - 1 < self.bits:
                for part in range(2):
                    _, size, kept, _ = self.pieces(part, step - 1)
                    for array in range(len(self.bufs)):
                        here = self.view(self.bufs, array, kept, size)
                        ended = self.outs if step == self.bits else self.bufs
                        self.view(ended, array, kept, size)[...] = (
                            here[...].astype(F32)
                            + self.landings[step - 1][array][part].astype(F32)
                        ).astype(BF16)
        if go and step < 2 * self.bits:
            for copy in self.copies(step):
                copy.start()


def plane_scratch(bits, shapes):
    made = [pltpu.VMEM(shape, BF16) for shape, _ in shapes]
    for index in range(bits):
        for shape, axis in shapes:
            size = list(shape)
            size[axis] = size[axis] >> (index + 2)
            made.append(pltpu.VMEM((2, *size), BF16))
    return made + [pltpu.SemaphoreType.DMA((2, 2, 2 * bits, len(shapes)))]


def plane_sum(bits, outs, axes, scratch):
    count = len(outs)
    bufs, scratch = scratch[:count], scratch[count:]
    landings = [scratch[index * count : (index + 1) * count] for index in range(bits)]
    return PlaneSum(
        bits, list(zip(bufs, axes)), list(zip(outs, axes)), landings, scratch[bits * count]
    )


class SmallSum:
    def __init__(self, flips, peers, total_ref, landing, everyone, sems, peer_sems):
        self.flips, self.peers, self.total_ref = flips, peers, total_ref
        self.landing, self.everyone = landing, everyone
        self.sems, self.peer_sems = sems, peer_sems

    def copy(self, step):
        return pltpu.make_async_remote_copy(
            src_ref=self.total_ref,
            dst_ref=self.landing.at[step],
            send_sem=self.sems.at[0, step],
            recv_sem=self.sems.at[1, step],
            device_id=flip_bit(*self.flips[step])[1],
            device_id_type=MESH,
        )

    def spread(self):
        me = lax.axis_index("dp")
        return [
            pltpu.make_async_remote_copy(
                src_ref=self.everyone.at[me],
                dst_ref=self.everyone.at[me],
                send_sem=self.peer_sems.at[0, step],
                recv_sem=self.peer_sems.at[1, step],
                device_id={"dp": lax.rem(me + step + 1, self.peers)},
                device_id_type=MESH,
            )
            for step in range(self.peers - 1)
        ]

    def advance(self, step):
        if 0 < step <= len(self.flips):
            self.copy(step - 1).wait()
            self.total_ref[...] += self.landing[step - 1]
        if step < len(self.flips):
            self.copy(step).start()
        elif step == len(self.flips):
            self.everyone[lax.axis_index("dp")] = self.total_ref[...]
            for copy in self.spread():
                copy.start()

    def end(self, result_ref):
        for copy in self.spread():
            copy.wait()
        total = self.everyone[0]
        for peer in range(1, self.peers):
            total = total + self.everyone[peer]
        result_ref[...] = total


def line_sems(chips):
    return pltpu.SemaphoreType.DMA((6, chips))


def scatter_scratch(chips, block, depth):
    return [
        pltpu.VMEM((chips, block, depth), BF16),
        pltpu.VMEM((chips, block, depth), BF16),
        pltpu.VMEM((chips + 1, block, depth), BF16),
        line_sems(chips),
    ]


class Drain:
    def __init__(self, sems):
        self.sems, self.copies = sems, []

    def start(self, source, target):
        copy = pltpu.make_async_copy(source, target, self.sems.at[len(self.copies)])
        copy.start()
        self.copies.append(copy)

    def finish(self):
        for copy in self.copies:
            copy.wait()


def near_item(chips, chip, index):
    ahead, behind = chips - 1 - chip, chip
    both = jnp.minimum(ahead, behind)
    near = (index + 1) // 2
    turn = 1 - 2 * lax.rem(index + 1, 2)
    far = jnp.where(ahead > behind, 1, -1)
    return chip + jnp.where(index <= 2 * both, turn * near, far * (index - both))


def near_copies(chip, chips, source, target, sems):
    pair = source.shape[0] // chips
    made = []
    for index in range(3):
        other = chip + index - 1
        rows = pl.ds(pl.multiple_of(jnp.clip(other, 0, chips - 1) * pair, pair), pair)
        copy = pltpu.make_async_copy(source.at[rows, :], target.at[rows, :], sems.at[index])
        made.append((jnp.logical_and(other >= 0, other < chips), copy))
    return made


def project_mix_kernel(
    chips,
    heads_here,
    ids_ref,
    tokens_ref,
    norm_ref,
    weight_ref,
    beta_ref,
    conv_ref,
    gain_ref,
    grad_ref,
    *refs,
):
    outs, bufs, refs = refs[:13], refs[13:26], refs[26:]
    held, u_scr, add_scr, load_sem, drain_sems, sems, grad_sems, near_sems = refs
    (
        rows_ref,
        proj_ref,
        query_ref,
        key_ref,
        solve_ref,
        w_ref,
        score_ref,
        map_ref,
        start_ref,
        heads_ref,
        mixed_ref,
        update_ref,
        grads_ref,
    ) = bufs
    load = pltpu.make_async_copy(weight_ref, held, load_sem)
    load.start()
    tokens = tokens_ref[...].astype(F32)
    normed = (tokens * row_scale(tokens) * norm_ref[...]).astype(BF16)
    line_barrier(chips)
    gather = LineGather(chips, rows_ref, sems)
    gather.start(normed)
    load.wait()
    width = heads_here * DH
    rows_total = rows_ref.shape[0]
    groups = rows_total // GROUP
    spans = LEN // SPAN
    sequences = rows_total // LEN
    drain = Drain(drain_sems)

    def project(chip):
        rows = pl.ds(pl.multiple_of(chip * GROUP, GROUP), GROUP)
        here = rows_ref[rows, :]
        for kind in range(3):
            proj_ref[rows, kind * width : (kind + 1) * width] = dot_nn(here, held[kind])
        proj_ref[rows, 3 * width : 3 * width + LANES] = dot_nt(here, beta_ref[...])

    def local_part(group, carry):
        start = pl.multiple_of(group * GROUP, GROUP)
        rows = pl.ds(start, GROUP)
        keep_rows = span_rows(ids_ref, group)
        row, col = grid_masks()
        for head in range(heads_here):
            cols = slice(head * DH, (head + 1) * DH)
            act_q = jax.nn.silu(
                conv_rows(proj_ref, conv_ref, group, 0, head * DH, head, keep_rows)
            )
            query = (act_q * (unit_scale(act_q) * DH ** (-0.5))).astype(BF16)
            act_k = jax.nn.silu(
                conv_rows(proj_ref, conv_ref, group, 1, width + head * DH, head, keep_rows)
            )
            key = act_k * unit_scale(act_k)
            value = jax.nn.silu(
                conv_rows(proj_ref, conv_ref, group, 2, 2 * width + head * DH, head, keep_rows)
            )
            beta = jax.nn.sigmoid(proj_ref[rows, 3 * width + head : 3 * width + head + 1])
            key_low = key.astype(BF16)
            query_ref[rows, cols] = query
            key_ref[rows, cols] = key_low
            inside = same_block(row, col, SPAN)
            system = jnp.where(
                jnp.logical_and(inside, row > col), dot_nt(key_low, key_low) * beta, 0.0
            )
            score = jnp.where(jnp.logical_and(inside, row >= col), dot_nt(query, key_low), 0.0)
            score_ref[group * heads_here + head] = score.astype(BF16)
            solve = jnp.where(
                row == col, 1.0, jnp.where(same_block(row, col, 2), -system, 0.0)
            )
            size = 2
            while size < SPAN:
                cross = jnp.where(
                    jnp.logical_and(
                        same_block(row, col, 2 * size),
                        jnp.logical_not(same_block(row, col, size)),
                    ),
                    system,
                    0.0,
                )
                solve_low = solve.astype(BF16)
                solve = solve - dot_nn(solve_low, dot_nn(cross, solve_low))
                size *= 2
            solve_low = solve.astype(BF16)
            solve_ref[group * heads_here + head] = solve_low
            both = dot_nn(solve_low, jnp.concatenate([key * beta, value * beta], 1))
            both_low = both.astype(BF16)
            w_ref[rows, cols] = both_low[:, :DH]
            u_scr[rows, cols] = both[:, DH:]
            for piece in range(PER_GROUP):
                part = slice(piece * SPAN, (piece + 1) * SPAN)
                carry_pair = dot_tn(key_low[part], both_low[part])
                slot = (group * PER_GROUP + piece) * heads_here + head
                map_ref[slot] = carry_pair[:, :DH].astype(BF16)
                add_scr[slot] = carry_pair[:, DH:]
        return carry

    def after(step):
        gather.each_new(step, project)
        local_part(near_item(chips, gather.chip, step - 1), 0)

    gather.arrive(gather.chip)
    project(gather.chip)
    gather.hops(after)
    gather_grads = LineGather(chips, grads_ref, grad_sems)
    gather_grads.start(grad_ref[...])
    drain.start(bufs[0], outs[0])
    drain.start(bufs[1], outs[1])
    local_part(near_item(chips, gather.chip, chips - 1), 0)
    for index in range(2, 8):
        drain.start(bufs[index], outs[index])

    def scan_part(span, states):
        ended = []
        for sequence in range(sequences):
            for head in range(heads_here):
                block = sequence * spans + span
                slot = block * heads_here + head
                memory = states[sequence * heads_here + head] * span_keep(ids_ref, block)
                memory_low = memory.astype(BF16)
                start_ref[slot] = memory_low
                ended.append(memory - dot_nn(map_ref[slot], memory_low) + add_scr[slot])
        return tuple(ended)

    blank = tuple(jnp.zeros((DH, DH), F32) for _ in range(sequences * heads_here))
    lax.fori_loop(0, spans, scan_part, blank)

    drain.start(bufs[8], outs[8])

    def output_part(group, carry):
        start = pl.multiple_of(group * GROUP, GROUP)
        rows = pl.ds(start, GROUP)
        for head in range(heads_here):
            cols = slice(head * DH, (head + 1) * DH)
            query = query_ref[rows, cols]
            w_part = w_ref[rows, cols]
            updates, reads = [], []
            for piece in range(PER_GROUP):
                part = slice(piece * SPAN, (piece + 1) * SPAN)
                slot = (group * PER_GROUP + piece) * heads_here + head
                pair = dot_nn(jnp.concatenate([w_part[part], query[part]], 0), start_ref[slot])
                updates.append(pair[:SPAN])
                reads.append(pair[SPAN:])
            update = (u_scr[rows, cols] - jnp.concatenate(updates, 0)).astype(BF16)
            update_ref[rows, cols] = update
            mixed = jnp.concatenate(reads, 0) + dot_nn(score_ref[group * heads_here + head], update)
            mixed_ref[rows, cols] = mixed
            scale = lax.rsqrt(jnp.mean(mixed * mixed, axis=-1, keepdims=True) + EPSILON)
            heads_ref[rows, cols] = (mixed * scale * gain_ref[...]).astype(BF16)
        return carry

    lax.fori_loop(0, groups, output_part, 0)
    for index in range(9, 12):
        drain.start(bufs[index], outs[index])
    gather.finish()
    gather_grads.arrive(gather.chip)
    gather_grads.hop(1, False)
    near = near_copies(gather.chip, chips, grads_ref, outs[12], near_sems)
    for when, copy in near:
        pl.when(when)(copy.start)
    gather_grads.finish(0, 2)
    for when, copy in near:
        pl.when(when)(copy.wait)
    drain.finish()


def attend_feed_kernel(
    chips,
    heads_ref,
    weight_ref,
    tokens_ref,
    gain_ref,
    gate_up_any,
    down_any,
    grads_any,
    residual_ref,
    *refs,
):
    feed_outs, grad_outs, refs = refs[:3], refs[3:6], refs[6:]
    (stage, held, landing, scatter_sems, gather_sems, grad_sems, rows_ref) = refs[:7]
    (gate_up_ref, down_ref, grads_ref, d_hidden_ref, acc_ref, tile_ref, feed_ref) = refs[7:14]
    load_sems, tile_sems, feed_sems, near_sems = refs[14:]
    block, depth = tokens_ref.shape
    pair = 2 * block
    loads = [
        pltpu.make_async_copy(source, target, load_sems.at[index])
        for index, (source, target) in enumerate(
            ((down_any, down_ref), (gate_up_any, gate_up_ref))
        )
    ]
    gather_grads = LineGather(chips, grads_ref, grad_sems)
    near = near_copies(gather_grads.chip, chips, grads_any, grads_ref, near_sems)
    for when, copy in near:
        pl.when(when)(copy.start)
    for load in loads:
        load.start()
    line_barrier(chips)

    def pair_rows(chip):
        return pl.ds(pl.multiple_of(chip * pair, pair), pair)

    def term(chip, core):
        rows = pl.ds(pl.multiple_of((2 * chip + core) * block, block), block)
        return dot_nn(heads_ref[rows, :], weight_ref[...])

    def back_hidden(index):
        rows = pair_rows(near_item(chips, gather_grads.chip, index))
        d_hidden_ref[rows, :] = dot_nt(grads_ref[rows, :], down_ref[...]).astype(BF16)

    def each(index):
        @pl.when(index == 0)
        def _():
            loads[0].wait()

        back_hidden(index)

        @pl.when(index + 2 < chips)
        def _():
            gather_grads.hop(index + 2)

    for when, copy in near:
        pl.when(when)(copy.wait)
    gather_grads.pass_on(gather_grads.chip - 1, gather_grads.chip + 1)
    scatter = LineScatter(chips, term, stage, held, landing, scatter_sems)
    scatter.run(residual_ref, each)
    residual = residual_ref[...] + tokens_ref[...].astype(F32)
    residual_ref[...] = residual
    gather = LineGather(chips, rows_ref, gather_sems)
    gather.start((residual * row_scale(residual) * gain_ref[...]).astype(BF16))
    back_hidden(chips - 1)
    loads[1].wait()
    acc_ref[...] = jnp.zeros_like(acc_ref)
    gather.arrive(gather.chip)
    tiles = depth // TILE

    def feed_copies(rows):
        return [
            pltpu.make_async_copy(
                feed_ref.at[index], feed_outs[index].at[rows, :], feed_sems.at[index]
            )
            for index in range(3)
        ]

    def feed(chip):
        rows = pair_rows(chip)
        here = rows_ref[rows, :]
        gate = dot_nt(here, gate_up_ref[0])
        upward = dot_nt(here, gate_up_ref[1])
        d_hidden = d_hidden_ref[rows, :].astype(F32)
        sigmoid_gate = jax.nn.sigmoid(gate)
        activated = gate * sigmoid_gate
        feed_ref[0] = (activated * upward).astype(BF16)
        feed_ref[1] = (
            d_hidden * upward * sigmoid_gate * (1.0 + gate * (1.0 - sigmoid_gate))
        ).astype(BF16)
        feed_ref[2] = (d_hidden * activated).astype(BF16)
        for copy in feed_copies(rows):
            copy.start()
        return rows

    right_refs = (grads_ref, rows_ref, rows_ref)

    def add_grads(rows):
        for index, right_ref in enumerate(right_refs):

            def one_tile(tile, carry):
                cols = pl.ds(pl.multiple_of(tile * TILE, TILE), TILE)
                acc_ref[index, :, cols] += dot_tn(feed_ref[index], right_ref[rows, cols])
                return carry

            lax.fori_loop(0, tiles, one_tile, 0)

    def step_feed(step):
        rows = feed(near_item(chips, gather.chip, step))
        add_grads(rows)
        for copy in feed_copies(rows):
            copy.wait()

    step_feed(0)

    def after(step):
        @pl.when(step < chips - 1)
        def _():
            step_feed(step)

    gather.hops(after)
    rows = feed(near_item(chips, gather.chip, chips - 1))
    sent = []
    for index, right_ref in enumerate(right_refs):
        for tile in range(tiles):
            count = index * tiles + tile
            slot = count % 2
            if count >= 2:
                sent[count - 2].wait()
            cols = slice(tile * TILE, (tile + 1) * TILE)
            tile_ref[slot] = (
                acc_ref[index, :, cols] + dot_tn(feed_ref[index], right_ref[rows, cols])
            ).astype(BF16)
            copy = pltpu.make_async_copy(
                tile_ref.at[slot], grad_outs[index].at[:, cols], tile_sems.at[slot]
            )
            copy.start()
            sent.append(copy)
    for copy in sent[-2:] + feed_copies(rows):
        copy.wait()
    gather_grads.finish(2)
    gather.finish()
    scatter.finish()


def feed_back_kernel(
    chips,
    bits,
    flips,
    d_gate_ref,
    d_upward_ref,
    weight_ref,
    residual_ref,
    gain_ref,
    grad_ref,
    heads_ref,
    out_weight_ref,
    *refs,
):
    feed_in, refs = refs[:1], refs[1:]
    d_residual_ref, d_heads_ref, grad_out_ref, grad_gain_ref = refs[:4]
    feed_outs, refs = refs[4:5], refs[5:]
    stage, held, landing, scatter_sems, gather_sems, rows_ref, acc_ref = refs[:7]
    load_sems, drain_sems, summed = refs[7], refs[8], refs[9:10]
    block, depth = residual_ref.shape
    feed = plane_sum(bits, summed, (1,), refs[10:])
    loads = [
        pltpu.make_async_copy(source, feed.bufs[index][0], load_sems.at[index])
        for index, source in enumerate(feed_in)
    ]
    for load in loads:
        load.start()
    line_barrier(chips, flips)
    for load in loads:
        load.wait()
    feed.advance(0)

    def term(chip, core):
        rows = pl.ds(pl.multiple_of((2 * chip + core) * block, block), block)
        return dot_nn(d_gate_ref[rows, :], weight_ref[0]) + dot_nn(
            d_upward_ref[rows, :], weight_ref[1]
        )

    scatter = LineScatter(chips, term, stage, held, landing, scatter_sems)

    def each(index):
        @pl.when(index == chips - 2)
        def _():
            feed.advance(1)

    scatter.run(d_residual_ref, each)
    d_normed = d_residual_ref[...]
    residual = residual_ref[...]
    scale = row_scale(residual)
    hat = residual * scale
    weighted = gain_ref[...] * d_normed
    grad_gain_ref[...] = jnp.sum(d_normed * hat, axis=0, keepdims=True)
    d_residual = grad_ref[...].astype(F32) + scale * (
        weighted - hat * jnp.mean(weighted * hat, axis=-1, keepdims=True)
    )
    d_residual_ref[...] = d_residual
    gather = LineGather(chips, rows_ref, gather_sems)
    gather.start(d_residual.astype(BF16))
    acc_ref[...] = jnp.zeros_like(acc_ref)
    feed.advance(2)
    gather.arrive(gather.chip)

    def use(chip):
        rows = pl.ds(pl.multiple_of(chip * 2 * block, 2 * block), 2 * block)
        here = rows_ref[rows, :]
        d_heads_ref[rows, :] = dot_nt(here, out_weight_ref[...])
        acc_ref[...] += dot_tn(heads_ref[rows, :], here)

    use(gather.chip)

    def after(step):
        gather.each_new(step, use)

        @pl.when(step == max(chips - 2, 1))
        def _():
            feed.advance(3)

    gather.hops(after)
    grad_out_ref[...] = acc_ref[...].astype(BF16)
    gather.finish()
    scatter.finish()
    for step in range(4, 2 * bits + 1):
        feed.advance(step)
    drain = Drain(drain_sems)
    drain.start(summed[0], feed_outs[0])
    drain.finish()


def mixer_backward_kernel(
    chips,
    bits,
    flips,
    heads_here,
    ids_ref,
    conv_ref,
    gain_ref,
    residual_ref,
    hidden_any,
    down_any,
    rows_any,
    *refs,
):
    kept_in, mix_in, refs = refs[:11], refs[11:12], refs[12:]
    d_proj_ref, d_logit_ref, grad_conv_ref, grad_gain_ref, grad_beta_ref, out_ref = refs[:6]
    mix_grads, summed, refs = refs[6:9], refs[9:10], refs[10:]
    y_scr, add_scr, end_scr, d_query_scr, d_key_scr, d_conv_scr = refs[:6]
    hidden_ref, down_ref, rows_ref, result = refs[6:10]
    load_sems = refs[10]
    kept, kept_sems = refs[15:26], refs[26]
    (
        proj_ref,
        mixed_ref,
        query_ref,
        key_ref,
        solve_ref,
        w_ref,
        score_ref,
        map_ref,
        start_ref,
        update_ref,
        d_heads_ref,
    ) = kept
    mix = plane_sum(bits, summed, (1,), refs[27:])
    rows_total = proj_ref.shape[0]
    depth = rows_ref.shape[1]
    block = residual_ref.shape[0]
    loads = [
        pltpu.make_async_copy(source, target, load_sems.at[index])
        for index, (source, target) in enumerate(
            (
                (mix_in[0], mix.bufs[0][0]),
                (hidden_any, hidden_ref),
                (down_any, down_ref),
                (rows_any, rows_ref),
            )
        )
    ]
    for load in loads[:3]:
        load.start()
    keeps = [
        pltpu.make_async_copy(source, target, kept_sems.at[index])
        for index, (source, target) in enumerate(zip(kept_in, kept))
    ]
    for keep_load in keeps:
        keep_load.start()
    loads[3].start()
    line_barrier(chips, flips)
    loads[0].wait()
    mix.advance(0)

    def term_down(chip, core):
        rows = pl.ds(pl.multiple_of((2 * chip + core) * block, block), block)
        return dot_nn(hidden_ref[rows, :], down_ref[...])

    scatter = LineScatter(chips, term_down, *refs[11:15])
    loads[1].wait()
    loads[2].wait()
    scatter.begin()
    scatter.step(0)
    for keep_load in keeps:
        keep_load.wait()
    width = heads_here * DH
    groups = rows_total // GROUP
    spans = LEN // SPAN
    sequences = rows_total // LEN
    grad_gain_ref[...] = jnp.zeros_like(grad_gain_ref)
    grad_conv_ref[...] = jnp.zeros_like(grad_conv_ref)

    def local_part(group, carry):
        start = pl.multiple_of(group * GROUP, GROUP)
        rows = pl.ds(start, GROUP)
        row, col = grid_masks()
        for head in range(heads_here):
            cols = slice(head * DH, (head + 1) * DH)
            mixed = mixed_ref[rows, cols]
            d_heads = d_heads_ref[rows, cols]
            scale = lax.rsqrt(jnp.mean(mixed * mixed, axis=-1, keepdims=True) + EPSILON)
            hat = mixed * scale
            grad_gain_ref[...] += jnp.sum(d_heads * hat, axis=0, keepdims=True)
            weighted = gain_ref[...] * d_heads
            d_mixed = scale * (
                weighted - hat * jnp.mean(weighted * hat, axis=-1, keepdims=True)
            )
            d_low = d_mixed.astype(BF16)
            query = query_ref[rows, cols]
            key = key_ref[rows, cols]
            w_part = w_ref[rows, cols]
            inside = jnp.logical_and(same_block(row, col, SPAN), row >= col)
            d_score = jnp.where(inside, dot_nt(d_low, update_ref[rows, cols]), 0.0).astype(BF16)
            y_part = dot_tn(score_ref[group * heads_here + head], d_low)
            y_scr[rows, cols] = y_part
            y_low = y_part.astype(BF16)
            d_key_scr[rows, cols] = dot_tn(d_score, query)
            reads = []
            for piece in range(PER_GROUP):
                part = slice(piece * SPAN, (piece + 1) * SPAN)
                slot = (group * PER_GROUP + piece) * heads_here + head
                add_scr[slot] = dot_tn(
                    jnp.concatenate([query[part], w_part[part]], 0),
                    jnp.concatenate([d_low[part], -y_low[part]], 0),
                )
                reads.append(dot_nt(d_low[part], start_ref[slot]))
            d_query_scr[rows, cols] = dot_nn(d_score, key) + jnp.concatenate(reads, 0)
        return carry

    lax.fori_loop(0, groups, local_part, 0)
    if chips > 2:
        scatter.step(1)
    mix.advance(1)

    def scan_part(step, states):
        span = spans - 1 - step
        begun = []
        for sequence in range(sequences):
            for head in range(heads_here):
                block = sequence * spans + span
                slot = block * heads_here + head
                d_end = states[sequence * heads_here + head]
                d_end_low = d_end.astype(BF16)
                end_scr[slot] = d_end_low
                begun.append(
                    (d_end - dot_tn(map_ref[slot], d_end_low) + add_scr[slot])
                    * span_keep(ids_ref, block)
                )
        return tuple(begun)

    blank = tuple(jnp.zeros((DH, DH), F32) for _ in range(sequences * heads_here))
    lax.fori_loop(0, spans, scan_part, blank)
    scatter.steps(2)
    mix.advance(2)

    def finish_part(group, carry):
        start = pl.multiple_of(group * GROUP, GROUP)
        rows = pl.ds(start, GROUP)
        keep_rows = span_rows(ids_ref, group)
        row, col = grid_masks()
        d_logits = []
        for head in range(heads_here):
            cols = slice(head * DH, (head + 1) * DH)
            beta = jax.nn.sigmoid(proj_ref[rows, 3 * width + head : 3 * width + head + 1])
            key = key_ref[rows, cols]
            update = update_ref[rows, cols]
            reads = []
            for piece in range(PER_GROUP):
                part = slice(piece * SPAN, (piece + 1) * SPAN)
                slot = (group * PER_GROUP + piece) * heads_here + head
                reads.append(dot_nn(key[part], end_scr[slot]))
            d_update = y_scr[rows, cols] + jnp.concatenate(reads, 0)
            d_right = dot_tn(solve_ref[group * heads_here + head], d_update)
            d_value = beta * d_right
            d_value_low = d_value.astype(BF16)
            d_logit = (1.0 - beta) * jnp.sum(
                d_right * update.astype(F32), axis=-1, keepdims=True
            )
            d_logits.append(d_logit)
            inside = jnp.logical_and(same_block(row, col, SPAN), row > col)
            d_inner = jnp.where(inside, dot_nt(d_value_low, update), 0.0)
            reads = []
            for piece in range(PER_GROUP):
                part = slice(piece * SPAN, (piece + 1) * SPAN)
                slot = (group * PER_GROUP + piece) * heads_here + head
                reads.append(
                    dot_nt(
                        jnp.concatenate([update[part], -d_value_low[part]], 1),
                        jnp.concatenate([end_scr[slot], start_ref[slot]], 1),
                    )
                )
            d_key = (
                d_key_scr[rows, cols]
                + jnp.concatenate(reads, 0)
                - dot_nn(d_inner + d_inner.T, key)
            )
            grads = (d_query_scr[rows, cols] * DH ** (-0.5), d_key, d_value)
            for kind in range(3):
                pre = conv_rows(
                    proj_ref, conv_ref, group, kind, kind * width + head * DH, head, keep_rows
                )
                gate = jax.nn.sigmoid(pre)
                act = pre * gate
                d_act = grads[kind]
                if kind < 2:
                    scale = unit_scale(act)
                    hat = act * scale
                    d_act = scale * (d_act - hat * jnp.sum(hat * d_act, axis=-1, keepdims=True))
                first = kind * width + head * DH
                d_conv_scr[rows, first : first + DH] = d_act * gate * (1.0 + pre * (1.0 - gate))
        lane = lax.broadcasted_iota(jnp.int32, (GROUP, LANES), 1)
        spread = jnp.zeros((GROUP, LANES), F32)
        for head in range(heads_here):
            spread = jnp.where(lane == head, d_logits[head], spread)
        d_logit_ref[rows, :] = spread.astype(BF16)
        return carry

    lax.fori_loop(0, groups, finish_part, 0)
    mix.advance(3)
    d_conv_scr[rows_total : rows_total + 8, :] = jnp.zeros((8, 3 * width), F32)

    def conv_part(group, carry):
        start = pl.multiple_of(group * GROUP, GROUP)
        rows = pl.ds(start, GROUP)
        after = pl.ds(pl.multiple_of(start + GROUP, GROUP), 8)
        keep_rows = span_rows(ids_ref, group)
        follower = jnp.minimum((group + 1) * PER_GROUP, rows_total // SPAN - 1)
        keep_after = jnp.full((8, 1), 1.0, F32) * span_keep(ids_ref, follower)
        keep_joined = jnp.concatenate([keep_rows, keep_after], 0)
        place = lax.broadcasted_iota(jnp.int32, (GROUP + 8, 1), 0) % SPAN
        for kind in range(3):
            for head in range(heads_here):
                first = kind * width + head * DH
                cols = slice(first, first + DH)
                taps = conv_ref[kind, :, head * DH : (head + 1) * DH]
                here = d_conv_scr[rows, cols]
                joined = jnp.concatenate([here, d_conv_scr[after, cols]], 0)
                total = taps[KCONV - 1 : KCONV] * here
                sums = [jnp.sum(here * proj_ref[rows, cols], axis=0, keepdims=True)]
                for offset in range(1, KCONV):
                    counted = jnp.logical_or(place >= offset, keep_joined > 0.0)
                    masked = jnp.where(counted, joined, 0.0)
                    shifted = pltpu.roll(masked, GROUP + 8 - offset, 0)[:GROUP]
                    total = total + taps[KCONV - 1 - offset : KCONV - offset] * shifted
                    sums.append(
                        jnp.sum(
                            here * earlier_rows(proj_ref, group, first, offset, keep_rows),
                            axis=0,
                            keepdims=True,
                        )
                    )
                d_proj_ref[rows, cols] = total.astype(BF16)
                grad_conv_ref[kind, :, head * DH : (head + 1) * DH] += jnp.concatenate(
                    sums[::-1], 0
                )
        return carry

    lax.fori_loop(0, groups, conv_part, 0)
    loads[3].wait()

    def grad_part(tile, carry):
        cols = pl.ds(pl.multiple_of(tile * TILE, TILE), TILE)
        here = rows_ref[:, cols]
        grads = dot_tn(here, d_proj_ref[...]).astype(BF16)
        for kind in range(3):
            mix_grads[kind][cols, :] = grads[:, kind * width : (kind + 1) * width]
        grad_beta_ref[:, cols] = dot_tn(d_logit_ref[...], here)[:8]
        return carry

    lax.fori_loop(0, depth // TILE, grad_part, 0)
    scatter.end(result)
    out_ref[...] = (residual_ref[...] + result[...]).astype(BF16)
    for step in range(4, 2 * bits + 1):
        mix.advance(step)
    scatter.finish()


def project_back_kernel(
    chips,
    bits,
    flips,
    d_proj_ref,
    d_logit_ref,
    weight_ref,
    beta_ref,
    tokens_ref,
    gain_ref,
    d_residual_ref,
    grad_beta_ref,
    grad_conv_ref,
    part_head_ref,
    part_ffn_ref,
    *refs,
):
    mix_in, refs = refs[:3], refs[3:]
    grad_tokens_ref, gains_ref = refs[:2]
    mix_out, scratch = refs[2:6], refs[6:]
    block, depth = tokens_ref.shape
    mp_flips, peers = flips, 2**bits
    load_sems, scatter_refs, gain_total = scratch[0], scratch[1:5], scratch[5]
    gains = SmallSum(mp_flips, peers, gain_total, *scratch[6:10])
    mix = plane_sum(bits, mix_out, (0, 0, 0, 1), scratch[10:])
    loads = [
        pltpu.make_async_copy(source, mix.bufs[index][0], load_sems.at[index])
        for index, source in enumerate(mix_in)
    ]
    for load in loads:
        load.start()
    small_ref = mix.bufs[3][0]
    taps = jnp.zeros((8, grad_conv_ref.shape[2]), F32)
    small_ref[...] = jnp.zeros_like(small_ref)
    small_ref[:16, :] = jnp.concatenate(
        [grad_beta_ref[...], jnp.zeros((8, depth), F32)], 0
    ).astype(BF16)
    small_ref[16:32, : grad_conv_ref.shape[2]] = jnp.concatenate(
        [grad_conv_ref[0], grad_conv_ref[1], grad_conv_ref[2], taps[:4]], 0
    ).astype(BF16)
    line_barrier(chips, mp_flips, peers)
    for load in loads:
        load.wait()
    width = weight_ref.shape[2]
    mix.advance(0)

    def term(chip, core):
        rows = pl.ds(pl.multiple_of((2 * chip + core) * block, block), block)
        total = dot_nn(d_logit_ref[rows, :], beta_ref[...])
        for kind in range(3):
            total = total + dot_nt(
                d_proj_ref[rows, kind * width : (kind + 1) * width], weight_ref[kind]
            )
        return total

    def each(index):
        @pl.when(index == max(chips - 3, 0))
        def _():
            mix.advance(1)

        @pl.when(index == chips - 2)
        def _():
            mix.advance(2)

    scatter = LineScatter(chips, term, *scatter_refs)
    scatter.run(grad_tokens_ref, each)
    for step in range(3, 2 * bits):
        mix.advance(step)
    d_normed = grad_tokens_ref[...]
    tokens = tokens_ref[...].astype(F32)
    scale = row_scale(tokens)
    hat = tokens * scale
    weighted = gain_ref[...] * d_normed
    gain_total[...] = jnp.zeros_like(gain_total)
    gain_total[0:1, :] = jnp.sum(d_normed * hat, axis=0, keepdims=True)
    gain_total[1:2, :] = part_ffn_ref[...]
    gain_total[2:3, :DH] = part_head_ref[...]
    gains.advance(0)
    grad_tokens_ref[...] = d_residual_ref[...] + scale * (
        weighted - hat * jnp.mean(weighted * hat, axis=-1, keepdims=True)
    )
    for step in range(1, len(mp_flips) + 1):
        gains.advance(step)
    scatter.finish()
    mix.advance(2 * bits)
    gains.end(gains_ref)


def line_call(kernel, name, collective, shapes, scratch, specs, args, out_specs=None):
    return pl.pallas_call(
        kernel,
        out_shape=shapes,
        in_specs=specs,
        out_specs=tuple(out_specs or [whole()] * len(shapes)),
        scratch_shapes=scratch,
        compiler_params=pltpu.CompilerParams(
            collective_id=collective, has_side_effects=True, vmem_limit_bytes=VMEM_LIMIT
        ),
        name=name,
    )(*args)


def widen_kernel(*refs):
    gate_ref, upward_ref, down_ref, q_ref, k_ref, v_ref, out_ref, small_ref, gains_ref = refs[:9]
    wide_gate_up, wide_down, wide_qkv, wide_out = refs[9:13]
    beta_ref, conv_ref, norm_ref, ffn_ref, head_ref = refs[13:]
    wide_gate_up[0] = gate_ref[...].astype(F32)
    wide_gate_up[1] = upward_ref[...].astype(F32)
    wide_down[...] = down_ref[...].astype(F32)
    for kind, ref in enumerate((q_ref, k_ref, v_ref)):
        wide_qkv[kind] = ref[...].astype(F32)
    wide_out[...] = out_ref[...].astype(F32)

    @pl.when(pl.program_id(0) == 0)
    def _():
        small = small_ref[...].astype(F32)
        beta_ref[...] = small[: beta_ref.shape[0]]
        for kind in range(3):
            first = 16 + KCONV * kind
            conv_ref[kind] = small[first : first + KCONV, : conv_ref.shape[2]]
        norm_ref[...] = gains_ref[0:1, :]
        ffn_ref[...] = gains_ref[1:2, :]
        head_ref[...] = gains_ref[2:3, :DH]


def widen(gate, upward, down, query, key, value, out, small, gains):
    hidden_width, depth = gate.shape
    width = query.shape[1]
    steps = depth // LANES // 4
    across = pl.BlockSpec((hidden_width, depth // steps), lambda step: (0, step))
    along = pl.BlockSpec((depth // steps, width), lambda step: (step, 0))
    flat = pl.BlockSpec((width, depth // steps), lambda step: (0, step))

    def fixed(shape):
        return pl.BlockSpec(shape, lambda step: (0,) * len(shape))

    like = jax.ShapeDtypeStruct
    return pl.pallas_call(
        widen_kernel,
        out_shape=(
            like((2, hidden_width, depth), F32),
            like((hidden_width, depth), F32),
            like((3, depth, width), F32),
            like((width, depth), F32),
            like((width // DH, depth), F32),
            like((3, KCONV, width), F32),
            like((1, depth), F32),
            like((1, depth), F32),
            like((1, DH), F32),
        ),
        grid=(steps,),
        in_specs=[across] * 3 + [along] * 3 + [flat, fixed((32, depth)), fixed((8, depth))],
        out_specs=(
            pl.BlockSpec((2, hidden_width, depth // steps), lambda step: (0, 0, step)),
            across,
            pl.BlockSpec((3, depth // steps, width), lambda step: (0, step, 0)),
            flat,
            fixed((width // DH, depth)),
            fixed((3, KCONV, width)),
            fixed((1, depth)),
            fixed((1, depth)),
            fixed((1, DH)),
        ),
        compiler_params=pltpu.CompilerParams(vmem_limit_bytes=VMEM_LIMIT),
        name="widen_sums",
    )(gate, upward, down, query, key, value, out, small, gains)


def body(
    chips,
    dp_bits,
    mp_bits,
    tokens,
    grad_out,
    doc_ids,
    norm_gain,
    qkv_weight,
    beta_weight,
    conv_weight,
    head_gain,
    out_weight,
    ffn_gain,
    gate_up_weight,
    down_weight,
):
    width = qkv_weight.shape[2]
    heads_here = width // DH
    block, depth = tokens.shape
    rows_total = 2 * chips * block
    hidden_width = down_weight.shape[0]
    like = jax.ShapeDtypeStruct
    any_spec = pl.BlockSpec(memory_space=pl.ANY)
    norm_row = norm_gain.reshape(1, depth)
    ffn_row = ffn_gain.reshape(1, depth)
    beta_pad = jnp.pad(beta_weight.T, ((0, LANES - heads_here), (0, 0)))
    gate_up_rows = jnp.swapaxes(gate_up_weight, 1, 2)

    f32_rows = pltpu.VMEM((rows_total, width), F32)
    grids = rows_total // GROUP * heads_here
    slots = rows_total // SPAN * heads_here
    mix_shapes = (
        like((rows_total, depth), BF16),
        like((rows_total, 3 * width + LANES), F32),
        like((rows_total, width), BF16),
        like((rows_total, width), BF16),
        like((grids, GROUP, GROUP), BF16),
        like((rows_total, width), BF16),
        like((grids, GROUP, GROUP), BF16),
        like((slots, DH, DH), BF16),
        like((slots, DH, DH), BF16),
        like((rows_total, width), BF16),
        like((rows_total, width), F32),
        like((rows_total, width), BF16),
        like((rows_total, depth), BF16),
    )
    rows_one, projected, query, key, solve, w_part, score, maps, starts, *rest = (
        line_call(
            functools.partial(project_mix_kernel, chips, heads_here),
            "project_mix",
            1,
            mix_shapes,
            [pltpu.VMEM(shape.shape, shape.dtype) for shape in mix_shapes]
            + [
                pltpu.VMEM(qkv_weight.shape, BF16),
                f32_rows,
                pltpu.VMEM((slots, DH, DH), F32),
                pltpu.SemaphoreType.DMA,
                pltpu.SemaphoreType.DMA((len(mix_shapes),)),
                line_sems(chips),
                line_sems(chips),
                pltpu.SemaphoreType.DMA((3,)),
            ],
            [pl.BlockSpec(memory_space=pltpu.SMEM)] + [whole()] * 2 + [any_spec] + [whole()] * 4,
            (
                doc_ids,
                tokens,
                norm_row,
                qkv_weight,
                beta_pad,
                conv_weight,
                head_gain.reshape(1, DH),
                grad_out,
            ),
            [any_spec] * len(mix_shapes),
        )
    )
    heads_out, mixed, update, grads_all = rest
    kept = (mixed, query, key, solve, w_part, score, maps, starts, update)
    feed_shape = like((rows_total, hidden_width), BF16)
    grad_shape = like((hidden_width, depth), BF16)
    residual, hidden, d_gate, d_upward, *feed_grads = line_call(
        functools.partial(attend_feed_kernel, chips),
        "attend_feed",
        2,
        (like((block, depth), F32),) + (feed_shape,) * 3 + (grad_shape,) * 3,
        scatter_scratch(chips, block, depth)
        + [
            line_sems(chips),
            line_sems(chips),
            pltpu.VMEM((rows_total, depth), BF16),
            pltpu.VMEM(gate_up_rows.shape, BF16),
            pltpu.VMEM(down_weight.shape, BF16),
            pltpu.VMEM((rows_total, depth), BF16),
            pltpu.VMEM((rows_total, hidden_width), BF16),
            pltpu.VMEM((3, hidden_width, depth), F32),
            pltpu.VMEM((2, hidden_width, TILE), BF16),
            pltpu.VMEM((3, 2 * block, hidden_width), BF16),
            pltpu.SemaphoreType.DMA((2,)),
            pltpu.SemaphoreType.DMA((2,)),
            pltpu.SemaphoreType.DMA((3,)),
            pltpu.SemaphoreType.DMA((3,)),
        ],
        [whole()] * 4 + [any_spec] * 3,
        (heads_out, out_weight, tokens, ffn_row, gate_up_rows, down_weight, grads_all),
        [whole()] + [any_spec] * 6,
    )
    dp_flips = tuple(("dp", bit) for bit in range(dp_bits))
    mp_flips = tuple(("mp", bit) for bit in range(mp_bits))
    feed_sums = lax.psum(tuple(feed_grads[1:]), "dp")
    d_residual, d_heads, grad_out_weight, part_ffn_gain, sum_down = line_call(
        functools.partial(feed_back_kernel, chips, dp_bits, dp_flips),
        "feed_back",
        3,
        (
            like((block, depth), F32),
            like((rows_total, width), F32),
            like((width, depth), BF16),
            like((1, depth), F32),
        )
        + (grad_shape,),
        scatter_scratch(chips, block, depth)
        + [
            line_sems(chips),
            pltpu.VMEM((rows_total, depth), BF16),
            pltpu.VMEM((width, depth), F32),
            pltpu.SemaphoreType.DMA((1,)),
            pltpu.SemaphoreType.DMA((1,)),
            pltpu.VMEM(grad_shape.shape, BF16),
        ]
        + plane_scratch(dp_bits, [(grad_shape.shape, 1)]),
        [whole()] * 8 + [any_spec],
        (
            d_gate,
            d_upward,
            gate_up_rows,
            residual,
            ffn_row,
            grad_out,
            heads_out,
            out_weight,
            feed_grads[0],
        ),
        [whole()] * 4 + [any_spec],
    )
    qkv_shape = like((depth, width), BF16)
    kept = (projected, *kept, d_heads)
    d_projected, d_logit, grad_conv, part_head_gain, grad_beta, block_out, *sums = line_call(
        functools.partial(mixer_backward_kernel, chips, dp_bits, dp_flips, heads_here),
        "mixer_backward",
        5,
        (
            like((rows_total, 3 * width), BF16),
            like((rows_total, LANES), BF16),
            like(conv_weight.shape, F32),
            like((1, DH), F32),
            like((8, depth), F32),
            like((block, depth), BF16),
        )
        + (qkv_shape,) * 3
        + (like((width, depth), BF16),),
        [
            f32_rows,
            pltpu.VMEM((slots, DH, DH), F32),
            pltpu.VMEM((slots, DH, DH), BF16),
            f32_rows,
            f32_rows,
            pltpu.VMEM((rows_total + 8, 3 * width), F32),
            pltpu.VMEM((rows_total, hidden_width), BF16),
            pltpu.VMEM(down_weight.shape, BF16),
            pltpu.VMEM((rows_total, depth), BF16),
            pltpu.VMEM((block, depth), F32),
            pltpu.SemaphoreType.DMA((4,)),
        ]
        + scatter_scratch(chips, block, depth)
        + [pltpu.VMEM(array.shape, array.dtype) for array in kept]
        + [pltpu.SemaphoreType.DMA((len(kept),))]
        + plane_scratch(dp_bits, [((width, depth), 1)]),
        [pl.BlockSpec(memory_space=pltpu.SMEM)] + [whole()] * 3 + [any_spec] * 15,
        (
            doc_ids,
            conv_weight,
            head_gain.reshape(1, DH),
            residual,
            hidden,
            down_weight,
            rows_one,
            *kept,
            grad_out_weight,
        ),
    )
    mix_grads, sum_out = sums[:3], sums[3]
    sum_shapes = (qkv_shape,) * 3 + (like((32, depth), BF16),)
    grad_tokens, gains, *mix_sums = line_call(
        functools.partial(project_back_kernel, chips, dp_bits, mp_flips),
        "project_back",
        4,
        (like((block, depth), F32), like((8, depth), F32), *sum_shapes),
        [pltpu.SemaphoreType.DMA((3,))]
        + scatter_scratch(chips, block, depth)
        + [
            pltpu.VMEM((8, depth), F32),
            pltpu.VMEM((mp_bits, 8, depth), F32),
            pltpu.VMEM((2**dp_bits, 8, depth), F32),
            pltpu.SemaphoreType.DMA((2, mp_bits)),
            pltpu.SemaphoreType.DMA((2, 2**dp_bits - 1)),
        ]
        + plane_scratch(
            dp_bits, [(shape.shape, 1 if index == 3 else 0) for index, shape in enumerate(sum_shapes)]
        ),
        [whole()] * 11 + [any_spec] * 3,
        (
            d_projected,
            d_logit,
            qkv_weight,
            beta_pad,
            tokens,
            norm_row,
            d_residual,
            grad_beta,
            grad_conv,
            part_head_gain,
            part_ffn_gain,
            *mix_grads,
        ),
    )
    wide_gate_up, wide_down, wide_qkv, wide_out, *rest = widen(
        *feed_sums, sum_down, *mix_sums[:3], sum_out, mix_sums[3], gains
    )
    sum_beta, sum_conv, sum_norm, sum_ffn, sum_head = rest
    return (
        block_out,
        grad_tokens,
        sum_norm.reshape(depth),
        wide_qkv,
        sum_beta.T,
        sum_conv,
        sum_head.reshape(DH),
        wide_out,
        sum_ffn.reshape(depth),
        jnp.swapaxes(wide_gate_up, 1, 2),
        wide_down,
    )


def solution(mesh):
    in_specs = (
        P(("dp", "mp"), None),
        P(("dp", "mp"), None),
        P("dp"),
        P(),
        P(None, None, "mp"),
        P(None, "mp"),
        P(None, None, "mp"),
        P(),
        P("mp", None),
        P(),
        P(None, None, "mp"),
        P("mp", None),
    )
    out_specs = (
        P(("dp", "mp"), None),
        P(("dp", "mp"), None),
        P(),
        P(None, None, "mp"),
        P(None, "mp"),
        P(None, None, "mp"),
        P(),
        P("mp", None),
        P(),
        P(None, None, "mp"),
        P("mp", None),
    )
    chips = mesh.shape["mp"] // 2
    dp_bits = mesh.shape["dp"].bit_length() - 1
    mp_bits = mesh.shape["mp"].bit_length() - 1
    part = functools.partial(body, chips, dp_bits, mp_bits)
    return jax.shard_map(part, mesh=mesh, in_specs=in_specs, out_specs=out_specs, check_vma=False)
```

```python
import functools

import jax
import jax.numpy as jnp
from jax import lax
from jax.experimental import pallas as pl
from jax.experimental.pallas import tpu as pltpu
from jax.sharding import PartitionSpec as P

DH = 128
KCONV = 4
SPAN = 64
LEN = 1024


EPSILON = 1e-06


def row_scale(values):
    return lax.rsqrt(jnp.mean(values * values, axis=-1, keepdims=True) + EPSILON)


BF16 = jnp.bfloat16
F32 = jnp.float32
GROUP = 256
LANES = 128
PER_GROUP = GROUP // SPAN


def dot_nn(left, right):
    return lax.dot_general(
        left.astype(BF16), right.astype(BF16), (((1,), (0,)), ((), ())), preferred_element_type=F32
    )


def dot_nt(left, right):
    return lax.dot_general(
        left.astype(BF16), right.astype(BF16), (((1,), (1,)), ((), ())), preferred_element_type=F32
    )


def dot_tn(left, right):
    return lax.dot_general(
        left.astype(BF16), right.astype(BF16), (((0,), (0,)), ((), ())), preferred_element_type=F32
    )


def span_keep(ids_ref, block):
    first = block * SPAN
    same = ids_ref[first] == ids_ref[jnp.maximum(first - 1, 0)]
    return jnp.where(jnp.logical_and(same, lax.rem(first, LEN) != 0), 1.0, 0.0)


def span_rows(ids_ref, group):
    piece = lax.broadcasted_iota(jnp.int32, (GROUP, 1), 0) // SPAN
    rows = jnp.zeros((GROUP, 1), F32)
    for index in range(PER_GROUP):
        rows = jnp.where(piece == index, span_keep(ids_ref, group * PER_GROUP + index), rows)
    return rows


def grid_masks():
    row = lax.broadcasted_iota(jnp.int32, (GROUP, GROUP), 0)
    col = lax.broadcasted_iota(jnp.int32, (GROUP, GROUP), 1)
    return row, col


def same_block(row, col, size):
    return (row // size) == (col // size)


def tap_rows(offset, keep_rows):
    place = lax.broadcasted_iota(jnp.int32, (GROUP, 1), 0) % SPAN
    return jnp.logical_or(place >= offset, keep_rows > 0.0)


def earlier_rows(ref, group, first_col, offset, keep_rows):
    start = pl.multiple_of(group * GROUP, GROUP)
    prior = pl.multiple_of(jnp.maximum(start - 8, 0), 8)
    cols = slice(first_col, first_col + DH)
    joined = jnp.concatenate([ref[pl.ds(prior, 8), cols], ref[pl.ds(start, GROUP), cols]], 0)
    shifted = pltpu.roll(joined, offset, 0)[8:]
    return jnp.where(tap_rows(offset, keep_rows), shifted, 0.0)


def conv_rows(ref, conv_ref, group, kind, first_col, head, keep_rows):
    taps = conv_ref[kind, :, head * DH : (head + 1) * DH]
    start = pl.multiple_of(group * GROUP, GROUP)
    running = taps[KCONV - 1 : KCONV] * ref[pl.ds(start, GROUP), first_col : first_col + DH]
    for offset in range(1, KCONV):
        running = running + taps[KCONV - 1 - offset : KCONV - offset] * earlier_rows(
            ref, group, first_col, offset, keep_rows
        )
    return running


def unit_scale(values):
    return lax.rsqrt(jnp.sum(values * values, axis=-1, keepdims=True) + EPSILON)


VMEM_LIMIT = 60 * 1024 * 1024


def whole():
    return pl.BlockSpec(memory_space=pltpu.VMEM)


MESH = pl.DeviceIdType.MESH
TILE = 512
CORE, RIGHT, LEFT = 0, 1, 2


def line_place():
    me = lax.axis_index("mp")
    core = lax.rem(me, 2)
    return me, me // 2, core


def flip_bit(axis, bit):
    place = lax.axis_index(axis)
    scale = 2**bit
    mine = lax.rem(place // scale, 2)
    return mine, {axis: place + (1 - 2 * mine) * scale}


def line_barrier(chips, flips=(), peers=1):
    me, chip, core = line_place()
    barrier = pltpu.get_barrier_semaphore()
    for axis, bit in flips:
        pl.semaphore_signal(
            barrier, inc=1, device_id=flip_bit(axis, bit)[1], device_id_type=MESH
        )
    for step in range(1, peers):
        place = lax.rem(lax.axis_index("dp") + step, peers)
        pl.semaphore_signal(barrier, inc=1, device_id={"dp": place}, device_id_type=MESH)

    def greet(other):
        pl.semaphore_signal(barrier, inc=1, device_id={"mp": other}, device_id_type=MESH)

    greet(me + 1 - 2 * core)

    @pl.when(chip > 0)
    def _():
        greet(me - 2)

    @pl.when(chip < chips - 1)
    def _():
        greet(me + 2)

    beside = (chip > 0).astype(jnp.int32) + (chip < chips - 1).astype(jnp.int32)
    pl.semaphore_wait(barrier, beside + len(flips) + peers)


def line_target(kind):
    me, chip, core = line_place()
    return {CORE: me + 1 - 2 * core, RIGHT: me + 2, LEFT: me - 2}[kind]


class LineGather:
    def __init__(self, chips, out_ref, sems):
        self.chips, self.out_ref, self.sems = chips, out_ref, sems
        self.block = out_ref.shape[0] // (2 * chips)
        self.me, self.chip, self.core = line_place()

    def rows(self, chip, core):
        return pl.ds(pl.multiple_of((2 * chip + core) * self.block, self.block), self.block)

    def copy(self, kind, chip, core):
        part = self.out_ref.at[self.rows(chip, core), :]
        return pltpu.make_async_remote_copy(
            src_ref=part,
            dst_ref=part,
            send_sem=self.sems.at[2 * kind, chip],
            recv_sem=self.sems.at[2 * kind + 1, chip],
            device_id={"mp": line_target(kind)},
            device_id_type=MESH,
        )

    def start(self, block):
        self.out_ref[self.rows(self.chip, self.core), :] = block

        @pl.when(self.chip < self.chips - 1)
        def _():
            self.copy(RIGHT, self.chip, self.core).start()

        @pl.when(self.chip > 0)
        def _():
            self.copy(LEFT, self.chip, self.core).start()

        self.copy(CORE, self.chip, self.core).start()

    def arrive(self, chip):
        self.copy(CORE, chip, 1 - self.core).wait_recv()

    def each_new(self, step, use):
        behind, ahead = self.chip - step, self.chip + step

        @pl.when(behind >= 0)
        def _():
            use(behind)

        @pl.when(ahead < self.chips)
        def _():
            use(ahead)

    def pass_on(self, behind, ahead):
        @pl.when(jnp.logical_and(behind >= 0, self.chip < self.chips - 1))
        def _():
            self.copy(RIGHT, behind, self.core).start()

        @pl.when(jnp.logical_and(ahead < self.chips, self.chip > 0))
        def _():
            self.copy(LEFT, ahead, self.core).start()

    def hop(self, step, forward=True):
        behind, ahead = self.chip - step, self.chip + step

        @pl.when(behind >= 0)
        def _():
            self.copy(RIGHT, behind, self.core).wait_recv()

        @pl.when(ahead < self.chips)
        def _():
            self.copy(LEFT, ahead, self.core).wait_recv()

        if forward:
            self.pass_on(behind, ahead)

        self.each_new(step, lambda chip: self.copy(CORE, chip, self.core).start())
        self.each_new(step, self.arrive)

    def hops(self, after):
        def one_hop(step, carry):
            self.hop(step)
            after(step)
            return carry

        lax.fori_loop(1, self.chips, one_hop, 0)

    def finish(self, first=0, end=None):
        end = self.chips if end is None else end

        def sent(chip, carry):
            apart = jnp.abs(chip - self.chip)
            relay = jnp.logical_and(apart >= first - 1, apart < end - 1)
            if first == 0:
                relay = jnp.logical_or(relay, apart == 0)
            to_right = jnp.logical_and(chip <= self.chip, self.chip < self.chips - 1)
            to_left = jnp.logical_and(chip >= self.chip, self.chip > 0)

            @pl.when(jnp.logical_and(relay, to_right))
            def _():
                self.copy(RIGHT, chip, self.core).wait_send()

            @pl.when(jnp.logical_and(relay, to_left))
            def _():
                self.copy(LEFT, chip, self.core).wait_send()

            @pl.when(jnp.logical_and(apart >= first, apart < end))
            def _():
                self.copy(CORE, chip, self.core).wait_send()

            return carry

        lax.fori_loop(0, self.chips, sent, 0)


class LineScatter:
    def __init__(self, chips, term, stage, held, landing, sems):
        self.chips, self.term = chips, term
        self.stage, self.held, self.landing, self.sems = stage, held, landing, sems
        self.me, self.chip, self.core = line_place()

    def left_slot(self, chip, receiver):
        return jnp.where(chip == receiver, self.chips, chip)

    def copy(self, kind, chip):
        source = (self.stage if kind == CORE else self.held).at[chip]
        if kind == CORE:
            target = self.held.at[chip]
        elif kind == RIGHT:
            target = self.landing.at[chip]
        else:
            target = self.landing.at[self.left_slot(chip, self.chip - 1)]
        return pltpu.make_async_remote_copy(
            src_ref=source,
            dst_ref=target,
            send_sem=self.sems.at[2 * kind, chip],
            recv_sem=self.sems.at[2 * kind + 1, chip],
            device_id={"mp": line_target(kind)},
            device_id_type=MESH,
        )

    def exchange(self, chip):
        self.stage[chip] = self.term(chip, 1 - self.core).astype(BF16)
        self.copy(CORE, chip).start()

    def collect(self, chip):
        own = self.term(chip, self.core)
        self.copy(CORE, chip).wait_recv()
        return own + self.held[chip].astype(F32)

    def pass_on(self, kind, chip, first):
        both = self.collect(chip)

        @pl.when(first)
        def _():
            self.held[chip] = both.astype(BF16)

        @pl.when(jnp.logical_not(first))
        def _():
            self.copy(kind, chip).wait_recv()
            self.held[chip] = (both + self.landing[chip].astype(F32)).astype(BF16)

        self.copy(kind, chip).start()

    def exchange_pair(self, step):
        @pl.when(self.chip + step < self.chips)
        def _():
            self.exchange(self.chip + step)

        @pl.when(self.chip - step >= 0)
        def _():
            self.exchange(self.chip - step)

    def begin(self):
        self.exchange_pair(self.chips - 1)

    def step(self, index):
        last = self.chips - 1
        step = last - index

        @pl.when(step > 1)
        def _():
            self.exchange_pair(step - 1)

        @pl.when(self.chip + step < self.chips)
        def _():
            self.pass_on(RIGHT, self.chip + step, self.chip == 0)

        @pl.when(self.chip - step >= 0)
        def _():
            self.pass_on(LEFT, self.chip - step, self.chip == last)

    def steps(self, first, each=None):
        def one_step(index, carry):
            self.step(index)
            if each is not None:
                each(index)
            return carry

        lax.fori_loop(first, self.chips - 1, one_step, 0)

    def end(self, result_ref):
        self.exchange(self.chip)
        result_ref[...] = self.collect(self.chip)

        @pl.when(self.chip > 0)
        def _():
            self.copy(RIGHT, self.chip).wait_recv()
            result_ref[...] += self.landing[self.chip].astype(F32)

        @pl.when(self.chip < self.chips - 1)
        def _():
            self.copy(LEFT, self.chip).wait_recv()
            result_ref[...] += self.landing[self.chips].astype(F32)

    def run(self, result_ref, each=None):
        self.begin()
        self.steps(0, each)
        self.end(result_ref)

    def finish(self):
        def sent(chip, carry):
            @pl.when(chip > self.chip)
            def _():
                self.copy(RIGHT, chip).wait_send()

            @pl.when(chip < self.chip)
            def _():
                self.copy(LEFT, chip).wait_send()

            self.copy(CORE, chip).wait_send()
            return carry

        lax.fori_loop(0, self.chips, sent, 0)


class PlaneSum:
    def __init__(self, bits, bufs, outs, landings, sems):
        self.bits, self.bufs, self.outs = bits, bufs, outs
        self.landings, self.sems = landings, sems
        self.orders = (tuple(range(bits)), tuple(reversed(range(bits))))
        self.half = bufs[0][0].shape[bufs[0][1]] // 2

    def span(self, part, level):
        start = part * self.half
        for index in range(level):
            mine, _ = flip_bit("dp", self.orders[part][index])
            start = start + mine * (self.half >> (index + 1))
        return start

    def view(self, pairs, array, start, size):
        ref, axis = pairs[array]
        where = pl.ds(pl.multiple_of(start, size), size)
        return ref.at[where, :] if axis == 0 else ref.at[:, where]

    def pieces(self, part, index):
        mine, target = flip_bit("dp", self.orders[part][index])
        size = self.half >> (index + 1)
        start = self.span(part, index)
        return target, size, start + mine * size, start + (1 - mine) * size

    def copies(self, step):
        made = []
        for part in range(2):
            index = step if step < self.bits else 2 * self.bits - 1 - step
            target, size, kept, given = self.pieces(part, index)
            for array in range(len(self.bufs)):
                if step < self.bits:
                    source = self.view(self.bufs, array, given, size)
                    landing = self.landings[index][array].at[part]
                else:
                    source = self.view(self.outs, array, kept, size)
                    landing = source
                made.append(
                    pltpu.make_async_remote_copy(
                        src_ref=source,
                        dst_ref=landing,
                        send_sem=self.sems.at[0, part, step, array],
                        recv_sem=self.sems.at[1, part, step, array],
                        device_id=target,
                        device_id_type=MESH,
                    )
                )
        return made

    def advance(self, step, go=True):
        if step > 0:
            for copy in self.copies(step - 1):
                copy.wait()
            if step - 1 < self.bits:
                for part in range(2):
                    _, size, kept, _ = self.pieces(part, step - 1)
                    for array in range(len(self.bufs)):
                        here = self.view(self.bufs, array, kept, size)
                        ended = self.outs if step == self.bits else self.bufs
                        self.view(ended, array, kept, size)[...] = (
                            here[...].astype(F32)
                            + self.landings[step - 1][array][part].astype(F32)
                        ).astype(BF16)
        if go and step < 2 * self.bits:
            for copy in self.copies(step):
                copy.start()


def plane_scratch(bits, shapes):
    made = [pltpu.VMEM(shape, BF16) for shape, _ in shapes]
    for index in range(bits):
        for shape, axis in shapes:
            size = list(shape)
            size[axis] = size[axis] >> (index + 2)
            made.append(pltpu.VMEM((2, *size), BF16))
    return made + [pltpu.SemaphoreType.DMA((2, 2, 2 * bits, len(shapes)))]


def plane_sum(bits, outs, axes, scratch):
    count = len(outs)
    bufs, scratch = scratch[:count], scratch[count:]
    landings = [scratch[index * count : (index + 1) * count] for index in range(bits)]
    return PlaneSum(
        bits, list(zip(bufs, axes)), list(zip(outs, axes)), landings, scratch[bits * count]
    )


class SmallSum:
    def __init__(self, flips, peers, total_ref, landing, everyone, sems, peer_sems):
        self.flips, self.peers, self.total_ref = flips, peers, total_ref
        self.landing, self.everyone = landing, everyone
        self.sems, self.peer_sems = sems, peer_sems

    def copy(self, step):
        return pltpu.make_async_remote_copy(
            src_ref=self.total_ref,
            dst_ref=self.landing.at[step],
            send_sem=self.sems.at[0, step],
            recv_sem=self.sems.at[1, step],
            device_id=flip_bit(*self.flips[step])[1],
            device_id_type=MESH,
        )

    def spread(self):
        me = lax.axis_index("dp")
        return [
            pltpu.make_async_remote_copy(
                src_ref=self.everyone.at[me],
                dst_ref=self.everyone.at[me],
                send_sem=self.peer_sems.at[0, step],
                recv_sem=self.peer_sems.at[1, step],
                device_id={"dp": lax.rem(me + step + 1, self.peers)},
                device_id_type=MESH,
            )
            for step in range(self.peers - 1)
        ]

    def advance(self, step):
        if 0 < step <= len(self.flips):
            self.copy(step - 1).wait()
            self.total_ref[...] += self.landing[step - 1]
        if step < len(self.flips):
            self.copy(step).start()
        elif step == len(self.flips):
            self.everyone[lax.axis_index("dp")] = self.total_ref[...]
            for copy in self.spread():
                copy.start()

    def end(self, result_ref):
        for copy in self.spread():
            copy.wait()
        total = self.everyone[0]
        for peer in range(1, self.peers):
            total = total + self.everyone[peer]
        result_ref[...] = total


def line_sems(chips):
    return pltpu.SemaphoreType.DMA((6, chips))


def scatter_scratch(chips, block, depth):
    return [
        pltpu.VMEM((chips, block, depth), BF16),
        pltpu.VMEM((chips, block, depth), BF16),
        pltpu.VMEM((chips + 1, block, depth), BF16),
        line_sems(chips),
    ]


class Drain:
    def __init__(self, sems):
        self.sems, self.copies = sems, []

    def start(self, source, target):
        copy = pltpu.make_async_copy(source, target, self.sems.at[len(self.copies)])
        copy.start()
        self.copies.append(copy)

    def finish(self):
        for copy in self.copies:
            copy.wait()


def near_item(chips, chip, index):
    ahead, behind = chips - 1 - chip, chip
    both = jnp.minimum(ahead, behind)
    near = (index + 1) // 2
    turn = 1 - 2 * lax.rem(index + 1, 2)
    far = jnp.where(ahead > behind, 1, -1)
    return chip + jnp.where(index <= 2 * both, turn * near, far * (index - both))


def near_copies(chip, chips, source, target, sems):
    pair = source.shape[0] // chips
    made = []
    for index in range(3):
        other = chip + index - 1
        rows = pl.ds(pl.multiple_of(jnp.clip(other, 0, chips - 1) * pair, pair), pair)
        copy = pltpu.make_async_copy(source.at[rows, :], target.at[rows, :], sems.at[index])
        made.append((jnp.logical_and(other >= 0, other < chips), copy))
    return made


def project_mix_kernel(
    chips,
    heads_here,
    ids_ref,
    tokens_ref,
    norm_ref,
    weight_ref,
    beta_ref,
    conv_ref,
    gain_ref,
    grad_ref,
    *refs,
):
    outs, bufs, refs = refs[:13], refs[13:26], refs[26:]
    held, u_scr, add_scr, load_sem, drain_sems, sems, grad_sems, near_sems = refs
    (
        rows_ref,
        proj_ref,
        query_ref,
        key_ref,
        solve_ref,
        w_ref,
        score_ref,
        map_ref,
        start_ref,
        heads_ref,
        mixed_ref,
        update_ref,
        grads_ref,
    ) = bufs
    load = pltpu.make_async_copy(weight_ref, held, load_sem)
    load.start()
    tokens = tokens_ref[...].astype(F32)
    normed = (tokens * row_scale(tokens) * norm_ref[...]).astype(BF16)
    line_barrier(chips)
    gather = LineGather(chips, rows_ref, sems)
    gather.start(normed)
    load.wait()
    width = heads_here * DH
    rows_total = rows_ref.shape[0]
    groups = rows_total // GROUP
    spans = LEN // SPAN
    sequences = rows_total // LEN
    drain = Drain(drain_sems)

    def project(chip):
        rows = pl.ds(pl.multiple_of(chip * GROUP, GROUP), GROUP)
        here = rows_ref[rows, :]
        for kind in range(3):
            proj_ref[rows, kind * width : (kind + 1) * width] = dot_nn(here, held[kind])
        proj_ref[rows, 3 * width : 3 * width + LANES] = dot_nt(here, beta_ref[...])

    def local_part(group, carry):
        start = pl.multiple_of(group * GROUP, GROUP)
        rows = pl.ds(start, GROUP)
        keep_rows = span_rows(ids_ref, group)
        row, col = grid_masks()
        for head in range(heads_here):
            cols = slice(head * DH, (head + 1) * DH)
            act_q = jax.nn.silu(
                conv_rows(proj_ref, conv_ref, group, 0, head * DH, head, keep_rows)
            )
            query = (act_q * (unit_scale(act_q) * DH ** (-0.5))).astype(BF16)
            act_k = jax.nn.silu(
                conv_rows(proj_ref, conv_ref, group, 1, width + head * DH, head, keep_rows)
            )
            key = act_k * unit_scale(act_k)
            value = jax.nn.silu(
                conv_rows(proj_ref, conv_ref, group, 2, 2 * width + head * DH, head, keep_rows)
            )
            beta = jax.nn.sigmoid(proj_ref[rows, 3 * width + head : 3 * width + head + 1])
            key_low = key.astype(BF16)
            query_ref[rows, cols] = query
            key_ref[rows, cols] = key_low
            inside = same_block(row, col, SPAN)
            system = jnp.where(
                jnp.logical_and(inside, row > col), dot_nt(key_low, key_low) * beta, 0.0
            )
            score = jnp.where(jnp.logical_and(inside, row >= col), dot_nt(query, key_low), 0.0)
            score_ref[group * heads_here + head] = score.astype(BF16)
            solve = jnp.where(
                row == col, 1.0, jnp.where(same_block(row, col, 2), -system, 0.0)
            )
            size = 2
            while size < SPAN:
                cross = jnp.where(
                    jnp.logical_and(
                        same_block(row, col, 2 * size),
                        jnp.logical_not(same_block(row, col, size)),
                    ),
                    system,
                    0.0,
                )
                solve_low = solve.astype(BF16)
                solve = solve - dot_nn(solve_low, dot_nn(cross, solve_low))
                size *= 2
            solve_low = solve.astype(BF16)
            solve_ref[group * heads_here + head] = solve_low
            both = dot_nn(solve_low, jnp.concatenate([key * beta, value * beta], 1))
            both_low = both.astype(BF16)
            w_ref[rows, cols] = both_low[:, :DH]
            u_scr[rows, cols] = both[:, DH:]
            for piece in range(PER_GROUP):
                part = slice(piece * SPAN, (piece + 1) * SPAN)
                carry_pair = dot_tn(key_low[part], both_low[part])
                slot = (group * PER_GROUP + piece) * heads_here + head
                map_ref[slot] = carry_pair[:, :DH].astype(BF16)
                add_scr[slot] = carry_pair[:, DH:]
        return carry

    def after(step):
        gather.each_new(step, project)
        local_part(near_item(chips, gather.chip, step - 1), 0)

    gather.arrive(gather.chip)
    project(gather.chip)
    gather.hops(after)
    gather_grads = LineGather(chips, grads_ref, grad_sems)
    gather_grads.start(grad_ref[...])
    drain.start(bufs[0], outs[0])
    drain.start(bufs[1], outs[1])
    local_part(near_item(chips, gather.chip, chips - 1), 0)
    for index in range(2, 8):
        drain.start(bufs[index], outs[index])

    def scan_part(span, states):
        ended = []
        for sequence in range(sequences):
            for head in range(heads_here):
                block = sequence * spans + span
                slot = block * heads_here + head
                memory = states[sequence * heads_here + head] * span_keep(ids_ref, block)
                memory_low = memory.astype(BF16)
                start_ref[slot] = memory_low
                ended.append(memory - dot_nn(map_ref[slot], memory_low) + add_scr[slot])
        return tuple(ended)

    blank = tuple(jnp.zeros((DH, DH), F32) for _ in range(sequences * heads_here))
    lax.fori_loop(0, spans, scan_part, blank)

    drain.start(bufs[8], outs[8])

    def output_part(group, carry):
        start = pl.multiple_of(group * GROUP, GROUP)
        rows = pl.ds(start, GROUP)
        for head in range(heads_here):
            cols = slice(head * DH, (head + 1) * DH)
            query = query_ref[rows, cols]
            w_part = w_ref[rows, cols]
            updates, reads = [], []
            for piece in range(PER_GROUP):
                part = slice(piece * SPAN, (piece + 1) * SPAN)
                slot = (group * PER_GROUP + piece) * heads_here + head
                pair = dot_nn(jnp.concatenate([w_part[part], query[part]], 0), start_ref[slot])
                updates.append(pair[:SPAN])
                reads.append(pair[SPAN:])
            update = (u_scr[rows, cols] - jnp.concatenate(updates, 0)).astype(BF16)
            update_ref[rows, cols] = update
            mixed = jnp.concatenate(reads, 0) + dot_nn(score_ref[group * heads_here + head], update)
            mixed_ref[rows, cols] = mixed
            scale = lax.rsqrt(jnp.mean(mixed * mixed, axis=-1, keepdims=True) + EPSILON)
            heads_ref[rows, cols] = (mixed * scale * gain_ref[...]).astype(BF16)
        return carry

    lax.fori_loop(0, groups, output_part, 0)
    for index in range(9, 12):
        drain.start(bufs[index], outs[index])
    gather.finish()
    gather_grads.arrive(gather.chip)
    gather_grads.hop(1, False)
    near = near_copies(gather.chip, chips, grads_ref, outs[12], near_sems)
    for when, copy in near:
        pl.when(when)(copy.start)
    gather_grads.finish(0, 2)
    for when, copy in near:
        pl.when(when)(copy.wait)
    drain.finish()


def attend_feed_kernel(
    chips,
    heads_ref,
    weight_ref,
    tokens_ref,
    gain_ref,
    gate_up_any,
    down_any,
    grads_any,
    residual_ref,
    *refs,
):
    feed_outs, grad_outs, refs = refs[:3], refs[3:6], refs[6:]
    (stage, held, landing, scatter_sems, gather_sems, grad_sems, rows_ref) = refs[:7]
    (gate_up_ref, down_ref, grads_ref, d_hidden_ref, acc_ref, tile_ref, feed_ref) = refs[7:14]
    load_sems, tile_sems, feed_sems, near_sems = refs[14:]
    block, depth = tokens_ref.shape
    pair = 2 * block
    loads = [
        pltpu.make_async_copy(source, target, load_sems.at[index])
        for index, (source, target) in enumerate(
            ((down_any, down_ref), (gate_up_any, gate_up_ref))
        )
    ]
    gather_grads = LineGather(chips, grads_ref, grad_sems)
    near = near_copies(gather_grads.chip, chips, grads_any, grads_ref, near_sems)
    for when, copy in near:
        pl.when(when)(copy.start)
    for load in loads:
        load.start()
    line_barrier(chips)

    def pair_rows(chip):
        return pl.ds(pl.multiple_of(chip * pair, pair), pair)

    def term(chip, core):
        rows = pl.ds(pl.multiple_of((2 * chip + core) * block, block), block)
        return dot_nn(heads_ref[rows, :], weight_ref[...])

    def back_hidden(index):
        rows = pair_rows(near_item(chips, gather_grads.chip, index))
        d_hidden_ref[rows, :] = dot_nt(grads_ref[rows, :], down_ref[...]).astype(BF16)

    def each(index):
        @pl.when(index == 0)
        def _():
            loads[0].wait()

        back_hidden(index)

        @pl.when(index + 2 < chips)
        def _():
            gather_grads.hop(index + 2)

    for when, copy in near:
        pl.when(when)(copy.wait)
    gather_grads.pass_on(gather_grads.chip - 1, gather_grads.chip + 1)
    scatter = LineScatter(chips, term, stage, held, landing, scatter_sems)
    scatter.run(residual_ref, each)
    residual = residual_ref[...] + tokens_ref[...].astype(F32)
    residual_ref[...] = residual
    gather = LineGather(chips, rows_ref, gather_sems)
    gather.start((residual * row_scale(residual) * gain_ref[...]).astype(BF16))
    back_hidden(chips - 1)
    loads[1].wait()
    acc_ref[...] = jnp.zeros_like(acc_ref)
    gather.arrive(gather.chip)
    tiles = depth // TILE

    def feed_copies(rows):
        return [
            pltpu.make_async_copy(
                feed_ref.at[index], feed_outs[index].at[rows, :], feed_sems.at[index]
            )
            for index in range(3)
        ]

    def feed(chip):
        rows = pair_rows(chip)
        here = rows_ref[rows, :]
        gate = dot_nt(here, gate_up_ref[0])
        upward = dot_nt(here, gate_up_ref[1])
        d_hidden = d_hidden_ref[rows, :].astype(F32)
        sigmoid_gate = jax.nn.sigmoid(gate)
        activated = gate * sigmoid_gate
        feed_ref[0] = (activated * upward).astype(BF16)
        feed_ref[1] = (
            d_hidden * upward * sigmoid_gate * (1.0 + gate * (1.0 - sigmoid_gate))
        ).astype(BF16)
        feed_ref[2] = (d_hidden * activated).astype(BF16)
        for copy in feed_copies(rows):
            copy.start()
        return rows

    right_refs = (grads_ref, rows_ref, rows_ref)

    def add_grads(rows):
        for index, right_ref in enumerate(right_refs):

            def one_tile(tile, carry):
                cols = pl.ds(pl.multiple_of(tile * TILE, TILE), TILE)
                acc_ref[index, :, cols] += dot_tn(feed_ref[index], right_ref[rows, cols])
                return carry

            lax.fori_loop(0, tiles, one_tile, 0)

    def step_feed(step):
        rows = feed(near_item(chips, gather.chip, step))
        add_grads(rows)
        for copy in feed_copies(rows):
            copy.wait()

    step_feed(0)

    def after(step):
        @pl.when(step < chips - 1)
        def _():
            step_feed(step)

    gather.hops(after)
    rows = feed(near_item(chips, gather.chip, chips - 1))
    sent = []
    for index, right_ref in enumerate(right_refs):
        for tile in range(tiles):
            count = index * tiles + tile
            slot = count % 2
            if count >= 2:
                sent[count - 2].wait()
            cols = slice(tile * TILE, (tile + 1) * TILE)
            tile_ref[slot] = (
                acc_ref[index, :, cols] + dot_tn(feed_ref[index], right_ref[rows, cols])
            ).astype(BF16)
            copy = pltpu.make_async_copy(
                tile_ref.at[slot], grad_outs[index].at[:, cols], tile_sems.at[slot]
            )
            copy.start()
            sent.append(copy)
    for copy in sent[-2:] + feed_copies(rows):
        copy.wait()
    gather_grads.finish(2)
    gather.finish()
    scatter.finish()


def feed_back_kernel(
    chips,
    bits,
    flips,
    d_gate_any,
    d_upward_any,
    weight_any,
    residual_ref,
    gain_ref,
    grad_ref,
    heads_ref,
    out_weight_ref,
    *refs,
):
    feed_in, refs = refs[:1], refs[1:]
    d_residual_ref, d_heads_ref, grad_out_ref, grad_gain_ref = refs[:4]
    feed_outs, refs = refs[4:5], refs[5:]
    stage, held, landing, scatter_sems, gather_sems, rows_ref, acc_ref = refs[:7]
    load_sems, drain_sems, summed = refs[7], refs[8], refs[9:10]
    block, depth = residual_ref.shape
    feed = plane_sum(bits, summed, (1,), refs[10:])
    loads = [
        pltpu.make_async_copy(source, feed.bufs[index][0], load_sems.at[index])
        for index, source in enumerate(feed_in)
    ]
    d_gate_ref, d_upward_ref, weight_ref, operand_sems = refs[-4:]
    operands = [
        pltpu.make_async_copy(source, target, operand_sems.at[index])
        for index, (source, target) in enumerate(
            (
                (d_gate_any, d_gate_ref),
                (d_upward_any, d_upward_ref),
                (weight_any, weight_ref),
            )
        )
    ]
    for load in loads + operands:
        load.start()
    line_barrier(chips, flips)
    for load in loads:
        load.wait()
    feed.advance(0)
    for operand in operands:
        operand.wait()

    def term(chip, core):
        rows = pl.ds(pl.multiple_of((2 * chip + core) * block, block), block)
        return dot_nn(d_gate_ref[rows, :], weight_ref[0]) + dot_nn(
            d_upward_ref[rows, :], weight_ref[1]
        )

    scatter = LineScatter(chips, term, stage, held, landing, scatter_sems)

    def each(index):
        @pl.when(index == chips - 2)
        def _():
            feed.advance(1)

    scatter.run(d_residual_ref, each)
    d_normed = d_residual_ref[...]
    residual = residual_ref[...]
    scale = row_scale(residual)
    hat = residual * scale
    weighted = gain_ref[...] * d_normed
    grad_gain_ref[...] = jnp.sum(d_normed * hat, axis=0, keepdims=True)
    d_residual = grad_ref[...].astype(F32) + scale * (
        weighted - hat * jnp.mean(weighted * hat, axis=-1, keepdims=True)
    )
    d_residual_ref[...] = d_residual
    gather = LineGather(chips, rows_ref, gather_sems)
    gather.start(d_residual.astype(BF16))
    acc_ref[...] = jnp.zeros_like(acc_ref)
    feed.advance(2)
    gather.arrive(gather.chip)

    def use(chip):
        rows = pl.ds(pl.multiple_of(chip * 2 * block, 2 * block), 2 * block)
        here = rows_ref[rows, :]
        d_heads_ref[rows, :] = dot_nt(here, out_weight_ref[...])
        acc_ref[...] += dot_tn(heads_ref[rows, :], here)

    use(gather.chip)

    def after(step):
        gather.each_new(step, use)

        @pl.when(step == max(chips - 2, 1))
        def _():
            feed.advance(3)

    gather.hops(after)
    grad_out_ref[...] = acc_ref[...].astype(BF16)
    gather.finish()
    scatter.finish()
    for step in range(4, 2 * bits + 1):
        feed.advance(step)
    drain = Drain(drain_sems)
    drain.start(summed[0], feed_outs[0])
    drain.finish()


def mixer_backward_kernel(
    chips,
    bits,
    flips,
    heads_here,
    ids_ref,
    conv_ref,
    gain_ref,
    residual_ref,
    hidden_any,
    down_any,
    rows_any,
    *refs,
):
    kept_in, mix_in, refs = refs[:11], refs[11:12], refs[12:]
    d_proj_ref, d_logit_ref, grad_conv_ref, grad_gain_ref, grad_beta_ref, out_ref = refs[:6]
    mix_grads, summed, refs = refs[6:9], refs[9:10], refs[10:]
    y_scr, add_scr, end_scr, d_query_scr, d_key_scr, d_conv_scr = refs[:6]
    hidden_ref, down_ref, rows_ref, result = refs[6:10]
    load_sems = refs[10]
    kept, kept_sems = refs[15:26], refs[26]
    (
        proj_ref,
        mixed_ref,
        query_ref,
        key_ref,
        solve_ref,
        w_ref,
        score_ref,
        map_ref,
        start_ref,
        update_ref,
        d_heads_ref,
    ) = kept
    mix = plane_sum(bits, summed, (1,), refs[27:])
    rows_total = proj_ref.shape[0]
    depth = rows_ref.shape[1]
    block = residual_ref.shape[0]
    loads = [
        pltpu.make_async_copy(source, target, load_sems.at[index])
        for index, (source, target) in enumerate(
            (
                (mix_in[0], mix.bufs[0][0]),
                (hidden_any, hidden_ref),
                (down_any, down_ref),
                (rows_any, rows_ref),
            )
        )
    ]
    for load in loads[:3]:
        load.start()
    keeps = [
        pltpu.make_async_copy(source, target, kept_sems.at[index])
        for index, (source, target) in enumerate(zip(kept_in, kept))
    ]
    for keep_load in keeps:
        keep_load.start()
    loads[3].start()
    line_barrier(chips, flips)
    loads[0].wait()
    mix.advance(0)

    def term_down(chip, core):
        rows = pl.ds(pl.multiple_of((2 * chip + core) * block, block), block)
        return dot_nn(hidden_ref[rows, :], down_ref[...])

    scatter = LineScatter(chips, term_down, *refs[11:15])
    loads[1].wait()
    loads[2].wait()
    scatter.begin()
    scatter.step(0)
    for keep_load in keeps:
        keep_load.wait()
    width = heads_here * DH
    groups = rows_total // GROUP
    spans = LEN // SPAN
    sequences = rows_total // LEN
    grad_gain_ref[...] = jnp.zeros_like(grad_gain_ref)
    grad_conv_ref[...] = jnp.zeros_like(grad_conv_ref)

    def local_part(group, carry):
        start = pl.multiple_of(group * GROUP, GROUP)
        rows = pl.ds(start, GROUP)
        row, col = grid_masks()
        for head in range(heads_here):
            cols = slice(head * DH, (head + 1) * DH)
            mixed = mixed_ref[rows, cols]
            d_heads = d_heads_ref[rows, cols]
            scale = lax.rsqrt(jnp.mean(mixed * mixed, axis=-1, keepdims=True) + EPSILON)
            hat = mixed * scale
            grad_gain_ref[...] += jnp.sum(d_heads * hat, axis=0, keepdims=True)
            weighted = gain_ref[...] * d_heads
            d_mixed = scale * (
                weighted - hat * jnp.mean(weighted * hat, axis=-1, keepdims=True)
            )
            d_low = d_mixed.astype(BF16)
            query = query_ref[rows, cols]
            key = key_ref[rows, cols]
            w_part = w_ref[rows, cols]
            inside = jnp.logical_and(same_block(row, col, SPAN), row >= col)
            d_score = jnp.where(inside, dot_nt(d_low, update_ref[rows, cols]), 0.0).astype(BF16)
            y_part = dot_tn(score_ref[group * heads_here + head], d_low)
            y_scr[rows, cols] = y_part
            y_low = y_part.astype(BF16)
            d_key_scr[rows, cols] = dot_tn(d_score, query)
            reads = []
            for piece in range(PER_GROUP):
                part = slice(piece * SPAN, (piece + 1) * SPAN)
                slot = (group * PER_GROUP + piece) * heads_here + head
                add_scr[slot] = dot_tn(
                    jnp.concatenate([query[part], w_part[part]], 0),
                    jnp.concatenate([d_low[part], -y_low[part]], 0),
                )
                reads.append(dot_nt(d_low[part], start_ref[slot]))
            d_query_scr[rows, cols] = dot_nn(d_score, key) + jnp.concatenate(reads, 0)
        return carry

    lax.fori_loop(0, groups, local_part, 0)
    if chips > 2:
        scatter.step(1)
    mix.advance(1)

    def scan_part(step, states):
        span = spans - 1 - step
        begun = []
        for sequence in range(sequences):
            for head in range(heads_here):
                block = sequence * spans + span
                slot = block * heads_here + head
                d_end = states[sequence * heads_here + head]
                d_end_low = d_end.astype(BF16)
                end_scr[slot] = d_end_low
                begun.append(
                    (d_end - dot_tn(map_ref[slot], d_end_low) + add_scr[slot])
                    * span_keep(ids_ref, block)
                )
        return tuple(begun)

    blank = tuple(jnp.zeros((DH, DH), F32) for _ in range(sequences * heads_here))
    lax.fori_loop(0, spans, scan_part, blank)
    scatter.steps(2)
    mix.advance(2)

    def finish_part(group, carry):
        start = pl.multiple_of(group * GROUP, GROUP)
        rows = pl.ds(start, GROUP)
        keep_rows = span_rows(ids_ref, group)
        row, col = grid_masks()
        d_logits = []
        for head in range(heads_here):
            cols = slice(head * DH, (head + 1) * DH)
            beta = jax.nn.sigmoid(proj_ref[rows, 3 * width + head : 3 * width + head + 1])
            key = key_ref[rows, cols]
            update = update_ref[rows, cols]
            reads = []
            for piece in range(PER_GROUP):
                part = slice(piece * SPAN, (piece + 1) * SPAN)
                slot = (group * PER_GROUP + piece) * heads_here + head
                reads.append(dot_nn(key[part], end_scr[slot]))
            d_update = y_scr[rows, cols] + jnp.concatenate(reads, 0)
            d_right = dot_tn(solve_ref[group * heads_here + head], d_update)
            d_value = beta * d_right
            d_value_low = d_value.astype(BF16)
            d_logit = (1.0 - beta) * jnp.sum(
                d_right * update.astype(F32), axis=-1, keepdims=True
            )
            d_logits.append(d_logit)
            inside = jnp.logical_and(same_block(row, col, SPAN), row > col)
            d_inner = jnp.where(inside, dot_nt(d_value_low, update), 0.0)
            reads = []
            for piece in range(PER_GROUP):
                part = slice(piece * SPAN, (piece + 1) * SPAN)
                slot = (group * PER_GROUP + piece) * heads_here + head
                reads.append(
                    dot_nt(
                        jnp.concatenate([update[part], -d_value_low[part]], 1),
                        jnp.concatenate([end_scr[slot], start_ref[slot]], 1),
                    )
                )
            d_key = (
                d_key_scr[rows, cols]
                + jnp.concatenate(reads, 0)
                - dot_nn(d_inner + d_inner.T, key)
            )
            grads = (d_query_scr[rows, cols] * DH ** (-0.5), d_key, d_value)
            for kind in range(3):
                pre = conv_rows(
                    proj_ref, conv_ref, group, kind, kind * width + head * DH, head, keep_rows
                )
                gate = jax.nn.sigmoid(pre)
                act = pre * gate
                d_act = grads[kind]
                if kind < 2:
                    scale = unit_scale(act)
                    hat = act * scale
                    d_act = scale * (d_act - hat * jnp.sum(hat * d_act, axis=-1, keepdims=True))
                first = kind * width + head * DH
                d_conv_scr[rows, first : first + DH] = d_act * gate * (1.0 + pre * (1.0 - gate))
        lane = lax.broadcasted_iota(jnp.int32, (GROUP, LANES), 1)
        spread = jnp.zeros((GROUP, LANES), F32)
        for head in range(heads_here):
            spread = jnp.where(lane == head, d_logits[head], spread)
        d_logit_ref[rows, :] = spread.astype(BF16)
        return carry

    lax.fori_loop(0, groups, finish_part, 0)
    mix.advance(3)
    d_conv_scr[rows_total : rows_total + 8, :] = jnp.zeros((8, 3 * width), F32)

    def conv_part(group, carry):
        start = pl.multiple_of(group * GROUP, GROUP)
        rows = pl.ds(start, GROUP)
        after = pl.ds(pl.multiple_of(start + GROUP, GROUP), 8)
        keep_rows = span_rows(ids_ref, group)
        follower = jnp.minimum((group + 1) * PER_GROUP, rows_total // SPAN - 1)
        keep_after = jnp.full((8, 1), 1.0, F32) * span_keep(ids_ref, follower)
        keep_joined = jnp.concatenate([keep_rows, keep_after], 0)
        place = lax.broadcasted_iota(jnp.int32, (GROUP + 8, 1), 0) % SPAN
        for kind in range(3):
            for head in range(heads_here):
                first = kind * width + head * DH
                cols = slice(first, first + DH)
                taps = conv_ref[kind, :, head * DH : (head + 1) * DH]
                here = d_conv_scr[rows, cols]
                joined = jnp.concatenate([here, d_conv_scr[after, cols]], 0)
                total = taps[KCONV - 1 : KCONV] * here
                sums = [jnp.sum(here * proj_ref[rows, cols], axis=0, keepdims=True)]
                for offset in range(1, KCONV):
                    counted = jnp.logical_or(place >= offset, keep_joined > 0.0)
                    masked = jnp.where(counted, joined, 0.0)
                    shifted = pltpu.roll(masked, GROUP + 8 - offset, 0)[:GROUP]
                    total = total + taps[KCONV - 1 - offset : KCONV - offset] * shifted
                    sums.append(
                        jnp.sum(
                            here * earlier_rows(proj_ref, group, first, offset, keep_rows),
                            axis=0,
                            keepdims=True,
                        )
                    )
                d_proj_ref[rows, cols] = total.astype(BF16)
                grad_conv_ref[kind, :, head * DH : (head + 1) * DH] += jnp.concatenate(
                    sums[::-1], 0
                )
        return carry

    lax.fori_loop(0, groups, conv_part, 0)
    loads[3].wait()

    def grad_part(tile, carry):
        cols = pl.ds(pl.multiple_of(tile * TILE, TILE), TILE)
        here = rows_ref[:, cols]
        grads = dot_tn(here, d_proj_ref[...]).astype(BF16)
        for kind in range(3):
            mix_grads[kind][cols, :] = grads[:, kind * width : (kind + 1) * width]
        grad_beta_ref[:, cols] = dot_tn(d_logit_ref[...], here)[:8]
        return carry

    lax.fori_loop(0, depth // TILE, grad_part, 0)
    scatter.end(result)
    out_ref[...] = (residual_ref[...] + result[...]).astype(BF16)
    for step in range(4, 2 * bits + 1):
        mix.advance(step)
    scatter.finish()


def project_back_kernel(
    chips,
    bits,
    flips,
    d_proj_any,
    d_logit_ref,
    weight_any,
    beta_ref,
    tokens_ref,
    gain_ref,
    d_residual_ref,
    grad_beta_ref,
    grad_conv_ref,
    part_head_ref,
    part_ffn_ref,
    *refs,
):
    mix_in, refs = refs[:3], refs[3:]
    grad_tokens_ref, gains_ref = refs[:2]
    mix_out, scratch = refs[2:6], refs[6:]
    block, depth = tokens_ref.shape
    mp_flips, peers = flips, 2**bits
    load_sems, scatter_refs, gain_total = scratch[0], scratch[1:5], scratch[5]
    gains = SmallSum(mp_flips, peers, gain_total, *scratch[6:10])
    mix = plane_sum(bits, mix_out, (0, 0, 0, 1), scratch[10:])
    loads = [
        pltpu.make_async_copy(source, mix.bufs[index][0], load_sems.at[index])
        for index, source in enumerate(mix_in)
    ]
    d_proj_ref, weight_ref, operand_sems = refs[-3:]
    operands = [
        pltpu.make_async_copy(source, target, operand_sems.at[index])
        for index, (source, target) in enumerate(
            ((d_proj_any, d_proj_ref), (weight_any, weight_ref))
        )
    ]
    for load in loads + operands:
        load.start()
    small_ref = mix.bufs[3][0]
    taps = jnp.zeros((8, grad_conv_ref.shape[2]), F32)
    small_ref[...] = jnp.zeros_like(small_ref)
    small_ref[:16, :] = jnp.concatenate(
        [grad_beta_ref[...], jnp.zeros((8, depth), F32)], 0
    ).astype(BF16)
    small_ref[16:32, : grad_conv_ref.shape[2]] = jnp.concatenate(
        [grad_conv_ref[0], grad_conv_ref[1], grad_conv_ref[2], taps[:4]], 0
    ).astype(BF16)
    line_barrier(chips, mp_flips, peers)
    for load in loads:
        load.wait()
    width = weight_ref.shape[2]
    mix.advance(0)
    for operand in operands:
        operand.wait()

    def term(chip, core):
        rows = pl.ds(pl.multiple_of((2 * chip + core) * block, block), block)
        total = dot_nn(d_logit_ref[rows, :], beta_ref[...])
        for kind in range(3):
            total = total + dot_nt(
                d_proj_ref[rows, kind * width : (kind + 1) * width], weight_ref[kind]
            )
        return total

    def each(index):
        @pl.when(index == max(chips - 3, 0))
        def _():
            mix.advance(1)

        @pl.when(index == chips - 2)
        def _():
            mix.advance(2)

    scatter = LineScatter(chips, term, *scatter_refs)
    scatter.run(grad_tokens_ref, each)
    for step in range(3, 2 * bits):
        mix.advance(step)
    d_normed = grad_tokens_ref[...]
    tokens = tokens_ref[...].astype(F32)
    scale = row_scale(tokens)
    hat = tokens * scale
    weighted = gain_ref[...] * d_normed
    gain_total[...] = jnp.zeros_like(gain_total)
    gain_total[0:1, :] = jnp.sum(d_normed * hat, axis=0, keepdims=True)
    gain_total[1:2, :] = part_ffn_ref[...]
    gain_total[2:3, :DH] = part_head_ref[...]
    gains.advance(0)
    grad_tokens_ref[...] = d_residual_ref[...] + scale * (
        weighted - hat * jnp.mean(weighted * hat, axis=-1, keepdims=True)
    )
    for step in range(1, len(mp_flips) + 1):
        gains.advance(step)
    scatter.finish()
    mix.advance(2 * bits)
    gains.end(gains_ref)


def line_call(kernel, name, collective, shapes, scratch, specs, args, out_specs=None):
    return pl.pallas_call(
        kernel,
        out_shape=shapes,
        in_specs=specs,
        out_specs=tuple(out_specs or [whole()] * len(shapes)),
        scratch_shapes=scratch,
        compiler_params=pltpu.CompilerParams(
            collective_id=collective, has_side_effects=True, vmem_limit_bytes=VMEM_LIMIT
        ),
        name=name,
    )(*args)


def widen_kernel(*refs):
    gate_ref, upward_ref, down_ref, q_ref, k_ref, v_ref, out_ref, small_ref, gains_ref = refs[:9]
    wide_gate_up, wide_down, wide_qkv, wide_out = refs[9:13]
    beta_ref, conv_ref, norm_ref, ffn_ref, head_ref = refs[13:]
    wide_gate_up[0] = gate_ref[...].astype(F32)
    wide_gate_up[1] = upward_ref[...].astype(F32)
    wide_down[...] = down_ref[...].astype(F32)
    for kind, ref in enumerate((q_ref, k_ref, v_ref)):
        wide_qkv[kind] = ref[...].astype(F32)
    wide_out[...] = out_ref[...].astype(F32)

    @pl.when(pl.program_id(0) == 0)
    def _():
        small = small_ref[...].astype(F32)
        beta_ref[...] = small[: beta_ref.shape[0]]
        for kind in range(3):
            first = 16 + KCONV * kind
            conv_ref[kind] = small[first : first + KCONV, : conv_ref.shape[2]]
        norm_ref[...] = gains_ref[0:1, :]
        ffn_ref[...] = gains_ref[1:2, :]
        head_ref[...] = gains_ref[2:3, :DH]


def widen(gate, upward, down, query, key, value, out, small, gains):
    hidden_width, depth = gate.shape
    width = query.shape[1]
    steps = depth // LANES // 4
    across = pl.BlockSpec((hidden_width, depth // steps), lambda step: (0, step))
    along = pl.BlockSpec((depth // steps, width), lambda step: (step, 0))
    flat = pl.BlockSpec((width, depth // steps), lambda step: (0, step))

    def fixed(shape):
        return pl.BlockSpec(shape, lambda step: (0,) * len(shape))

    like = jax.ShapeDtypeStruct
    return pl.pallas_call(
        widen_kernel,
        out_shape=(
            like((2, hidden_width, depth), F32),
            like((hidden_width, depth), F32),
            like((3, depth, width), F32),
            like((width, depth), F32),
            like((width // DH, depth), F32),
            like((3, KCONV, width), F32),
            like((1, depth), F32),
            like((1, depth), F32),
            like((1, DH), F32),
        ),
        grid=(steps,),
        in_specs=[across] * 3 + [along] * 3 + [flat, fixed((32, depth)), fixed((8, depth))],
        out_specs=(
            pl.BlockSpec((2, hidden_width, depth // steps), lambda step: (0, 0, step)),
            across,
            pl.BlockSpec((3, depth // steps, width), lambda step: (0, step, 0)),
            flat,
            fixed((width // DH, depth)),
            fixed((3, KCONV, width)),
            fixed((1, depth)),
            fixed((1, depth)),
            fixed((1, DH)),
        ),
        compiler_params=pltpu.CompilerParams(vmem_limit_bytes=VMEM_LIMIT),
        name="widen_sums",
    )(gate, upward, down, query, key, value, out, small, gains)


def body(
    chips,
    dp_bits,
    mp_bits,
    tokens,
    grad_out,
    doc_ids,
    norm_gain,
    qkv_weight,
    beta_weight,
    conv_weight,
    head_gain,
    out_weight,
    ffn_gain,
    gate_up_weight,
    down_weight,
):
    width = qkv_weight.shape[2]
    heads_here = width // DH
    block, depth = tokens.shape
    rows_total = 2 * chips * block
    hidden_width = down_weight.shape[0]
    like = jax.ShapeDtypeStruct
    any_spec = pl.BlockSpec(memory_space=pl.ANY)
    norm_row = norm_gain.reshape(1, depth)
    ffn_row = ffn_gain.reshape(1, depth)
    beta_pad = jnp.pad(beta_weight.T, ((0, LANES - heads_here), (0, 0)))
    gate_up_rows = jnp.swapaxes(gate_up_weight, 1, 2)

    f32_rows = pltpu.VMEM((rows_total, width), F32)
    grids = rows_total // GROUP * heads_here
    slots = rows_total // SPAN * heads_here
    mix_shapes = (
        like((rows_total, depth), BF16),
        like((rows_total, 3 * width + LANES), F32),
        like((rows_total, width), BF16),
        like((rows_total, width), BF16),
        like((grids, GROUP, GROUP), BF16),
        like((rows_total, width), BF16),
        like((grids, GROUP, GROUP), BF16),
        like((slots, DH, DH), BF16),
        like((slots, DH, DH), BF16),
        like((rows_total, width), BF16),
        like((rows_total, width), F32),
        like((rows_total, width), BF16),
        like((rows_total, depth), BF16),
    )
    rows_one, projected, query, key, solve, w_part, score, maps, starts, *rest = (
        line_call(
            functools.partial(project_mix_kernel, chips, heads_here),
            "project_mix",
            1,
            mix_shapes,
            [pltpu.VMEM(shape.shape, shape.dtype) for shape in mix_shapes]
            + [
                pltpu.VMEM(qkv_weight.shape, BF16),
                f32_rows,
                pltpu.VMEM((slots, DH, DH), F32),
                pltpu.SemaphoreType.DMA,
                pltpu.SemaphoreType.DMA((len(mix_shapes),)),
                line_sems(chips),
                line_sems(chips),
                pltpu.SemaphoreType.DMA((3,)),
            ],
            [pl.BlockSpec(memory_space=pltpu.SMEM)] + [whole()] * 2 + [any_spec] + [whole()] * 4,
            (
                doc_ids,
                tokens,
                norm_row,
                qkv_weight,
                beta_pad,
                conv_weight,
                head_gain.reshape(1, DH),
                grad_out,
            ),
            [any_spec] * len(mix_shapes),
        )
    )
    heads_out, mixed, update, grads_all = rest
    kept = (mixed, query, key, solve, w_part, score, maps, starts, update)
    feed_shape = like((rows_total, hidden_width), BF16)
    grad_shape = like((hidden_width, depth), BF16)
    residual, hidden, d_gate, d_upward, *feed_grads = line_call(
        functools.partial(attend_feed_kernel, chips),
        "attend_feed",
        2,
        (like((block, depth), F32),) + (feed_shape,) * 3 + (grad_shape,) * 3,
        scatter_scratch(chips, block, depth)
        + [
            line_sems(chips),
            line_sems(chips),
            pltpu.VMEM((rows_total, depth), BF16),
            pltpu.VMEM(gate_up_rows.shape, BF16),
            pltpu.VMEM(down_weight.shape, BF16),
            pltpu.VMEM((rows_total, depth), BF16),
            pltpu.VMEM((rows_total, hidden_width), BF16),
            pltpu.VMEM((3, hidden_width, depth), F32),
            pltpu.VMEM((2, hidden_width, TILE), BF16),
            pltpu.VMEM((3, 2 * block, hidden_width), BF16),
            pltpu.SemaphoreType.DMA((2,)),
            pltpu.SemaphoreType.DMA((2,)),
            pltpu.SemaphoreType.DMA((3,)),
            pltpu.SemaphoreType.DMA((3,)),
        ],
        [whole()] * 4 + [any_spec] * 3,
        (heads_out, out_weight, tokens, ffn_row, gate_up_rows, down_weight, grads_all),
        [whole()] + [any_spec] * 6,
    )
    dp_flips = tuple(("dp", bit) for bit in range(dp_bits))
    mp_flips = tuple(("mp", bit) for bit in range(mp_bits))
    feed_sums = lax.psum(tuple(feed_grads[1:]), "dp")
    d_residual, d_heads, grad_out_weight, part_ffn_gain, sum_down = line_call(
        functools.partial(feed_back_kernel, chips, dp_bits, dp_flips),
        "feed_back",
        3,
        (
            like((block, depth), F32),
            like((rows_total, width), F32),
            like((width, depth), BF16),
            like((1, depth), F32),
        )
        + (grad_shape,),
        scatter_scratch(chips, block, depth)
        + [
            line_sems(chips),
            pltpu.VMEM((rows_total, depth), BF16),
            pltpu.VMEM((width, depth), F32),
            pltpu.SemaphoreType.DMA((1,)),
            pltpu.SemaphoreType.DMA((1,)),
            pltpu.VMEM(grad_shape.shape, BF16),
        ]
        + plane_scratch(dp_bits, [(grad_shape.shape, 1)])
        + [
            pltpu.VMEM(d_gate.shape, BF16),
            pltpu.VMEM(d_upward.shape, BF16),
            pltpu.VMEM(gate_up_rows.shape, BF16),
            pltpu.SemaphoreType.DMA((3,)),
        ],
        [any_spec] * 3 + [whole()] * 5 + [any_spec],
        (
            d_gate,
            d_upward,
            gate_up_rows,
            residual,
            ffn_row,
            grad_out,
            heads_out,
            out_weight,
            feed_grads[0],
        ),
        [whole()] * 4 + [any_spec],
    )
    qkv_shape = like((depth, width), BF16)
    kept = (projected, *kept, d_heads)
    d_projected, d_logit, grad_conv, part_head_gain, grad_beta, block_out, *sums = line_call(
        functools.partial(mixer_backward_kernel, chips, dp_bits, dp_flips, heads_here),
        "mixer_backward",
        5,
        (
            like((rows_total, 3 * width), BF16),
            like((rows_total, LANES), BF16),
            like(conv_weight.shape, F32),
            like((1, DH), F32),
            like((8, depth), F32),
            like((block, depth), BF16),
        )
        + (qkv_shape,) * 3
        + (like((width, depth), BF16),),
        [
            f32_rows,
            pltpu.VMEM((slots, DH, DH), F32),
            pltpu.VMEM((slots, DH, DH), BF16),
            f32_rows,
            f32_rows,
            pltpu.VMEM((rows_total + 8, 3 * width), F32),
            pltpu.VMEM((rows_total, hidden_width), BF16),
            pltpu.VMEM(down_weight.shape, BF16),
            pltpu.VMEM((rows_total, depth), BF16),
            pltpu.VMEM((block, depth), F32),
            pltpu.SemaphoreType.DMA((4,)),
        ]
        + scatter_scratch(chips, block, depth)
        + [pltpu.VMEM(array.shape, array.dtype) for array in kept]
        + [pltpu.SemaphoreType.DMA((len(kept),))]
        + plane_scratch(dp_bits, [((width, depth), 1)]),
        [pl.BlockSpec(memory_space=pltpu.SMEM)] + [whole()] * 3 + [any_spec] * 15,
        (
            doc_ids,
            conv_weight,
            head_gain.reshape(1, DH),
            residual,
            hidden,
            down_weight,
            rows_one,
            *kept,
            grad_out_weight,
        ),
    )
    mix_grads, sum_out = sums[:3], sums[3]
    sum_shapes = (qkv_shape,) * 3 + (like((32, depth), BF16),)
    grad_tokens, gains, *mix_sums = line_call(
        functools.partial(project_back_kernel, chips, dp_bits, mp_flips),
        "project_back",
        4,
        (like((block, depth), F32), like((8, depth), F32), *sum_shapes),
        [pltpu.SemaphoreType.DMA((3,))]
        + scatter_scratch(chips, block, depth)
        + [
            pltpu.VMEM((8, depth), F32),
            pltpu.VMEM((mp_bits, 8, depth), F32),
            pltpu.VMEM((2**dp_bits, 8, depth), F32),
            pltpu.SemaphoreType.DMA((2, mp_bits)),
            pltpu.SemaphoreType.DMA((2, 2**dp_bits - 1)),
        ]
        + plane_scratch(
            dp_bits, [(shape.shape, 1 if index == 3 else 0) for index, shape in enumerate(sum_shapes)]
        )
        + [
            pltpu.VMEM(d_projected.shape, BF16),
            pltpu.VMEM(qkv_weight.shape, BF16),
            pltpu.SemaphoreType.DMA((2,)),
        ],
        [any_spec, whole(), any_spec] + [whole()] * 8 + [any_spec] * 3,
        (
            d_projected,
            d_logit,
            qkv_weight,
            beta_pad,
            tokens,
            norm_row,
            d_residual,
            grad_beta,
            grad_conv,
            part_head_gain,
            part_ffn_gain,
            *mix_grads,
        ),
    )
    wide_gate_up, wide_down, wide_qkv, wide_out, *rest = widen(
        *feed_sums, sum_down, *mix_sums[:3], sum_out, mix_sums[3], gains
    )
    sum_beta, sum_conv, sum_norm, sum_ffn, sum_head = rest
    return (
        block_out,
        grad_tokens,
        sum_norm.reshape(depth),
        wide_qkv,
        sum_beta.T,
        sum_conv,
        sum_head.reshape(DH),
        wide_out,
        sum_ffn.reshape(depth),
        jnp.swapaxes(wide_gate_up, 1, 2),
        wide_down,
    )


def solution(mesh):
    in_specs = (
        P(("dp", "mp"), None),
        P(("dp", "mp"), None),
        P("dp"),
        P(),
        P(None, None, "mp"),
        P(None, "mp"),
        P(None, None, "mp"),
        P(),
        P("mp", None),
        P(),
        P(None, None, "mp"),
        P("mp", None),
    )
    out_specs = (
        P(("dp", "mp"), None),
        P(("dp", "mp"), None),
        P(),
        P(None, None, "mp"),
        P(None, "mp"),
        P(None, None, "mp"),
        P(),
        P("mp", None),
        P(),
        P(None, None, "mp"),
        P("mp", None),
    )
    chips = mesh.shape["mp"] // 2
    dp_bits = mesh.shape["dp"].bit_length() - 1
    mp_bits = mesh.shape["mp"].bit_length() - 1
    part = functools.partial(body, chips, dp_bits, mp_bits)
    return jax.shard_map(part, mesh=mesh, in_specs=in_specs, out_specs=out_specs, check_vma=False)
```
